256 devices in a mesh: depth: 8 (over x_hi, y), row: 32 (over x_lo, z, core).
Axes of the slice: x: 4 (x_hi: 2, x_lo: 2; x = x_hi * 2 + x_lo), y: 4, z: 8, core: 2. Of those that a mesh axis runs over, the one named last changes fastest.
Arguments:
- index_volume: bfloat16 [8, 512, 2048], P('depth', 'row'), may hold values from -4 to 4
- angles: int32 [2], replicated, may hold values from 0 to 15
- offsets: int32 [8], P('depth'), may hold values from -4 to 4, as said below
- measured: bfloat16 [2, 512, 2048], P(None, 'row'), may hold values from 0 to 2
Outputs:
- gradient: float32 [8, 512, 2048], P('depth', 'row')
The draws below stay inside these ranges and needn't reach their ends.
Inputs may be any that keep to these rules, and one draw needn't show every extreme that they name: `offsets`: each of -4 and 4 is taken by at least one slice.
All inputs are finite; a program needn't handle non-finite values.
Results may differ from the reference program's by a relative error of at most 0.0003.
Values may be sent and summed in bfloat16 or wider, within the bound.
A program may use at most 64 MiB of HBM per device.

```python
import math
import jax
import jax.numpy as jnp
from jax import lax

NX = 2048
ANG = 2
TILTS = 16
HALF = 10
SHIFT = 4
HALFCOL = 64
NY = 512
SLICES = 8


def draw_offsets(key, part):
    values = jax.random.randint(key, (SLICES,), -SHIFT, SHIFT + 1)
    ranking = jax.random.permutation(jax.random.fold_in(key, 7), SLICES)
    values = values.at[ranking[0]].set(SHIFT)
    values = values.at[ranking[1]].set(-SHIFT)
    return values.astype(jnp.int32)


def steps_of(own_key, dims, shards, low, top_value):
    def one(dim, blocks):
        steps = jax.random.uniform(jax.random.fold_in(jax.random.fold_in(own_key, 6), dim), (blocks,), jnp.float32, low / len(shards), top_value / len(shards))
        return jnp.repeat(jnp.exp(steps), dims[dim] // blocks).reshape((-1,) + (1,) * (len(dims) - dim - 1))

    level = one(*shards[0])
    for cut in shards[1:]:
        level = level * one(*cut)
    return level


def normal_values(rng, shape, width, limit, split=(), kind=jnp.bfloat16):
    array = jax.random.normal(rng, shape, jnp.float32) * width
    if len(split) > 0:
        array = steps_of(rng, shape, split, -0.22, 0.18) * array
    return jnp.clip(array, min=-limit, max=limit).astype(kind)


def setup_inputs(seed: int = 0) -> dict:
    streams_of = jax.random.split(jax.random.key(seed), 5)
    index_volume = normal_values(streams_of[0], (SLICES, NY, NX), 1.0, 4.0, ((0, 8), (1, 32)))
    angles = jax.random.randint(streams_of[1], (ANG,), 0, TILTS).astype(jnp.int32)
    offsets = draw_offsets(jax.random.fold_in(streams_of[4], 71), 0)
    measured = jnp.clip(2.0 * jax.random.uniform(streams_of[3], (ANG, NY, NX), jnp.float32) ** steps_of(streams_of[3], (ANG, NY, NX), ((1, 32),), -0.2, 0.2), 0.0, 2.0).astype(jnp.bfloat16)
    return dict(index_volume=index_volume, angles=angles, offsets=offsets, measured=measured)


PHASE_SCALE = 0.5
CHIRP_ROW = 1.3
CHIRP_COL = 1.7

def kernel_taps(radius, chirp_rate):
    distance = jnp.arange(-radius, radius + 1).astype(jnp.float32)
    phase_arg = chirp_rate / radius * distance * distance
    weight = 1.0 / math.sqrt(2 * radius + 1)
    return (jnp.cos(phase_arg) * weight, jnp.sin(phase_arg) * weight)

def plane_waves(angles, row_start, height, columns, total_rows):
    across = angles - TILTS // 2
    along = jnp.mod(3 * angles, TILTS) - TILTS // 2
    row_index = row_start + lax.broadcasted_iota(jnp.int32, (height, columns), 0)
    col_index = lax.broadcasted_iota(jnp.int32, (height, columns), 1)
    period = columns * total_rows
    cycles_int = jnp.mod(across[:, None, None] * col_index[None] * total_rows + along[:, None, None] * row_index[None] * columns, period).astype(jnp.int32)
    phase_arg = 2.0 * math.pi / period * cycles_int.astype(jnp.float32)
    return jnp.stack([jnp.cos(phase_arg), jnp.sin(phase_arg)], axis=1)

def banded(real_part, imag_part, taps, radius, offset, axis_no):
    length = real_part.shape[axis_no]
    padded_len = 1 << (length + 2 * radius).bit_length()
    spectrum = jnp.fft.fft(real_part + 1j * imag_part, n=padded_len, axis=axis_no)
    kernel = jnp.fft.fft(taps[0] + 1j * taps[1], n=padded_len)
    extent = [1] * real_part.ndim
    extent[axis_no] = padded_len
    full_conv = jnp.fft.ifft(spectrum * kernel.reshape(extent), axis=axis_no)
    window = lax.dynamic_slice_in_dim(full_conv, offset + radius, length, axis_no)
    return (jnp.real(window), jnp.imag(window))

def reference(index_volume, angles, offsets, measured):
    incident = plane_waves(angles, 0, NY, NX, NY)
    row_taps = kernel_taps(HALF, CHIRP_ROW)
    col_taps = kernel_taps(HALFCOL, CHIRP_COL)
    intensity = measured.astype(jnp.float32)

    def loss_value(volume):
        real_part = incident[:, 0]
        imag_part = incident[:, 1]
        for layer_no in range(SLICES):
            phase_arg = PHASE_SCALE * volume[layer_no]
            cosine = jnp.cos(phase_arg)
            sine = jnp.sin(phase_arg)
            real_part, imag_part = (cosine * real_part - sine * imag_part, cosine * imag_part + sine * real_part)
            real_part, imag_part = banded(real_part, imag_part, row_taps, HALF, offsets[layer_no], 1)
            real_part, imag_part = banded(real_part, imag_part, col_taps, HALFCOL, 0, 2)
        errors = real_part * real_part + imag_part * imag_part - intensity
        return 0.5 * jnp.sum(errors * errors)
    volume = index_volume.astype(jnp.float32)
    return jax.grad(loss_value)(volume)
```

```python
import math

import jax
import jax.numpy as jnp
from jax import lax
from jax.sharding import PartitionSpec as P

TILTS = 16
HALF = 10
SHIFT = 4
HALFCOL = 64
COLBLK = 128


PHASE_SCALE = 0.5
CHIRP_ROW = 1.3
CHIRP_COL = 1.7


def halo_rows(shard, axis, width):
    size, length = (lax.axis_size(axis), shard.shape[-2])
    up = [(i, i + 1) for i in range(size - 1)]
    down = [(j, i) for i, j in up]
    last = shard[..., length - width :, :]
    initial = shard[..., :width, :]
    before = lax.ppermute(last, axis, up)
    after = lax.ppermute(initial, axis, down)
    return jnp.concatenate([before, shard, after], axis=-2)


def kernel_values(distance, radius, chirp_rate):
    inside = jnp.abs(distance) <= radius
    phase_arg = chirp_rate / radius * distance * distance
    weight = 1.0 / math.sqrt(2 * radius + 1)
    real_part = jnp.where(inside, jnp.cos(phase_arg) * weight, 0.0)
    imag_part = jnp.where(inside, jnp.sin(phase_arg) * weight, 0.0)
    return (real_part, imag_part)


def row_band(offset, height, margin, conjugate):
    extent = (height, height + 2 * margin)
    target = lax.broadcasted_iota(jnp.int32, extent, 0)
    source = lax.broadcasted_iota(jnp.int32, extent, 1)
    offset_used = -offset if conjugate else offset
    distance = (source - target - margin - offset_used).astype(jnp.float32)
    real_part, imag_part = kernel_values(distance, HALF, CHIRP_ROW)
    return (real_part, -imag_part) if conjugate else (real_part, imag_part)


def column_band(conjugate, block_width):
    extent = (block_width + 2 * HALFCOL, block_width)
    source = lax.broadcasted_iota(jnp.int32, extent, 0)
    target = lax.broadcasted_iota(jnp.int32, extent, 1)
    distance = (source - target - HALFCOL).astype(jnp.float32)
    real_part, imag_part = kernel_values(distance, HALFCOL, CHIRP_COL)
    return (real_part, -imag_part) if conjugate else (real_part, imag_part)


def mix_rows(band, extended):

    def product(matrix, operand):
        return jnp.einsum("ij,jc->ic", matrix, operand, precision=lax.Precision.HIGHEST)

    real_part = product(band[0], extended[0]) - product(band[1], extended[1])
    imag_part = product(band[0], extended[1]) + product(band[1], extended[0])
    return jnp.stack([real_part, imag_part], axis=0)


def mix_columns(band, field):
    _, height, columns = field.shape
    blocks = columns // COLBLK
    padded = jnp.pad(field, ((0, 0), (0, 0), (HALFCOL, COLBLK - HALFCOL)))
    middle = padded[..., :columns].reshape(2, height, blocks, COLBLK)
    beyond = padded[..., COLBLK : columns + COLBLK].reshape(2, height, blocks, COLBLK)
    window = jnp.concatenate([middle, beyond], axis=3)

    def product(operand, matrix):
        return jnp.einsum("rbj,ji->rbi", operand, matrix, precision=lax.Precision.HIGH)

    real_part = product(window[0], band[0]) - product(window[1], band[1])
    imag_part = product(window[1], band[0]) + product(window[0], band[1])
    return jnp.stack([real_part, imag_part], axis=0).reshape(2, height, columns)


def rotate(field, cosine, sine):
    real_part = cosine * field[0] - sine * field[1]
    imag_part = cosine * field[1] + sine * field[0]
    return jnp.stack([real_part, imag_part], axis=0)


def plane_wave(angle, row_start, height, columns, total_rows, total_cols):
    across = angle - TILTS // 2
    along = jnp.mod(3 * angle, TILTS) - TILTS // 2
    row_index = row_start + lax.broadcasted_iota(jnp.int32, (height, columns), 0)
    col_index = lax.broadcasted_iota(jnp.int32, (height, columns), 1)
    period = total_cols * total_rows
    cycles_int = jnp.mod(across * col_index * total_rows + along * row_index * total_cols, period)
    phase_arg = 2.0 * math.pi / period * cycles_int.astype(jnp.float32)
    return jnp.stack([jnp.cos(phase_arg), jnp.sin(phase_arg)], axis=0)


def body(index_volume, angles, offsets, measured):
    sections = lax.axis_size("depth")
    section_no = lax.axis_index("depth")
    height = index_volume.shape[1]
    columns = index_volume.shape[2]
    margin = HALF + SHIFT
    row_start = lax.axis_index("row") * height
    total_rows = height * lax.axis_size("row")
    angle_count = angles.shape[0]
    angle_no = section_no % angle_count
    volume = lax.all_gather(index_volume, "depth", axis=0, tiled=True)
    shifts = lax.all_gather(offsets, "depth", axis=0, tiled=True)
    layers = volume.shape[0]
    intensity = lax.dynamic_index_in_dim(measured, angle_no, 0, keepdims=False).astype(jnp.float32)
    angle = lax.dynamic_index_in_dim(angles, angle_no, 0, keepdims=False)
    field = plane_wave(angle, row_start, height, columns, total_rows, columns)
    col_fwd = column_band(False, COLBLK)
    col_adj = column_band(True, COLBLK)

    phases = PHASE_SCALE * volume.astype(jnp.float32)
    cosines = jnp.cos(phases)
    sines = jnp.sin(phases)
    def forward_step(layer_no, carried):
        field, stored = carried
        transmitted = rotate(field, cosines[layer_no], sines[layer_no])
        stored = lax.dynamic_update_index_in_dim(stored, transmitted, layer_no, 0)
        extended = halo_rows(transmitted, "row", margin)
        band = row_band(shifts[layer_no], height, margin, False)
        return (mix_columns(col_fwd, mix_rows(band, extended)), stored)

    stored = jnp.zeros((layers,) + field.shape, jnp.float32)
    field, stored = lax.fori_loop(0, layers, forward_step, (field, stored))
    errors = field[0] * field[0] + field[1] * field[1] - intensity
    adjoint = 2.0 * errors[None] * field

    def backward_step(step, carried):
        adjoint, terms = carried
        layer_no = layers - 1 - step
        returned = mix_columns(col_adj, adjoint)
        extended = halo_rows(returned, "row", margin)
        band = row_band(shifts[layer_no], height, margin, True)
        returned = mix_rows(band, extended)
        transmitted = stored[layer_no]
        term = PHASE_SCALE * (transmitted[0] * returned[1] - transmitted[1] * returned[0])
        terms = lax.dynamic_update_index_in_dim(terms, term, layer_no, 0)
        return (rotate(returned, cosines[layer_no], -sines[layer_no]), terms)

    terms = jnp.zeros((layers, height, columns), jnp.float32)
    adjoint, terms = lax.fori_loop(0, layers, backward_step, (adjoint, terms))
    own = lax.dynamic_index_in_dim(terms, section_no, 0, keepdims=True)
    partner_slice = section_no ^ 1
    for_partner = lax.dynamic_index_in_dim(terms, partner_slice, 0, keepdims=True)
    pairs = [(i, i ^ 1) for i in range(sections)]
    received = lax.ppermute(for_partner, "depth", pairs)
    first = jnp.where(angle_no == 0, own, received)
    second = jnp.where(angle_no == 0, received, own)
    return first + second


def solution(mesh):
    in_specs = (P("depth", "row", None), P(), P("depth"), P(None, "row", None))
    out_specs = P("depth", "row", None)
    return jax.shard_map(body, mesh=mesh, in_specs=in_specs, out_specs=out_specs, check_vma=False)
```

```python
import functools
import math

import jax
import jax.numpy as jnp
from jax import lax
from jax.experimental import pallas as pl
from jax.experimental.pallas import tpu as pltpu
from jax.sharding import PartitionSpec as P

TILTS = 16
HALF = 10
SHIFT = 4
HALFCOL = 64
LANE = 128

PHASE_SCALE = 0.5
CHIRP_ROW = 1.3
CHIRP_COL = 1.7
MESH = pl.DeviceIdType.MESH


def kernel_values(distance, radius, chirp_rate):
    inside = jnp.abs(distance) <= radius
    phase_arg = chirp_rate / radius * distance * distance
    weight = 1.0 / math.sqrt(2 * radius + 1)
    real_part = jnp.where(inside, jnp.cos(phase_arg) * weight, 0.0)
    imag_part = jnp.where(inside, jnp.sin(phase_arg) * weight, 0.0)
    return (real_part, imag_part)


def split_bf16(x):
    high = x.astype(jnp.bfloat16)
    low = (x - high.astype(jnp.float32)).astype(jnp.bfloat16)
    return high, low


def complex_block(real_part, imag_part):
    top = jnp.concatenate([real_part, -imag_part], axis=-1)
    bottom = jnp.concatenate([imag_part, real_part], axis=-1)
    return jnp.concatenate([top, bottom], axis=-2)


def row_bands(shifts, height):
    layers = shifts.shape[0]
    signs = jnp.concatenate([jnp.ones((layers,), jnp.int32), -jnp.ones((layers,), jnp.int32)])
    used = jnp.concatenate([shifts, shifts[::-1]]) * signs
    extent = (2 * layers, 3, height, height)
    part = lax.broadcasted_iota(jnp.int32, extent, 1)
    target = lax.broadcasted_iota(jnp.int32, extent, 2)
    source = lax.broadcasted_iota(jnp.int32, extent, 3) + (part - 1) * height
    distance = (source - target - used[:, None, None, None]).astype(jnp.float32)
    real_part, imag_part = kernel_values(distance, HALF, CHIRP_ROW)
    imag_part = imag_part * signs[:, None, None, None].astype(jnp.float32)
    return complex_block(real_part, imag_part)


def column_bands():
    extent = (3, LANE, LANE)
    part = lax.broadcasted_iota(jnp.int32, extent, 0)
    source = lax.broadcasted_iota(jnp.int32, extent, 1) + (part - 1) * LANE
    target = lax.broadcasted_iota(jnp.int32, extent, 2)
    distance = (source - target).astype(jnp.float32)
    real_part, imag_part = kernel_values(distance, HALFCOL, CHIRP_COL)
    forward = jnp.concatenate([real_part, imag_part], axis=-1)
    adjoint = jnp.concatenate([real_part, -imag_part], axis=-1)
    return jnp.stack([forward, adjoint], axis=0)


def dot3(a, x):
    a_high, a_low = split_bf16(a)
    x_high, x_low = split_bf16(x)
    f32 = jnp.float32
    return (
        jnp.dot(a_high, x_high, preferred_element_type=f32)
        + jnp.dot(a_high, x_low, preferred_element_type=f32)
        + jnp.dot(a_low, x_high, preferred_element_type=f32)
    )


def chain_kernel(rows, u0_ref, cos_ref, sin_ref, inten_ref, rband_ref, cband_ref,
                 terms_ref, field_ref, acc_ref, y_store, b_store, before, after, bmh_ref, bml_ref,
                 send_dn, send_up, recv_bf, recv_af):
    me = lax.axis_index("row")
    layers, height, columns = cos_ref.shape
    blocks = columns // LANE
    has_up = me > 0
    has_dn = me < rows - 1

    barrier = pltpu.get_barrier_semaphore()

    @pl.when(has_up)
    def _():
        pl.semaphore_signal(barrier, 1, device_id={"row": me - 1}, device_id_type=MESH)

    @pl.when(has_dn)
    def _():
        pl.semaphore_signal(barrier, 1, device_id={"row": me + 1}, device_id_type=MESH)

    peers = (me + rows - 1) // rows + (2 * rows - 2 - me) // rows
    pl.semaphore_wait(barrier, peers)

    zero_block = jnp.zeros((2 * height, LANE), jnp.bfloat16)
    for ref in (bmh_ref, bml_ref):
        ref[0] = zero_block
        ref[blocks + 1] = zero_block

    def copies(k, source):
        down = pltpu.make_async_remote_copy(
            src_ref=source, dst_ref=before.at[k], send_sem=send_dn.at[k], recv_sem=recv_bf.at[k],
            device_id={"row": me + 1}, device_id_type=MESH)
        up = pltpu.make_async_remote_copy(
            src_ref=source, dst_ref=after.at[k], send_sem=send_up.at[k], recv_sem=recv_af.at[k],
            device_id={"row": me - 1}, device_id_type=MESH)
        return down, up

    def start(k, source):
        down, up = copies(k, source)

        @pl.when(has_dn)
        def _():
            down.start()

        @pl.when(has_up)
        def _():
            up.start()

    def finish(k, source):
        down, up = copies(k, source)

        @pl.when(has_dn)
        def _():
            down.wait_send()

        @pl.when(has_up)
        def _():
            up.wait_send()

    def row_mix(k, source, z):
        down, up = copies(k, source)
        acc_ref[...] = dot3(rband_ref[k, 1], z)
        start(k, source)

        @pl.when(has_up)
        def _():
            down.wait_recv()
            acc_ref[...] += dot3(rband_ref[k, 0], before[k])

        @pl.when(has_dn)
        def _():
            up.wait_recv()
            acc_ref[...] += dot3(rband_ref[k, 2], after[k])

        return acc_ref[...]

    def col_mix(v, which):
        high, low = split_bf16(v)
        for b in range(blocks):
            bmh_ref[b + 1] = high[:, b * LANE:(b + 1) * LANE]
            bml_ref[b + 1] = low[:, b * LANE:(b + 1) * LANE]
        total = None
        f32 = jnp.float32
        for t in range(3):
            xh = bmh_ref[t:t + blocks].reshape(blocks * 2 * height, LANE)
            xl = bml_ref[t:t + blocks].reshape(blocks * 2 * height, LANE)
            wh, wl = split_bf16(cband_ref[which, t])
            part = (jnp.dot(xh, wh, preferred_element_type=f32) + jnp.dot(xh, wl, preferred_element_type=f32)
                    + jnp.dot(xl, wh, preferred_element_type=f32))
            total = part if total is None else total + part
        total = total.reshape(blocks, 2 * height, 2 * LANE)
        real_part = total[:, :height, :LANE] - total[:, height:, LANE:]
        imag_part = total[:, :height, LANE:] + total[:, height:, :LANE]
        out = jnp.concatenate([real_part, imag_part], axis=1)
        return jnp.concatenate([out[b] for b in range(blocks)], axis=1)

    field_ref[...] = u0_ref[...]

    def forward(s, carry):
        u = field_ref[...]
        c = cos_ref[s]
        sn = sin_ref[s]
        ur = u[:height]
        ui = u[height:]
        y_store[s] = jnp.concatenate([c * ur - sn * ui, c * ui + sn * ur], axis=0)
        source = y_store.at[s]
        v = row_mix(s, source, y_store[s])
        field_ref[...] = col_mix(v, 0)
        finish(s, source)
        return carry

    lax.fori_loop(0, layers, forward, 0)
    u = field_ref[...]
    ur = u[:height]
    ui = u[height:]
    errors = ur * ur + ui * ui - inten_ref[...]
    field_ref[...] = jnp.concatenate([2.0 * errors * ur, 2.0 * errors * ui], axis=0)

    def backward(j, carry):
        s = layers - 1 - j
        k = layers + j
        b_store[j] = col_mix(field_ref[...], 1)
        source = b_store.at[j]
        acc = row_mix(k, source, b_store[j])
        ar = acc[:height]
        ai = acc[height:]
        y = y_store[s]
        terms_ref[s] = PHASE_SCALE * (y[:height] * ai - y[height:] * ar)
        c = cos_ref[s]
        sn = sin_ref[s]
        field_ref[...] = jnp.concatenate([c * ar + sn * ai, c * ai - sn * ar], axis=0)
        finish(k, source)
        return carry

    lax.fori_loop(0, layers, backward, 0)


def run_chain(u0, cosines, sines, intensity, row_band, col_band, rows):
    layers, height, columns = cosines.shape
    blocks = columns // LANE
    field = (2 * height, columns)
    return pl.pallas_call(
        functools.partial(chain_kernel, rows),
        out_shape=jax.ShapeDtypeStruct((layers, height, columns), jnp.float32),
        in_specs=[pl.BlockSpec(memory_space=pltpu.VMEM)] * 6,
        out_specs=pl.BlockSpec(memory_space=pltpu.VMEM),
        scratch_shapes=[
            pltpu.VMEM(field, jnp.float32),
            pltpu.VMEM(field, jnp.float32),
            pltpu.VMEM((layers,) + field, jnp.float32),
            pltpu.VMEM((layers,) + field, jnp.float32),
            pltpu.VMEM((2 * layers,) + field, jnp.float32),
            pltpu.VMEM((2 * layers,) + field, jnp.float32),
            pltpu.VMEM((blocks + 2, 2 * height, LANE), jnp.bfloat16),
            pltpu.VMEM((blocks + 2, 2 * height, LANE), jnp.bfloat16),
            pltpu.SemaphoreType.DMA((2 * layers,)),
            pltpu.SemaphoreType.DMA((2 * layers,)),
            pltpu.SemaphoreType.DMA((2 * layers,)),
            pltpu.SemaphoreType.DMA((2 * layers,)),
        ],
        compiler_params=pltpu.CompilerParams(
            collective_id=0, has_side_effects=True, vmem_limit_bytes=56 * 1024 * 1024),
    )(u0, cosines, sines, intensity, row_band, col_band)


def plane_wave(angle, row_start, height, columns, total_rows, total_cols):
    across = angle - TILTS // 2
    along = jnp.mod(3 * angle, TILTS) - TILTS // 2
    row_index = row_start + lax.broadcasted_iota(jnp.int32, (height, columns), 0)
    col_index = lax.broadcasted_iota(jnp.int32, (height, columns), 1)
    period = total_cols * total_rows
    cycles_int = jnp.mod(across * col_index * total_rows + along * row_index * total_cols, period)
    phase_arg = 2.0 * math.pi / period * cycles_int.astype(jnp.float32)
    return jnp.concatenate([jnp.cos(phase_arg), jnp.sin(phase_arg)], axis=0)


def body(index_volume, angles, offsets, measured):
    sections = lax.axis_size("depth")
    rows = lax.axis_size("row")
    section_no = lax.axis_index("depth")
    height = index_volume.shape[1]
    columns = index_volume.shape[2]
    row_start = lax.axis_index("row") * height
    total_rows = height * rows
    angle_count = angles.shape[0]
    angle_no = section_no % angle_count
    volume = lax.all_gather(index_volume, "depth", axis=0, tiled=True)
    shifts = lax.all_gather(offsets, "depth", axis=0, tiled=True)
    intensity = lax.dynamic_index_in_dim(measured, angle_no, 0, keepdims=False).astype(jnp.float32)
    angle = lax.dynamic_index_in_dim(angles, angle_no, 0, keepdims=False)
    incident = plane_wave(angle, row_start, height, columns, total_rows, columns)
    phases = PHASE_SCALE * volume.astype(jnp.float32)
    terms = run_chain(incident, jnp.cos(phases), jnp.sin(phases), intensity,
                      row_bands(shifts, height), column_bands(), rows)
    own = lax.dynamic_index_in_dim(terms, section_no, 0, keepdims=True)
    for_partner = lax.dynamic_index_in_dim(terms, section_no ^ 1, 0, keepdims=True)
    pairs = [(i, i ^ 1) for i in range(sections)]
    received = lax.ppermute(for_partner, "depth", pairs)
    first = jnp.where(angle_no == 0, own, received)
    second = jnp.where(angle_no == 0, received, own)
    return first + second


def solution(mesh):
    in_specs = (P("depth", "row", None), P(), P("depth"), P(None, "row", None))
    out_specs = P("depth", "row", None)
    return jax.shard_map(body, mesh=mesh, in_specs=in_specs, out_specs=out_specs, check_vma=False)
```

```python
import functools
import math

import jax
import jax.numpy as jnp
from jax import lax
from jax.experimental import pallas as pl
from jax.experimental.pallas import tpu as pltpu
from jax.sharding import PartitionSpec as P

TILTS = 16
HALF = 10
SHIFT = 4
HALFCOL = 64
LANE = 128

PHASE_SCALE = 0.5
CHIRP_ROW = 1.3
CHIRP_COL = 1.7
MESH = pl.DeviceIdType.MESH


def kernel_values(distance, radius, chirp_rate):
    inside = jnp.abs(distance) <= radius
    phase_arg = chirp_rate / radius * distance * distance
    weight = 1.0 / math.sqrt(2 * radius + 1)
    real_part = jnp.where(inside, jnp.cos(phase_arg) * weight, 0.0)
    imag_part = jnp.where(inside, jnp.sin(phase_arg) * weight, 0.0)
    return (real_part, imag_part)


def split_bf16(x):
    high = x.astype(jnp.bfloat16)
    low = (x - high.astype(jnp.float32)).astype(jnp.bfloat16)
    return high, low


def complex_block(real_part, imag_part):
    top = jnp.concatenate([real_part, -imag_part], axis=-1)
    bottom = jnp.concatenate([imag_part, real_part], axis=-1)
    return jnp.concatenate([top, bottom], axis=-2)


def row_bands(shifts, height):
    layers = shifts.shape[0]
    signs = jnp.concatenate([jnp.ones((layers,), jnp.int32), -jnp.ones((layers,), jnp.int32)])
    used = jnp.concatenate([shifts, shifts[::-1]]) * signs
    extent = (2 * layers, 3, height, height)
    part = lax.broadcasted_iota(jnp.int32, extent, 1)
    target = lax.broadcasted_iota(jnp.int32, extent, 2)
    source = lax.broadcasted_iota(jnp.int32, extent, 3) + (part - 1) * height
    distance = (source - target - used[:, None, None, None]).astype(jnp.float32)
    real_part, imag_part = kernel_values(distance, HALF, CHIRP_ROW)
    imag_part = imag_part * signs[:, None, None, None].astype(jnp.float32)
    return complex_block(real_part, imag_part)


def column_bands():
    extent = (3, LANE, LANE)
    part = lax.broadcasted_iota(jnp.int32, extent, 0)
    source = lax.broadcasted_iota(jnp.int32, extent, 1) + (part - 1) * LANE
    target = lax.broadcasted_iota(jnp.int32, extent, 2)
    distance = (source - target).astype(jnp.float32)
    real_part, imag_part = kernel_values(distance, HALFCOL, CHIRP_COL)
    forward = jnp.concatenate([real_part, imag_part], axis=-1)
    adjoint = jnp.concatenate([real_part, -imag_part], axis=-1)
    return jnp.stack([forward, adjoint], axis=0)


def dot3(a, x):
    a_high, a_low = split_bf16(a)
    x_high, x_low = split_bf16(x)
    f32 = jnp.float32
    return (
        jnp.dot(a_high, x_high, preferred_element_type=f32)
        + jnp.dot(a_high, x_low, preferred_element_type=f32)
        + jnp.dot(a_low, x_high, preferred_element_type=f32)
    )


def chain_kernel(rows, u0_ref, cos_ref, sin_ref, inten_ref, rband_ref, cband_ref,
                 terms_ref, field_ref, acc_ref, y_store, b_store, before, after, bmh_ref, bml_ref,
                 send_dn, send_up, recv_bf, recv_af):
    me = lax.axis_index("row")
    layers, height, columns = cos_ref.shape
    blocks = columns // LANE
    has_up = me > 0
    has_dn = me < rows - 1

    barrier = pltpu.get_barrier_semaphore()

    @pl.when(has_up)
    def _():
        pl.semaphore_signal(barrier, 1, device_id={"row": me - 1}, device_id_type=MESH)

    @pl.when(has_dn)
    def _():
        pl.semaphore_signal(barrier, 1, device_id={"row": me + 1}, device_id_type=MESH)

    peers = (me + rows - 1) // rows + (2 * rows - 2 - me) // rows
    pl.semaphore_wait(barrier, peers)

    zero_block = jnp.zeros((2 * height, LANE), jnp.bfloat16)
    for ref in (bmh_ref, bml_ref):
        ref[0] = zero_block
        ref[blocks + 1] = zero_block

    def copies(k, source):
        down = pltpu.make_async_remote_copy(
            src_ref=source, dst_ref=before.at[k], send_sem=send_dn.at[k], recv_sem=recv_bf.at[k],
            device_id={"row": me + 1}, device_id_type=MESH)
        up = pltpu.make_async_remote_copy(
            src_ref=source, dst_ref=after.at[k], send_sem=send_up.at[k], recv_sem=recv_af.at[k],
            device_id={"row": me - 1}, device_id_type=MESH)
        return down, up

    def start(k, source):
        down, up = copies(k, source)

        @pl.when(has_dn)
        def _():
            down.start()

        @pl.when(has_up)
        def _():
            up.start()

    def finish(k, source):
        down, up = copies(k, source)

        @pl.when(has_dn)
        def _():
            down.wait_send()

        @pl.when(has_up)
        def _():
            up.wait_send()

    def row_mix(k, source, z):
        down, up = copies(k, source)
        acc_ref[...] = dot3(rband_ref[k, 1], z)
        start(k, source)

        @pl.when(has_up)
        def _():
            down.wait_recv()
            acc_ref[...] += dot3(rband_ref[k, 0], before[k])

        @pl.when(has_dn)
        def _():
            up.wait_recv()
            acc_ref[...] += dot3(rband_ref[k, 2], after[k])

        return acc_ref[...]

    def col_mix(v, which):
        high, low = split_bf16(v)
        for b in range(blocks):
            bmh_ref[b + 1] = high[:, b * LANE:(b + 1) * LANE]
            bml_ref[b + 1] = low[:, b * LANE:(b + 1) * LANE]
        total = None
        f32 = jnp.float32
        for t in range(3):
            xh = bmh_ref[t:t + blocks].reshape(blocks * 2 * height, LANE)
            xl = bml_ref[t:t + blocks].reshape(blocks * 2 * height, LANE)
            wh, wl = split_bf16(cband_ref[which, t])
            part = (jnp.dot(xh, wh, preferred_element_type=f32) + jnp.dot(xh, wl, preferred_element_type=f32)
                    + jnp.dot(xl, wh, preferred_element_type=f32))
            total = part if total is None else total + part
        total = total.reshape(blocks, 2 * height, 2 * LANE)
        real_part = total[:, :height, :LANE] - total[:, height:, LANE:]
        imag_part = total[:, :height, LANE:] + total[:, height:, :LANE]
        out = jnp.concatenate([real_part, imag_part], axis=1)
        return jnp.concatenate([out[b] for b in range(blocks)], axis=1)

    field_ref[...] = u0_ref[...]

    def forward(s, carry):
        u = field_ref[...]
        c = cos_ref[s]
        sn = sin_ref[s]
        ur = u[:height]
        ui = u[height:]
        y_store[s] = jnp.concatenate([c * ur - sn * ui, c * ui + sn * ur], axis=0)
        source = y_store.at[s]
        v = row_mix(s, source, y_store[s])
        field_ref[...] = col_mix(v, 0)
        finish(s, source)
        return carry

    lax.fori_loop(0, layers, forward, 0)
    u = field_ref[...]
    ur = u[:height]
    ui = u[height:]
    errors = ur * ur + ui * ui - inten_ref[...]
    field_ref[...] = jnp.concatenate([2.0 * errors * ur, 2.0 * errors * ui], axis=0)

    def backward(j, carry):
        s = layers - 1 - j
        k = layers + j
        b_store[j] = col_mix(field_ref[...], 1)
        source = b_store.at[j]
        acc = row_mix(k, source, b_store[j])
        ar = acc[:height]
        ai = acc[height:]
        y = y_store[s]
        terms_ref[s] = PHASE_SCALE * (y[:height] * ai - y[height:] * ar)
        c = cos_ref[s]
        sn = sin_ref[s]
        field_ref[...] = jnp.concatenate([c * ar + sn * ai, c * ai - sn * ar], axis=0)
        finish(k, source)
        return carry

    lax.fori_loop(0, layers, backward, 0)


def run_chain(u0, cosines, sines, intensity, row_band, col_band, rows):
    layers, height, columns = cosines.shape
    blocks = columns // LANE
    field = (2 * height, columns)
    return pl.pallas_call(
        functools.partial(chain_kernel, rows),
        out_shape=jax.ShapeDtypeStruct((layers, height, columns), jnp.float32),
        in_specs=[pl.BlockSpec(memory_space=pltpu.VMEM)] * 6,
        out_specs=pl.BlockSpec(memory_space=pltpu.VMEM),
        scratch_shapes=[
            pltpu.VMEM(field, jnp.float32),
            pltpu.VMEM(field, jnp.float32),
            pltpu.VMEM((layers,) + field, jnp.float32),
            pltpu.VMEM((layers,) + field, jnp.float32),
            pltpu.VMEM((2 * layers,) + field, jnp.float32),
            pltpu.VMEM((2 * layers,) + field, jnp.float32),
            pltpu.VMEM((blocks + 2, 2 * height, LANE), jnp.bfloat16),
            pltpu.VMEM((blocks + 2, 2 * height, LANE), jnp.bfloat16),
            pltpu.SemaphoreType.DMA((2 * layers,)),
            pltpu.SemaphoreType.DMA((2 * layers,)),
            pltpu.SemaphoreType.DMA((2 * layers,)),
            pltpu.SemaphoreType.DMA((2 * layers,)),
        ],
        compiler_params=pltpu.CompilerParams(
            collective_id=0, has_side_effects=True, vmem_limit_bytes=56 * 1024 * 1024),
    )(u0, cosines, sines, intensity, row_band, col_band)


def gather_kernel(sections, vol_ref, off_ref, vol_out, off_out, vol_slots, off_slots,
                  send_vol, send_off, recv_vol, recv_off):
    me = lax.axis_index("depth")
    barrier = pltpu.get_barrier_semaphore()
    for step in range(1, sections):
        peer = (me + step) % sections
        pl.semaphore_signal(barrier, 1, device_id={"depth": peer}, device_id_type=MESH)
    pl.semaphore_wait(barrier, sections - 1)

    def copies(step):
        peer = (me + step) % sections
        source = (me + sections - step) % sections
        out_vol = pltpu.make_async_remote_copy(
            src_ref=vol_ref.at[0], dst_ref=vol_slots.at[me], send_sem=send_vol.at[step],
            recv_sem=recv_vol.at[me], device_id={"depth": peer}, device_id_type=MESH)
        out_off = pltpu.make_async_remote_copy(
            src_ref=off_ref, dst_ref=off_slots.at[me], send_sem=send_off.at[step],
            recv_sem=recv_off.at[me], device_id={"depth": peer}, device_id_type=MESH)
        in_vol = pltpu.make_async_remote_copy(
            src_ref=vol_ref.at[0], dst_ref=vol_slots.at[source], send_sem=send_vol.at[step],
            recv_sem=recv_vol.at[source], device_id={"depth": peer}, device_id_type=MESH)
        in_off = pltpu.make_async_remote_copy(
            src_ref=off_ref, dst_ref=off_slots.at[source], send_sem=send_off.at[step],
            recv_sem=recv_off.at[source], device_id={"depth": peer}, device_id_type=MESH)
        return out_vol, out_off, in_vol, in_off

    for step in range(1, sections):
        out_vol, out_off, _, _ = copies(step)
        out_vol.start()
        out_off.start()
    vol_slots[me] = vol_ref[0]
    off_slots[me] = off_ref[...]
    for step in range(1, sections):
        out_vol, out_off, in_vol, in_off = copies(step)
        in_vol.wait_recv()
        in_off.wait_recv()
        out_vol.wait_send()
        out_off.wait_send()
    vol_out[...] = vol_slots[...]
    off_out[...] = off_slots[...]


def gather_depth(index_volume, offsets, sections):
    _, height, columns = index_volume.shape
    off_tile = jnp.broadcast_to(offsets.astype(jnp.float32)[:, None], (8, LANE))
    vol_shape = (sections, height, columns)
    off_shape = (sections, 8, LANE)
    return pl.pallas_call(
        functools.partial(gather_kernel, sections),
        out_shape=(jax.ShapeDtypeStruct(vol_shape, index_volume.dtype),
                   jax.ShapeDtypeStruct(off_shape, jnp.float32)),
        in_specs=[pl.BlockSpec(memory_space=pltpu.VMEM)] * 2,
        out_specs=(pl.BlockSpec(memory_space=pltpu.VMEM),) * 2,
        scratch_shapes=[
            pltpu.VMEM(vol_shape, index_volume.dtype),
            pltpu.VMEM(off_shape, jnp.float32),
            pltpu.SemaphoreType.DMA((sections,)),
            pltpu.SemaphoreType.DMA((sections,)),
            pltpu.SemaphoreType.DMA((sections,)),
            pltpu.SemaphoreType.DMA((sections,)),
        ],
        compiler_params=pltpu.CompilerParams(collective_id=1, has_side_effects=True),
    )(index_volume, off_tile)


def plane_wave(angle, row_start, height, columns, total_rows, total_cols):
    across = angle - TILTS // 2
    along = jnp.mod(3 * angle, TILTS) - TILTS // 2
    row_index = row_start + lax.broadcasted_iota(jnp.int32, (height, columns), 0)
    col_index = lax.broadcasted_iota(jnp.int32, (height, columns), 1)
    period = total_cols * total_rows
    cycles_int = jnp.mod(across * col_index * total_rows + along * row_index * total_cols, period)
    phase_arg = 2.0 * math.pi / period * cycles_int.astype(jnp.float32)
    return jnp.concatenate([jnp.cos(phase_arg), jnp.sin(phase_arg)], axis=0)


def body(index_volume, angles, offsets, measured):
    sections = lax.axis_size("depth")
    rows = lax.axis_size("row")
    section_no = lax.axis_index("depth")
    height = index_volume.shape[1]
    columns = index_volume.shape[2]
    row_start = lax.axis_index("row") * height
    total_rows = height * rows
    angle_count = angles.shape[0]
    angle_no = section_no % angle_count
    volume, shift_tiles = gather_depth(index_volume, offsets, sections)
    shifts = shift_tiles[:, 0, 0].astype(jnp.int32)
    intensity = lax.dynamic_index_in_dim(measured, angle_no, 0, keepdims=False).astype(jnp.float32)
    angle = lax.dynamic_index_in_dim(angles, angle_no, 0, keepdims=False)
    incident = plane_wave(angle, row_start, height, columns, total_rows, columns)
    phases = PHASE_SCALE * volume.astype(jnp.float32)
    terms = run_chain(incident, jnp.cos(phases), jnp.sin(phases), intensity,
                      row_bands(shifts, height), column_bands(), rows)
    own = lax.dynamic_index_in_dim(terms, section_no, 0, keepdims=True)
    for_partner = lax.dynamic_index_in_dim(terms, section_no ^ 1, 0, keepdims=True)
    pairs = [(i, i ^ 1) for i in range(sections)]
    received = lax.ppermute(for_partner, "depth", pairs)
    first = jnp.where(angle_no == 0, own, received)
    second = jnp.where(angle_no == 0, received, own)
    return first + second


def solution(mesh):
    in_specs = (P("depth", "row", None), P(), P("depth"), P(None, "row", None))
    out_specs = P("depth", "row", None)
    return jax.shard_map(body, mesh=mesh, in_specs=in_specs, out_specs=out_specs, check_vma=False)
```

```python
import functools
import math

import jax
import jax.numpy as jnp
from jax import lax
from jax.experimental import pallas as pl
from jax.experimental.pallas import tpu as pltpu
from jax.sharding import PartitionSpec as P

TILTS = 16
HALF = 10
SHIFT = 4
HALFCOL = 64
LANE = 128

PHASE_SCALE = 0.5
CHIRP_ROW = 1.3
CHIRP_COL = 1.7
MESH = pl.DeviceIdType.MESH


def kernel_values(distance, radius, chirp_rate):
    inside = jnp.abs(distance) <= radius
    phase_arg = chirp_rate / radius * distance * distance
    weight = 1.0 / math.sqrt(2 * radius + 1)
    real_part = jnp.where(inside, jnp.cos(phase_arg) * weight, 0.0)
    imag_part = jnp.where(inside, jnp.sin(phase_arg) * weight, 0.0)
    return (real_part, imag_part)


def split_bf16(x):
    high = x.astype(jnp.bfloat16)
    low = (x - high.astype(jnp.float32)).astype(jnp.bfloat16)
    return high, low


def complex_block(real_part, imag_part):
    top = jnp.concatenate([real_part, -imag_part], axis=-1)
    bottom = jnp.concatenate([imag_part, real_part], axis=-1)
    return jnp.concatenate([top, bottom], axis=-2)


def row_bands(shifts, height):
    layers = shifts.shape[0]
    signs = jnp.concatenate([jnp.ones((layers,), jnp.int32), -jnp.ones((layers,), jnp.int32)])
    used = jnp.concatenate([shifts, shifts[::-1]]) * signs
    extent = (2 * layers, 3, height, height)
    part = lax.broadcasted_iota(jnp.int32, extent, 1)
    target = lax.broadcasted_iota(jnp.int32, extent, 2)
    source = lax.broadcasted_iota(jnp.int32, extent, 3) + (part - 1) * height
    distance = (source - target - used[:, None, None, None]).astype(jnp.float32)
    real_part, imag_part = kernel_values(distance, HALF, CHIRP_ROW)
    imag_part = imag_part * signs[:, None, None, None].astype(jnp.float32)
    return complex_block(real_part, imag_part)


def column_bands():
    extent = (3, LANE, LANE)
    part = lax.broadcasted_iota(jnp.int32, extent, 0)
    source = lax.broadcasted_iota(jnp.int32, extent, 1) + (part - 1) * LANE
    target = lax.broadcasted_iota(jnp.int32, extent, 2)
    distance = (source - target).astype(jnp.float32)
    real_part, imag_part = kernel_values(distance, HALFCOL, CHIRP_COL)
    forward = jnp.concatenate([real_part, imag_part], axis=-1)
    adjoint = jnp.concatenate([real_part, -imag_part], axis=-1)
    return jnp.stack([forward, adjoint], axis=0)


def dot3(a, x):
    a_high, a_low = split_bf16(a)
    x_high, x_low = split_bf16(x)
    f32 = jnp.float32
    return (
        jnp.dot(a_high, x_high, preferred_element_type=f32)
        + jnp.dot(a_high, x_low, preferred_element_type=f32)
        + jnp.dot(a_low, x_high, preferred_element_type=f32)
    )


CHUNKS = 4


def chain_kernel(rows, u0_ref, cos_ref, sin_ref, inten_ref, rband_ref, cband_ref,
                 terms_ref, field_ref, acc_ref, y_store, b_store, before, after, bmh_ref, bml_ref,
                 send_dn, send_up, recv_bf, recv_af):
    me = lax.axis_index("row")
    layers, height, columns = cos_ref.shape
    blocks = columns // LANE
    width = columns // CHUNKS
    per_chunk = blocks // CHUNKS
    has_up = me > 0
    has_dn = me < rows - 1

    barrier = pltpu.get_barrier_semaphore()

    @pl.when(has_up)
    def _():
        pl.semaphore_signal(barrier, 1, device_id={"row": me - 1}, device_id_type=MESH)

    @pl.when(has_dn)
    def _():
        pl.semaphore_signal(barrier, 1, device_id={"row": me + 1}, device_id_type=MESH)

    peers = (me + rows - 1) // rows + (2 * rows - 2 - me) // rows
    pl.semaphore_wait(barrier, peers)

    zero_block = jnp.zeros((2 * height, LANE), jnp.bfloat16)
    for ref in (bmh_ref, bml_ref):
        ref[0] = zero_block
        ref[blocks + 1] = zero_block

    def copies(k, c, store):
        cols = pl.ds(c * width, width)
        slot = k * CHUNKS + c
        down = pltpu.make_async_remote_copy(
            src_ref=store.at[:, cols], dst_ref=before.at[k, :, cols], send_sem=send_dn.at[slot],
            recv_sem=recv_bf.at[slot], device_id={"row": me + 1}, device_id_type=MESH)
        up = pltpu.make_async_remote_copy(
            src_ref=store.at[:, cols], dst_ref=after.at[k, :, cols], send_sem=send_up.at[slot],
            recv_sem=recv_af.at[slot], device_id={"row": me - 1}, device_id_type=MESH)
        return down, up

    def start(k, c, store):
        down, up = copies(k, c, store)

        @pl.when(has_dn)
        def _():
            down.start()

        @pl.when(has_up)
        def _():
            up.start()

    def finish(k, store):
        for c in range(CHUNKS):
            down, up = copies(k, c, store)

            @pl.when(has_dn)
            def _():
                down.wait_send()

            @pl.when(has_up)
            def _():
                up.wait_send()

    def produce(k, chunk_value, store):
        for c in range(CHUNKS):
            store[:, c * width:(c + 1) * width] = chunk_value(c)
            if c >= 1:
                start(k, c - 1, store)
        acc_ref[...] = dot3(rband_ref[k, 1], store[...])
        start(k, CHUNKS - 1, store)

    def consume(k, store):
        for c in range(CHUNKS):
            down, up = copies(k, c, store)
            cols = slice(c * width, (c + 1) * width)

            @pl.when(has_up)
            def _():
                down.wait_recv()
                acc_ref[:, cols] += dot3(rband_ref[k, 0], before[k, :, cols])

            @pl.when(has_dn)
            def _():
                up.wait_recv()
                acc_ref[:, cols] += dot3(rband_ref[k, 2], after[k, :, cols])

    def load_blocks(v):
        high, low = split_bf16(v)
        for b in range(blocks):
            bmh_ref[b + 1] = high[:, b * LANE:(b + 1) * LANE]
            bml_ref[b + 1] = low[:, b * LANE:(b + 1) * LANE]

    def col_chunk(c, which):
        total = None
        f32 = jnp.float32
        first = c * per_chunk
        for t in range(3):
            xh = bmh_ref[first + t:first + t + per_chunk].reshape(per_chunk * 2 * height, LANE)
            xl = bml_ref[first + t:first + t + per_chunk].reshape(per_chunk * 2 * height, LANE)
            wh, wl = split_bf16(cband_ref[which, t])
            part = (jnp.dot(xh, wh, preferred_element_type=f32) + jnp.dot(xh, wl, preferred_element_type=f32)
                    + jnp.dot(xl, wh, preferred_element_type=f32))
            total = part if total is None else total + part
        total = total.reshape(per_chunk, 2 * height, 2 * LANE)
        real_part = total[:, :height, :LANE] - total[:, height:, LANE:]
        imag_part = total[:, :height, LANE:] + total[:, height:, :LANE]
        out = jnp.concatenate([real_part, imag_part], axis=1)
        return jnp.concatenate([out[b] for b in range(per_chunk)], axis=1)

    def rotated(s, c, u):
        cols = pl.ds(c * width, width)
        cs = cos_ref[s, :, cols]
        sn = sin_ref[s, :, cols]
        ur = u[:height]
        ui = u[height:]
        return jnp.concatenate([cs * ur - sn * ui, cs * ui + sn * ur], axis=0)

    produce(0, lambda c: rotated(0, c, u0_ref[:, c * width:(c + 1) * width]), y_store.at[0])
    consume(0, y_store.at[0])
    finish(0, y_store.at[0])

    def forward(s, carry):
        load_blocks(acc_ref[...])
        produce(s, lambda c: rotated(s, c, col_chunk(c, 0)), y_store.at[s])
        consume(s, y_store.at[s])
        finish(s, y_store.at[s])
        return carry

    lax.fori_loop(1, layers, forward, 0)
    load_blocks(acc_ref[...])
    for c in range(CHUNKS):
        field_ref[:, c * width:(c + 1) * width] = col_chunk(c, 0)
    u = field_ref[...]
    ur = u[:height]
    ui = u[height:]
    errors = ur * ur + ui * ui - inten_ref[...]
    field_ref[...] = jnp.concatenate([2.0 * errors * ur, 2.0 * errors * ui], axis=0)

    def backward(j, carry):
        s = layers - 1 - j
        k = layers + j
        load_blocks(field_ref[...])
        produce(k, lambda c: col_chunk(c, 1), b_store.at[j])
        consume(k, b_store.at[j])
        acc = acc_ref[...]
        ar = acc[:height]
        ai = acc[height:]
        y = y_store[s]
        terms_ref[s] = PHASE_SCALE * (y[:height] * ai - y[height:] * ar)
        cs = cos_ref[s]
        sn = sin_ref[s]
        field_ref[...] = jnp.concatenate([cs * ar + sn * ai, cs * ai - sn * ar], axis=0)
        finish(k, b_store.at[j])
        return carry

    lax.fori_loop(0, layers, backward, 0)


def run_chain(u0, cosines, sines, intensity, row_band, col_band, rows):
    layers, height, columns = cosines.shape
    blocks = columns // LANE
    field = (2 * height, columns)
    return pl.pallas_call(
        functools.partial(chain_kernel, rows),
        out_shape=jax.ShapeDtypeStruct((layers, height, columns), jnp.float32),
        in_specs=[pl.BlockSpec(memory_space=pltpu.VMEM)] * 6,
        out_specs=pl.BlockSpec(memory_space=pltpu.VMEM),
        scratch_shapes=[
            pltpu.VMEM(field, jnp.float32),
            pltpu.VMEM(field, jnp.float32),
            pltpu.VMEM((layers,) + field, jnp.float32),
            pltpu.VMEM((layers,) + field, jnp.float32),
            pltpu.VMEM((2 * layers,) + field, jnp.float32),
            pltpu.VMEM((2 * layers,) + field, jnp.float32),
            pltpu.VMEM((blocks + 2, 2 * height, LANE), jnp.bfloat16),
            pltpu.VMEM((blocks + 2, 2 * height, LANE), jnp.bfloat16),
            pltpu.SemaphoreType.DMA((2 * layers * CHUNKS,)),
            pltpu.SemaphoreType.DMA((2 * layers * CHUNKS,)),
            pltpu.SemaphoreType.DMA((2 * layers * CHUNKS,)),
            pltpu.SemaphoreType.DMA((2 * layers * CHUNKS,)),
        ],
        compiler_params=pltpu.CompilerParams(
            collective_id=0, has_side_effects=True, vmem_limit_bytes=56 * 1024 * 1024),
    )(u0, cosines, sines, intensity, row_band, col_band)


def gather_kernel(sections, vol_ref, off_ref, vol_out, off_out, vol_slots, off_slots,
                  send_vol, send_off, recv_vol, recv_off):
    me = lax.axis_index("depth")
    barrier = pltpu.get_barrier_semaphore()
    for step in range(1, sections):
        peer = (me + step) % sections
        pl.semaphore_signal(barrier, 1, device_id={"depth": peer}, device_id_type=MESH)
    pl.semaphore_wait(barrier, sections - 1)

    def copies(step):
        peer = (me + step) % sections
        source = (me + sections - step) % sections
        out_vol = pltpu.make_async_remote_copy(
            src_ref=vol_ref.at[0], dst_ref=vol_slots.at[me], send_sem=send_vol.at[step],
            recv_sem=recv_vol.at[me], device_id={"depth": peer}, device_id_type=MESH)
        out_off = pltpu.make_async_remote_copy(
            src_ref=off_ref, dst_ref=off_slots.at[me], send_sem=send_off.at[step],
            recv_sem=recv_off.at[me], device_id={"depth": peer}, device_id_type=MESH)
        in_vol = pltpu.make_async_remote_copy(
            src_ref=vol_ref.at[0], dst_ref=vol_slots.at[source], send_sem=send_vol.at[step],
            recv_sem=recv_vol.at[source], device_id={"depth": peer}, device_id_type=MESH)
        in_off = pltpu.make_async_remote_copy(
            src_ref=off_ref, dst_ref=off_slots.at[source], send_sem=send_off.at[step],
            recv_sem=recv_off.at[source], device_id={"depth": peer}, device_id_type=MESH)
        return out_vol, out_off, in_vol, in_off

    for step in range(1, sections):
        out_vol, out_off, _, _ = copies(step)
        out_vol.start()
        out_off.start()
    vol_slots[me] = vol_ref[0]
    off_slots[me] = off_ref[...]
    for step in range(1, sections):
        out_vol, out_off, in_vol, in_off = copies(step)
        in_vol.wait_recv()
        in_off.wait_recv()
        out_vol.wait_send()
        out_off.wait_send()
    vol_out[...] = vol_slots[...]
    off_out[...] = off_slots[...]


def gather_depth(index_volume, offsets, sections):
    _, height, columns = index_volume.shape
    off_tile = jnp.broadcast_to(offsets.astype(jnp.float32)[:, None], (8, LANE))
    vol_shape = (sections, height, columns)
    off_shape = (sections, 8, LANE)
    return pl.pallas_call(
        functools.partial(gather_kernel, sections),
        out_shape=(jax.ShapeDtypeStruct(vol_shape, index_volume.dtype),
                   jax.ShapeDtypeStruct(off_shape, jnp.float32)),
        in_specs=[pl.BlockSpec(memory_space=pltpu.VMEM)] * 2,
        out_specs=(pl.BlockSpec(memory_space=pltpu.VMEM),) * 2,
        scratch_shapes=[
            pltpu.VMEM(vol_shape, index_volume.dtype),
            pltpu.VMEM(off_shape, jnp.float32),
            pltpu.SemaphoreType.DMA((sections,)),
            pltpu.SemaphoreType.DMA((sections,)),
            pltpu.SemaphoreType.DMA((sections,)),
            pltpu.SemaphoreType.DMA((sections,)),
        ],
        compiler_params=pltpu.CompilerParams(collective_id=1, has_side_effects=True),
    )(index_volume, off_tile)


def plane_wave(angle, row_start, height, columns, total_rows, total_cols):
    across = angle - TILTS // 2
    along = jnp.mod(3 * angle, TILTS) - TILTS // 2
    row_index = row_start + lax.broadcasted_iota(jnp.int32, (height, columns), 0)
    col_index = lax.broadcasted_iota(jnp.int32, (height, columns), 1)
    period = total_cols * total_rows
    cycles_int = jnp.mod(across * col_index * total_rows + along * row_index * total_cols, period)
    phase_arg = 2.0 * math.pi / period * cycles_int.astype(jnp.float32)
    return jnp.concatenate([jnp.cos(phase_arg), jnp.sin(phase_arg)], axis=0)


def body(index_volume, angles, offsets, measured):
    sections = lax.axis_size("depth")
    rows = lax.axis_size("row")
    section_no = lax.axis_index("depth")
    height = index_volume.shape[1]
    columns = index_volume.shape[2]
    row_start = lax.axis_index("row") * height
    total_rows = height * rows
    angle_count = angles.shape[0]
    angle_no = section_no % angle_count
    volume, shift_tiles = gather_depth(index_volume, offsets, sections)
    shifts = shift_tiles[:, 0, 0].astype(jnp.int32)
    intensity = lax.dynamic_index_in_dim(measured, angle_no, 0, keepdims=False).astype(jnp.float32)
    angle = lax.dynamic_index_in_dim(angles, angle_no, 0, keepdims=False)
    incident = plane_wave(angle, row_start, height, columns, total_rows, columns)
    phases = PHASE_SCALE * volume.astype(jnp.float32)
    terms = run_chain(incident, jnp.cos(phases), jnp.sin(phases), intensity,
                      row_bands(shifts, height), column_bands(), rows)
    own = lax.dynamic_index_in_dim(terms, section_no, 0, keepdims=True)
    for_partner = lax.dynamic_index_in_dim(terms, section_no ^ 1, 0, keepdims=True)
    pairs = [(i, i ^ 1) for i in range(sections)]
    received = lax.ppermute(for_partner, "depth", pairs)
    first = jnp.where(angle_no == 0, own, received)
    second = jnp.where(angle_no == 0, received, own)
    return first + second


def solution(mesh):
    in_specs = (P("depth", "row", None), P(), P("depth"), P(None, "row", None))
    out_specs = P("depth", "row", None)
    return jax.shard_map(body, mesh=mesh, in_specs=in_specs, out_specs=out_specs, check_vma=False)
```

```python
import functools
import math

import jax
import jax.numpy as jnp
from jax import lax
from jax.experimental import pallas as pl
from jax.experimental.pallas import tpu as pltpu
from jax.sharding import PartitionSpec as P

TILTS = 16
HALF = 10
SHIFT = 4
HALFCOL = 64
LANE = 128

PHASE_SCALE = 0.5
CHIRP_ROW = 1.3
CHIRP_COL = 1.7
MESH = pl.DeviceIdType.MESH


def kernel_values(distance, radius, chirp_rate):
    inside = jnp.abs(distance) <= radius
    phase_arg = chirp_rate / radius * distance * distance
    weight = 1.0 / math.sqrt(2 * radius + 1)
    real_part = jnp.where(inside, jnp.cos(phase_arg) * weight, 0.0)
    imag_part = jnp.where(inside, jnp.sin(phase_arg) * weight, 0.0)
    return (real_part, imag_part)


def split_bf16(x):
    high = x.astype(jnp.bfloat16)
    low = (x - high.astype(jnp.float32)).astype(jnp.bfloat16)
    return high, low


def complex_block(real_part, imag_part):
    top = jnp.concatenate([real_part, -imag_part], axis=-1)
    bottom = jnp.concatenate([imag_part, real_part], axis=-1)
    return jnp.concatenate([top, bottom], axis=-2)


def row_bands(shifts, height):
    layers = shifts.shape[0]
    signs = jnp.concatenate([jnp.ones((layers,), jnp.int32), -jnp.ones((layers,), jnp.int32)])
    used = jnp.concatenate([shifts, shifts[::-1]]) * signs
    extent = (2 * layers, 3, height, height)
    part = lax.broadcasted_iota(jnp.int32, extent, 1)
    target = lax.broadcasted_iota(jnp.int32, extent, 2)
    source = lax.broadcasted_iota(jnp.int32, extent, 3) + (part - 1) * height
    distance = (source - target - used[:, None, None, None]).astype(jnp.float32)
    real_part, imag_part = kernel_values(distance, HALF, CHIRP_ROW)
    imag_part = imag_part * signs[:, None, None, None].astype(jnp.float32)
    return complex_block(real_part, imag_part)


def column_bands():
    extent = (3, LANE, LANE)
    part = lax.broadcasted_iota(jnp.int32, extent, 0)
    source = lax.broadcasted_iota(jnp.int32, extent, 1) + (part - 1) * LANE
    target = lax.broadcasted_iota(jnp.int32, extent, 2)
    distance = (source - target).astype(jnp.float32)
    real_part, imag_part = kernel_values(distance, HALFCOL, CHIRP_COL)
    forward = jnp.concatenate([real_part, imag_part], axis=-1)
    adjoint = jnp.concatenate([real_part, -imag_part], axis=-1)
    return jnp.stack([forward, adjoint], axis=0)


def dot3(a, x):
    a_high, a_low = split_bf16(a)
    x_high, x_low = split_bf16(x)
    f32 = jnp.float32
    return (
        jnp.dot(a_high, x_high, preferred_element_type=f32)
        + jnp.dot(a_high, x_low, preferred_element_type=f32)
        + jnp.dot(a_low, x_high, preferred_element_type=f32)
    )


CHUNKS = 4


def chain_kernel(rows, u0_ref, cos_ref, sin_ref, inten_ref, rband_ref, cband_ref,
                 out_ref, terms_ref, partner_ref, field_ref, acc_ref, y_store, b_store, before, after,
                 bmh_ref, bml_ref, send_dn, send_up, recv_bf, recv_af, send_pair, recv_pair):
    me = lax.axis_index("row")
    section = lax.axis_index("depth")
    partner = section + 1 - 2 * (section % 2)
    layers, height, columns = cos_ref.shape
    blocks = columns // LANE
    width = columns // CHUNKS
    per_chunk = blocks // CHUNKS
    has_up = me > 0
    has_dn = me < rows - 1

    barrier = pltpu.get_barrier_semaphore()

    @pl.when(has_up)
    def _():
        pl.semaphore_signal(barrier, 1, device_id={"row": me - 1}, device_id_type=MESH)

    @pl.when(has_dn)
    def _():
        pl.semaphore_signal(barrier, 1, device_id={"row": me + 1}, device_id_type=MESH)

    pl.semaphore_signal(barrier, 1, device_id={"depth": partner}, device_id_type=MESH)
    peers = (me + rows - 1) // rows + (2 * rows - 2 - me) // rows
    pl.semaphore_wait(barrier, peers + 1)

    zero_block = jnp.zeros((2 * height, LANE), jnp.bfloat16)
    for ref in (bmh_ref, bml_ref):
        ref[0] = zero_block
        ref[blocks + 1] = zero_block

    def copies(k, c, store):
        cols = pl.ds(c * width, width)
        slot = k * CHUNKS + c
        down = pltpu.make_async_remote_copy(
            src_ref=store.at[:, cols], dst_ref=before.at[k, :, cols], send_sem=send_dn.at[slot],
            recv_sem=recv_bf.at[slot], device_id={"row": me + 1}, device_id_type=MESH)
        up = pltpu.make_async_remote_copy(
            src_ref=store.at[:, cols], dst_ref=after.at[k, :, cols], send_sem=send_up.at[slot],
            recv_sem=recv_af.at[slot], device_id={"row": me - 1}, device_id_type=MESH)
        return down, up

    def start(k, c, store):
        down, up = copies(k, c, store)

        @pl.when(has_dn)
        def _():
            down.start()

        @pl.when(has_up)
        def _():
            up.start()

    def finish(k, store):
        for c in range(CHUNKS):
            down, up = copies(k, c, store)

            @pl.when(has_dn)
            def _():
                down.wait_send()

            @pl.when(has_up)
            def _():
                up.wait_send()

    def produce(k, chunk_value, store):
        for c in range(CHUNKS):
            store[:, c * width:(c + 1) * width] = chunk_value(c)
            if c >= 1:
                start(k, c - 1, store)
        acc_ref[...] = dot3(rband_ref[k, 1], store[...])
        start(k, CHUNKS - 1, store)

    def consume(k, store):
        for c in range(CHUNKS):
            down, up = copies(k, c, store)
            cols = slice(c * width, (c + 1) * width)

            @pl.when(has_up)
            def _():
                down.wait_recv()
                acc_ref[:, cols] += dot3(rband_ref[k, 0], before[k, :, cols])

            @pl.when(has_dn)
            def _():
                up.wait_recv()
                acc_ref[:, cols] += dot3(rband_ref[k, 2], after[k, :, cols])

    def load_blocks(v):
        high, low = split_bf16(v)
        for b in range(blocks):
            bmh_ref[b + 1] = high[:, b * LANE:(b + 1) * LANE]
            bml_ref[b + 1] = low[:, b * LANE:(b + 1) * LANE]

    def col_chunk(c, which):
        total = None
        f32 = jnp.float32
        first = c * per_chunk
        for t in range(3):
            xh = bmh_ref[first + t:first + t + per_chunk].reshape(per_chunk * 2 * height, LANE)
            xl = bml_ref[first + t:first + t + per_chunk].reshape(per_chunk * 2 * height, LANE)
            wh, wl = split_bf16(cband_ref[which, t])
            part = (jnp.dot(xh, wh, preferred_element_type=f32) + jnp.dot(xh, wl, preferred_element_type=f32)
                    + jnp.dot(xl, wh, preferred_element_type=f32))
            total = part if total is None else total + part
        total = total.reshape(per_chunk, 2 * height, 2 * LANE)
        real_part = total[:, :height, :LANE] - total[:, height:, LANE:]
        imag_part = total[:, :height, LANE:] + total[:, height:, :LANE]
        out = jnp.concatenate([real_part, imag_part], axis=1)
        return jnp.concatenate([out[b] for b in range(per_chunk)], axis=1)

    def rotated(s, c, u):
        cols = pl.ds(c * width, width)
        cs = cos_ref[s, :, cols]
        sn = sin_ref[s, :, cols]
        ur = u[:height]
        ui = u[height:]
        return jnp.concatenate([cs * ur - sn * ui, cs * ui + sn * ur], axis=0)

    produce(0, lambda c: rotated(0, c, u0_ref[:, c * width:(c + 1) * width]), y_store.at[0])
    consume(0, y_store.at[0])
    finish(0, y_store.at[0])

    def forward(s, carry):
        load_blocks(acc_ref[...])
        produce(s, lambda c: rotated(s, c, col_chunk(c, 0)), y_store.at[s])
        consume(s, y_store.at[s])
        finish(s, y_store.at[s])
        return carry

    lax.fori_loop(1, layers, forward, 0)
    load_blocks(acc_ref[...])
    for c in range(CHUNKS):
        field_ref[:, c * width:(c + 1) * width] = col_chunk(c, 0)
    u = field_ref[...]
    ur = u[:height]
    ui = u[height:]
    errors = ur * ur + ui * ui - inten_ref[...]
    field_ref[...] = jnp.concatenate([2.0 * errors * ur, 2.0 * errors * ui], axis=0)

    def backward(j, carry):
        s = layers - 1 - j
        k = layers + j
        load_blocks(field_ref[...])
        produce(k, lambda c: col_chunk(c, 1), b_store.at[j])
        consume(k, b_store.at[j])
        acc = acc_ref[...]
        ar = acc[:height]
        ai = acc[height:]
        y = y_store[s]
        terms_ref[s] = PHASE_SCALE * (y[:height] * ai - y[height:] * ar)
        cs = cos_ref[s]
        sn = sin_ref[s]
        field_ref[...] = jnp.concatenate([cs * ar + sn * ai, cs * ai - sn * ar], axis=0)
        finish(k, b_store.at[j])
        return carry

    lax.fori_loop(0, layers, backward, 0)
    own = terms_ref[section]
    exchange = pltpu.make_async_remote_copy(
        src_ref=terms_ref.at[partner], dst_ref=partner_ref, send_sem=send_pair, recv_sem=recv_pair,
        device_id={"depth": partner}, device_id_type=MESH)
    exchange.start()
    exchange.wait_send()
    exchange.wait_recv()
    out_ref[0] = own + partner_ref[...]


def run_chain(u0, cosines, sines, intensity, row_band, col_band, rows):
    layers, height, columns = cosines.shape
    blocks = columns // LANE
    field = (2 * height, columns)
    return pl.pallas_call(
        functools.partial(chain_kernel, rows),
        out_shape=jax.ShapeDtypeStruct((1, height, columns), jnp.float32),
        in_specs=[pl.BlockSpec(memory_space=pltpu.VMEM)] * 6,
        out_specs=pl.BlockSpec(memory_space=pltpu.VMEM),
        scratch_shapes=[
            pltpu.VMEM((layers, height, columns), jnp.float32),
            pltpu.VMEM((height, columns), jnp.float32),
            pltpu.VMEM(field, jnp.float32),
            pltpu.VMEM(field, jnp.float32),
            pltpu.VMEM((layers,) + field, jnp.float32),
            pltpu.VMEM((layers,) + field, jnp.float32),
            pltpu.VMEM((2 * layers,) + field, jnp.float32),
            pltpu.VMEM((2 * layers,) + field, jnp.float32),
            pltpu.VMEM((blocks + 2, 2 * height, LANE), jnp.bfloat16),
            pltpu.VMEM((blocks + 2, 2 * height, LANE), jnp.bfloat16),
            pltpu.SemaphoreType.DMA((2 * layers * CHUNKS,)),
            pltpu.SemaphoreType.DMA((2 * layers * CHUNKS,)),
            pltpu.SemaphoreType.DMA((2 * layers * CHUNKS,)),
            pltpu.SemaphoreType.DMA((2 * layers * CHUNKS,)),
            pltpu.SemaphoreType.DMA,
            pltpu.SemaphoreType.DMA,
        ],
        compiler_params=pltpu.CompilerParams(
            collective_id=0, has_side_effects=True, vmem_limit_bytes=56 * 1024 * 1024),
    )(u0, cosines, sines, intensity, row_band, col_band)


def gather_kernel(sections, vol_ref, off_ref, vol_out, off_out, vol_slots, off_slots,
                  send_vol, send_off, recv_vol, recv_off):
    me = lax.axis_index("depth")
    barrier = pltpu.get_barrier_semaphore()
    for step in range(1, sections):
        peer = (me + step) % sections
        pl.semaphore_signal(barrier, 1, device_id={"depth": peer}, device_id_type=MESH)
    pl.semaphore_wait(barrier, sections - 1)

    def copies(step):
        peer = (me + step) % sections
        source = (me + sections - step) % sections
        out_vol = pltpu.make_async_remote_copy(
            src_ref=vol_ref.at[0], dst_ref=vol_slots.at[me], send_sem=send_vol.at[step],
            recv_sem=recv_vol.at[me], device_id={"depth": peer}, device_id_type=MESH)
        out_off = pltpu.make_async_remote_copy(
            src_ref=off_ref, dst_ref=off_slots.at[me], send_sem=send_off.at[step],
            recv_sem=recv_off.at[me], device_id={"depth": peer}, device_id_type=MESH)
        in_vol = pltpu.make_async_remote_copy(
            src_ref=vol_ref.at[0], dst_ref=vol_slots.at[source], send_sem=send_vol.at[step],
            recv_sem=recv_vol.at[source], device_id={"depth": peer}, device_id_type=MESH)
        in_off = pltpu.make_async_remote_copy(
            src_ref=off_ref, dst_ref=off_slots.at[source], send_sem=send_off.at[step],
            recv_sem=recv_off.at[source], device_id={"depth": peer}, device_id_type=MESH)
        return out_vol, out_off, in_vol, in_off

    for step in range(1, sections):
        out_vol, out_off, _, _ = copies(step)
        out_vol.start()
        out_off.start()
    vol_slots[me] = vol_ref[0]
    off_slots[me] = off_ref[...]
    for step in range(1, sections):
        out_vol, out_off, in_vol, in_off = copies(step)
        in_vol.wait_recv()
        in_off.wait_recv()
        out_vol.wait_send()
        out_off.wait_send()
    vol_out[...] = vol_slots[...]
    off_out[...] = off_slots[...]


def gather_depth(index_volume, offsets, sections):
    _, height, columns = index_volume.shape
    off_tile = jnp.broadcast_to(offsets.astype(jnp.float32)[:, None], (8, LANE))
    vol_shape = (sections, height, columns)
    off_shape = (sections, 8, LANE)
    return pl.pallas_call(
        functools.partial(gather_kernel, sections),
        out_shape=(jax.ShapeDtypeStruct(vol_shape, index_volume.dtype),
                   jax.ShapeDtypeStruct(off_shape, jnp.float32)),
        in_specs=[pl.BlockSpec(memory_space=pltpu.VMEM)] * 2,
        out_specs=(pl.BlockSpec(memory_space=pltpu.VMEM),) * 2,
        scratch_shapes=[
            pltpu.VMEM(vol_shape, index_volume.dtype),
            pltpu.VMEM(off_shape, jnp.float32),
            pltpu.SemaphoreType.DMA((sections,)),
            pltpu.SemaphoreType.DMA((sections,)),
            pltpu.SemaphoreType.DMA((sections,)),
            pltpu.SemaphoreType.DMA((sections,)),
        ],
        compiler_params=pltpu.CompilerParams(collective_id=1, has_side_effects=True),
    )(index_volume, off_tile)


def plane_wave(angle, row_start, height, columns, total_rows, total_cols):
    across = angle - TILTS // 2
    along = jnp.mod(3 * angle, TILTS) - TILTS // 2
    row_index = row_start + lax.broadcasted_iota(jnp.int32, (height, columns), 0)
    col_index = lax.broadcasted_iota(jnp.int32, (height, columns), 1)
    period = total_cols * total_rows
    cycles_int = jnp.mod(across * col_index * total_rows + along * row_index * total_cols, period)
    phase_arg = 2.0 * math.pi / period * cycles_int.astype(jnp.float32)
    return jnp.concatenate([jnp.cos(phase_arg), jnp.sin(phase_arg)], axis=0)


def body(index_volume, angles, offsets, measured):
    sections = lax.axis_size("depth")
    rows = lax.axis_size("row")
    section_no = lax.axis_index("depth")
    height = index_volume.shape[1]
    columns = index_volume.shape[2]
    row_start = lax.axis_index("row") * height
    total_rows = height * rows
    angle_count = angles.shape[0]
    angle_no = section_no % angle_count
    volume, shift_tiles = gather_depth(index_volume, offsets, sections)
    shifts = shift_tiles[:, 0, 0].astype(jnp.int32)
    intensity = lax.dynamic_index_in_dim(measured, angle_no, 0, keepdims=False).astype(jnp.float32)
    angle = lax.dynamic_index_in_dim(angles, angle_no, 0, keepdims=False)
    incident = plane_wave(angle, row_start, height, columns, total_rows, columns)
    phases = PHASE_SCALE * volume.astype(jnp.float32)
    return run_chain(incident, jnp.cos(phases), jnp.sin(phases), intensity,
                     row_bands(shifts, height), column_bands(), rows)


def solution(mesh):
    in_specs = (P("depth", "row", None), P(), P("depth"), P(None, "row", None))
    out_specs = P("depth", "row", None)
    return jax.shard_map(body, mesh=mesh, in_specs=in_specs, out_specs=out_specs, check_vma=False)
```

```python
import functools
import math

import jax
import jax.numpy as jnp
from jax import lax
from jax.experimental import pallas as pl
from jax.experimental.pallas import tpu as pltpu
from jax.sharding import PartitionSpec as P

TILTS = 16
HALF = 10
SHIFT = 4
HALFCOL = 64
LANE = 128

PHASE_SCALE = 0.5
CHIRP_ROW = 1.3
CHIRP_COL = 1.7
MESH = pl.DeviceIdType.MESH


def kernel_values(distance, radius, chirp_rate):
    inside = jnp.abs(distance) <= radius
    phase_arg = chirp_rate / radius * distance * distance
    weight = 1.0 / math.sqrt(2 * radius + 1)
    real_part = jnp.where(inside, jnp.cos(phase_arg) * weight, 0.0)
    imag_part = jnp.where(inside, jnp.sin(phase_arg) * weight, 0.0)
    return (real_part, imag_part)


def split_bf16(x):
    high = x.astype(jnp.bfloat16)
    low = (x - high.astype(jnp.float32)).astype(jnp.bfloat16)
    return high, low


def complex_block(real_part, imag_part):
    top = jnp.concatenate([real_part, -imag_part], axis=-1)
    bottom = jnp.concatenate([imag_part, real_part], axis=-1)
    return jnp.concatenate([top, bottom], axis=-2)


def row_bands(shifts, height):
    layers = shifts.shape[0]
    signs = jnp.concatenate([jnp.ones((layers,), jnp.int32), -jnp.ones((layers,), jnp.int32)])
    used = jnp.concatenate([shifts, shifts[::-1]]) * signs
    extent = (2 * layers, 3, height, height)
    part = lax.broadcasted_iota(jnp.int32, extent, 1)
    target = lax.broadcasted_iota(jnp.int32, extent, 2)
    source = lax.broadcasted_iota(jnp.int32, extent, 3) + (part - 1) * height
    distance = (source - target - used[:, None, None, None]).astype(jnp.float32)
    real_part, imag_part = kernel_values(distance, HALF, CHIRP_ROW)
    imag_part = imag_part * signs[:, None, None, None].astype(jnp.float32)
    return complex_block(real_part, imag_part)


def column_bands():
    extent = (3, LANE, LANE)
    part = lax.broadcasted_iota(jnp.int32, extent, 0)
    source = lax.broadcasted_iota(jnp.int32, extent, 1) + (part - 1) * LANE
    target = lax.broadcasted_iota(jnp.int32, extent, 2)
    distance = (source - target).astype(jnp.float32)
    real_part, imag_part = kernel_values(distance, HALFCOL, CHIRP_COL)
    forward = jnp.concatenate([real_part, imag_part], axis=-1)
    adjoint = jnp.concatenate([real_part, -imag_part], axis=-1)
    return jnp.stack([forward, adjoint], axis=0)


def dot3(a, x):
    a_high, a_low = split_bf16(a)
    x_high, x_low = split_bf16(x)
    f32 = jnp.float32
    return (
        jnp.dot(a_high, x_high, preferred_element_type=f32)
        + jnp.dot(a_high, x_low, preferred_element_type=f32)
        + jnp.dot(a_low, x_high, preferred_element_type=f32)
    )


CHUNKS = 4


def chain_kernel(rows, u0_ref, cos_ref, sin_ref, inten_ref, rband_ref, cband_ref,
                 out_ref, terms_ref, partner_ref, field_ref, acc_ref, y_store, b_store, before, after,
                 bmh_ref, bml_ref, send_dn, send_up, recv_bf, recv_af, send_pair, recv_pair):
    me = lax.axis_index("row")
    section = lax.axis_index("depth")
    partner = section + 1 - 2 * (section % 2)
    layers, height, columns = cos_ref.shape
    blocks = columns // LANE
    width = columns // CHUNKS
    per_chunk = blocks // CHUNKS
    has_up = me > 0
    has_dn = me < rows - 1

    barrier = pltpu.get_barrier_semaphore()

    @pl.when(has_up)
    def _():
        pl.semaphore_signal(barrier, 1, device_id={"row": me - 1}, device_id_type=MESH)

    @pl.when(has_dn)
    def _():
        pl.semaphore_signal(barrier, 1, device_id={"row": me + 1}, device_id_type=MESH)

    pl.semaphore_signal(barrier, 1, device_id={"depth": partner}, device_id_type=MESH)
    peers = (me + rows - 1) // rows + (2 * rows - 2 - me) // rows
    pl.semaphore_wait(barrier, peers + 1)

    zero_block = jnp.zeros((2 * height, LANE), jnp.bfloat16)
    for ref in (bmh_ref, bml_ref):
        ref[0] = zero_block
        ref[blocks + 1] = zero_block

    def copies(k, c, store):
        cols = pl.ds(c * width, width)
        slot = k * CHUNKS + c
        down = pltpu.make_async_remote_copy(
            src_ref=store.at[:, cols], dst_ref=before.at[k, :, cols], send_sem=send_dn.at[slot],
            recv_sem=recv_bf.at[slot], device_id={"row": me + 1}, device_id_type=MESH)
        up = pltpu.make_async_remote_copy(
            src_ref=store.at[:, cols], dst_ref=after.at[k, :, cols], send_sem=send_up.at[slot],
            recv_sem=recv_af.at[slot], device_id={"row": me - 1}, device_id_type=MESH)
        return down, up

    def start(k, c, store):
        down, up = copies(k, c, store)

        @pl.when(has_dn)
        def _():
            down.start()

        @pl.when(has_up)
        def _():
            up.start()

    def finish(k, store):
        for c in range(CHUNKS):
            down, up = copies(k, c, store)

            @pl.when(has_dn)
            def _():
                down.wait_send()

            @pl.when(has_up)
            def _():
                up.wait_send()

    def halo(k, c, store):
        down, up = copies(k, c, store)
        cols = pl.ds(c * width, width)
        slot = k % 2

        @pl.when(has_up)
        def _():
            down.wait_recv()
            acc_ref[slot, :, cols] += dot3(rband_ref[k, 0], before[k, :, cols])

        @pl.when(has_dn)
        def _():
            up.wait_recv()
            acc_ref[slot, :, cols] += dot3(rband_ref[k, 2], after[k, :, cols])

        return acc_ref[slot, :, cols]

    def emit(k, c, store, value):
        cols = pl.ds(c * width, width)
        store[:, cols] = value
        acc_ref[k % 2, :, cols] = dot3(rband_ref[k, 1], store[:, cols])
        start(k, c, store)

    def write_blocks(c, x):
        high, low = split_bf16(x)
        for b in range(per_chunk):
            bmh_ref[c * per_chunk + b + 1] = high[:, b * LANE:(b + 1) * LANE]
            bml_ref[c * per_chunk + b + 1] = low[:, b * LANE:(b + 1) * LANE]

    def wave(k, store, store_next, finish_chunk, make_chunk):
        for c in range(CHUNKS):
            write_blocks(c, finish_chunk(c, halo(k, c, store)))
            if c >= 1:
                emit(k + 1, c - 1, store_next, make_chunk(c - 1))
        emit(k + 1, CHUNKS - 1, store_next, make_chunk(CHUNKS - 1))
        finish(k, store)

    def col_chunk(c, which):
        total = None
        f32 = jnp.float32
        first = c * per_chunk
        for t in range(3):
            xh = bmh_ref[first + t:first + t + per_chunk].reshape(per_chunk * 2 * height, LANE)
            xl = bml_ref[first + t:first + t + per_chunk].reshape(per_chunk * 2 * height, LANE)
            wh, wl = split_bf16(cband_ref[which, t])
            part = (jnp.dot(xh, wh, preferred_element_type=f32) + jnp.dot(xh, wl, preferred_element_type=f32)
                    + jnp.dot(xl, wh, preferred_element_type=f32))
            total = part if total is None else total + part
        total = total.reshape(per_chunk, 2 * height, 2 * LANE)
        real_part = total[:, :height, :LANE] - total[:, height:, LANE:]
        imag_part = total[:, :height, LANE:] + total[:, height:, :LANE]
        out = jnp.concatenate([real_part, imag_part], axis=1)
        return jnp.concatenate([out[b] for b in range(per_chunk)], axis=1)

    def rotated(s, c, u):
        cols = pl.ds(c * width, width)
        cs = cos_ref[s, :, cols]
        sn = sin_ref[s, :, cols]
        ur = u[:height]
        ui = u[height:]
        return jnp.concatenate([cs * ur - sn * ui, cs * ui + sn * ur], axis=0)

    def adjoint_chunk(s, c, a):
        cols = pl.ds(c * width, width)
        ar = a[:height]
        ai = a[height:]
        y = y_store[s, :, cols]
        terms_ref[s, :, cols] = PHASE_SCALE * (y[:height] * ai - y[height:] * ar)
        cs = cos_ref[s, :, cols]
        sn = sin_ref[s, :, cols]
        return jnp.concatenate([cs * ar + sn * ai, cs * ai - sn * ar], axis=0)

    for c in range(CHUNKS):
        emit(0, c, y_store.at[0], rotated(0, c, u0_ref[:, c * width:(c + 1) * width]))

    def forward(k, carry):
        wave(k, y_store.at[k], y_store.at[k + 1], lambda c, a: a,
             lambda c: rotated(k + 1, c, col_chunk(c, 0)))
        return carry

    lax.fori_loop(0, layers - 1, forward, 0)
    for c in range(CHUNKS):
        write_blocks(c, halo(layers - 1, c, y_store.at[layers - 1]))
    finish(layers - 1, y_store.at[layers - 1])
    for c in range(CHUNKS):
        field_ref[:, c * width:(c + 1) * width] = col_chunk(c, 0)
    u = field_ref[...]
    ur = u[:height]
    ui = u[height:]
    errors = ur * ur + ui * ui - inten_ref[...]
    field_ref[...] = jnp.concatenate([2.0 * errors * ur, 2.0 * errors * ui], axis=0)
    for c in range(CHUNKS):
        write_blocks(c, field_ref[:, c * width:(c + 1) * width])
    for c in range(CHUNKS):
        emit(layers, c, b_store.at[0], col_chunk(c, 1))

    def backward(j, carry):
        s = layers - 1 - j
        wave(layers + j, b_store.at[j], b_store.at[j + 1], lambda c, a: adjoint_chunk(s, c, a),
             lambda c: col_chunk(c, 1))
        return carry

    lax.fori_loop(0, layers - 1, backward, 0)
    last = 2 * layers - 1
    for c in range(CHUNKS):
        adjoint_chunk(0, c, halo(last, c, b_store.at[layers - 1]))
    finish(last, b_store.at[layers - 1])
    own = terms_ref[section]
    exchange = pltpu.make_async_remote_copy(
        src_ref=terms_ref.at[partner], dst_ref=partner_ref, send_sem=send_pair, recv_sem=recv_pair,
        device_id={"depth": partner}, device_id_type=MESH)
    exchange.start()
    exchange.wait_send()
    exchange.wait_recv()
    out_ref[0] = own + partner_ref[...]


def run_chain(u0, cosines, sines, intensity, row_band, col_band, rows):
    layers, height, columns = cosines.shape
    blocks = columns // LANE
    field = (2 * height, columns)
    return pl.pallas_call(
        functools.partial(chain_kernel, rows),
        out_shape=jax.ShapeDtypeStruct((1, height, columns), jnp.float32),
        in_specs=[pl.BlockSpec(memory_space=pltpu.VMEM)] * 6,
        out_specs=pl.BlockSpec(memory_space=pltpu.VMEM),
        scratch_shapes=[
            pltpu.VMEM((layers, height, columns), jnp.float32),
            pltpu.VMEM((height, columns), jnp.float32),
            pltpu.VMEM(field, jnp.float32),
            pltpu.VMEM((2,) + field, jnp.float32),
            pltpu.VMEM((layers,) + field, jnp.float32),
            pltpu.VMEM((layers,) + field, jnp.float32),
            pltpu.VMEM((2 * layers,) + field, jnp.float32),
            pltpu.VMEM((2 * layers,) + field, jnp.float32),
            pltpu.VMEM((blocks + 2, 2 * height, LANE), jnp.bfloat16),
            pltpu.VMEM((blocks + 2, 2 * height, LANE), jnp.bfloat16),
            pltpu.SemaphoreType.DMA((2 * layers * CHUNKS,)),
            pltpu.SemaphoreType.DMA((2 * layers * CHUNKS,)),
            pltpu.SemaphoreType.DMA((2 * layers * CHUNKS,)),
            pltpu.SemaphoreType.DMA((2 * layers * CHUNKS,)),
            pltpu.SemaphoreType.DMA,
            pltpu.SemaphoreType.DMA,
        ],
        compiler_params=pltpu.CompilerParams(
            collective_id=0, has_side_effects=True, vmem_limit_bytes=56 * 1024 * 1024),
    )(u0, cosines, sines, intensity, row_band, col_band)


def gather_kernel(sections, vol_ref, off_ref, vol_out, off_out, vol_slots, off_slots,
                  send_vol, send_off, recv_vol, recv_off):
    me = lax.axis_index("depth")
    barrier = pltpu.get_barrier_semaphore()
    for step in range(1, sections):
        peer = (me + step) % sections
        pl.semaphore_signal(barrier, 1, device_id={"depth": peer}, device_id_type=MESH)
    pl.semaphore_wait(barrier, sections - 1)

    def copies(step):
        peer = (me + step) % sections
        source = (me + sections - step) % sections
        out_vol = pltpu.make_async_remote_copy(
            src_ref=vol_ref.at[0], dst_ref=vol_slots.at[me], send_sem=send_vol.at[step],
            recv_sem=recv_vol.at[me], device_id={"depth": peer}, device_id_type=MESH)
        out_off = pltpu.make_async_remote_copy(
            src_ref=off_ref, dst_ref=off_slots.at[me], send_sem=send_off.at[step],
            recv_sem=recv_off.at[me], device_id={"depth": peer}, device_id_type=MESH)
        in_vol = pltpu.make_async_remote_copy(
            src_ref=vol_ref.at[0], dst_ref=vol_slots.at[source], send_sem=send_vol.at[step],
            recv_sem=recv_vol.at[source], device_id={"depth": peer}, device_id_type=MESH)
        in_off = pltpu.make_async_remote_copy(
            src_ref=off_ref, dst_ref=off_slots.at[source], send_sem=send_off.at[step],
            recv_sem=recv_off.at[source], device_id={"depth": peer}, device_id_type=MESH)
        return out_vol, out_off, in_vol, in_off

    for step in range(1, sections):
        out_vol, out_off, _, _ = copies(step)
        out_vol.start()
        out_off.start()
    vol_slots[me] = vol_ref[0]
    off_slots[me] = off_ref[...]
    for step in range(1, sections):
        out_vol, out_off, in_vol, in_off = copies(step)
        in_vol.wait_recv()
        in_off.wait_recv()
        out_vol.wait_send()
        out_off.wait_send()
    vol_out[...] = vol_slots[...]
    off_out[...] = off_slots[...]


def gather_depth(index_volume, offsets, sections):
    _, height, columns = index_volume.shape
    off_tile = jnp.broadcast_to(offsets.astype(jnp.float32)[:, None], (8, LANE))
    vol_shape = (sections, height, columns)
    off_shape = (sections, 8, LANE)
    return pl.pallas_call(
        functools.partial(gather_kernel, sections),
        out_shape=(jax.ShapeDtypeStruct(vol_shape, index_volume.dtype),
                   jax.ShapeDtypeStruct(off_shape, jnp.float32)),
        in_specs=[pl.BlockSpec(memory_space=pltpu.VMEM)] * 2,
        out_specs=(pl.BlockSpec(memory_space=pltpu.VMEM),) * 2,
        scratch_shapes=[
            pltpu.VMEM(vol_shape, index_volume.dtype),
            pltpu.VMEM(off_shape, jnp.float32),
            pltpu.SemaphoreType.DMA((sections,)),
            pltpu.SemaphoreType.DMA((sections,)),
            pltpu.SemaphoreType.DMA((sections,)),
            pltpu.SemaphoreType.DMA((sections,)),
        ],
        compiler_params=pltpu.CompilerParams(collective_id=1, has_side_effects=True),
    )(index_volume, off_tile)


def plane_wave(angle, row_start, height, columns, total_rows, total_cols):
    across = angle - TILTS // 2
    along = jnp.mod(3 * angle, TILTS) - TILTS // 2
    row_index = row_start + lax.broadcasted_iota(jnp.int32, (height, columns), 0)
    col_index = lax.broadcasted_iota(jnp.int32, (height, columns), 1)
    period = total_cols * total_rows
    cycles_int = jnp.mod(across * col_index * total_rows + along * row_index * total_cols, period)
    phase_arg = 2.0 * math.pi / period * cycles_int.astype(jnp.float32)
    return jnp.concatenate([jnp.cos(phase_arg), jnp.sin(phase_arg)], axis=0)


def body(index_volume, angles, offsets, measured):
    sections = lax.axis_size("depth")
    rows = lax.axis_size("row")
    section_no = lax.axis_index("depth")
    height = index_volume.shape[1]
    columns = index_volume.shape[2]
    row_start = lax.axis_index("row") * height
    total_rows = height * rows
    angle_count = angles.shape[0]
    angle_no = section_no % angle_count
    volume, shift_tiles = gather_depth(index_volume, offsets, sections)
    shifts = shift_tiles[:, 0, 0].astype(jnp.int32)
    intensity = lax.dynamic_index_in_dim(measured, angle_no, 0, keepdims=False).astype(jnp.float32)
    angle = lax.dynamic_index_in_dim(angles, angle_no, 0, keepdims=False)
    incident = plane_wave(angle, row_start, height, columns, total_rows, columns)
    phases = PHASE_SCALE * volume.astype(jnp.float32)
    return run_chain(incident, jnp.cos(phases), jnp.sin(phases), intensity,
                     row_bands(shifts, height), column_bands(), rows)


def solution(mesh):
    in_specs = (P("depth", "row", None), P(), P("depth"), P(None, "row", None))
    out_specs = P("depth", "row", None)
    return jax.shard_map(body, mesh=mesh, in_specs=in_specs, out_specs=out_specs, check_vma=False)
```

```python
import functools
import math

import jax
import numpy as np
import jax.numpy as jnp
from jax import lax
from jax.experimental import pallas as pl
from jax.experimental.pallas import tpu as pltpu
from jax.sharding import PartitionSpec as P

TILTS = 16
HALF = 10
SHIFT = 4
HALFCOL = 64
LANE = 128

PHASE_SCALE = 0.5
CHIRP_ROW = 1.3
CHIRP_COL = 1.7
MESH = pl.DeviceIdType.MESH


def kernel_values(distance, radius, chirp_rate):
    inside = jnp.abs(distance) <= radius
    phase_arg = chirp_rate / radius * distance * distance
    weight = 1.0 / math.sqrt(2 * radius + 1)
    real_part = jnp.where(inside, jnp.cos(phase_arg) * weight, 0.0)
    imag_part = jnp.where(inside, jnp.sin(phase_arg) * weight, 0.0)
    return (real_part, imag_part)


def split_bf16(x):
    high = x.astype(jnp.bfloat16)
    low = (x - high.astype(jnp.float32)).astype(jnp.bfloat16)
    return high, low


def complex_block(real_part, imag_part):
    top = jnp.concatenate([real_part, -imag_part], axis=-1)
    bottom = jnp.concatenate([imag_part, real_part], axis=-1)
    return jnp.concatenate([top, bottom], axis=-2)


def row_bands(shifts, height):
    layers = shifts.shape[0]
    signs = jnp.concatenate([jnp.ones((layers,), jnp.int32), -jnp.ones((layers,), jnp.int32)])
    used = jnp.concatenate([shifts, shifts[::-1]]) * signs
    extent = (2 * layers, 3, height, height)
    part = lax.broadcasted_iota(jnp.int32, extent, 1)
    target = lax.broadcasted_iota(jnp.int32, extent, 2)
    source = lax.broadcasted_iota(jnp.int32, extent, 3) + (part - 1) * height
    distance = (source - target - used[:, None, None, None]).astype(jnp.float32)
    real_part, imag_part = kernel_values(distance, HALF, CHIRP_ROW)
    imag_part = imag_part * signs[:, None, None, None].astype(jnp.float32)
    return complex_block(real_part, imag_part)


def column_bands():
    part = np.arange(3)[:, None, None]
    source = np.arange(LANE)[None, :, None] + (part - 1) * LANE
    target = np.arange(LANE)[None, None, :]
    distance = (source - target).astype(np.float64)
    inside = np.abs(distance) <= HALFCOL
    phase_arg = CHIRP_COL / HALFCOL * distance * distance
    weight = 1.0 / math.sqrt(2 * HALFCOL + 1)
    real_part = np.where(inside, np.cos(phase_arg) * weight, 0.0)
    imag_part = np.where(inside, np.sin(phase_arg) * weight, 0.0)
    forward = np.concatenate([real_part, imag_part], axis=-1)
    adjoint = np.concatenate([real_part, -imag_part], axis=-1)
    return jnp.asarray(np.stack([forward, adjoint], axis=0).astype(np.float32))


def dot3(a, x):
    a_high, a_low = split_bf16(a)
    x_high, x_low = split_bf16(x)
    f32 = jnp.float32
    return (
        jnp.dot(a_high, x_high, preferred_element_type=f32)
        + jnp.dot(a_high, x_low, preferred_element_type=f32)
        + jnp.dot(a_low, x_high, preferred_element_type=f32)
    )


CHUNKS = 8


def chain_kernel(rows, u0_ref, cos_ref, sin_ref, inten_ref, rband_ref, cband_ref,
                 out_ref, terms_ref, partner_ref, field_ref, acc_ref, y_store, b_store, before, after,
                 bmh_ref, bml_ref, send_dn, send_up, recv_bf, recv_af, send_pair, recv_pair):
    me = lax.axis_index("row")
    section = lax.axis_index("depth")
    partner = section + 1 - 2 * (section % 2)
    layers, height, columns = cos_ref.shape
    blocks = columns // LANE
    width = columns // CHUNKS
    per_chunk = blocks // CHUNKS
    has_up = me > 0
    has_dn = me < rows - 1

    barrier = pltpu.get_barrier_semaphore()

    @pl.when(has_up)
    def _():
        pl.semaphore_signal(barrier, 1, device_id={"row": me - 1}, device_id_type=MESH)

    @pl.when(has_dn)
    def _():
        pl.semaphore_signal(barrier, 1, device_id={"row": me + 1}, device_id_type=MESH)

    pl.semaphore_signal(barrier, 1, device_id={"depth": partner}, device_id_type=MESH)
    peers = (me + rows - 1) // rows + (2 * rows - 2 - me) // rows
    pl.semaphore_wait(barrier, peers + 1)

    zero_block = jnp.zeros((2 * height, LANE), jnp.bfloat16)
    for ref in (bmh_ref, bml_ref):
        ref[0] = zero_block
        ref[blocks + 1] = zero_block

    def copies(k, c, store):
        cols = pl.ds(c * width, width)
        slot = k * CHUNKS + c
        down = pltpu.make_async_remote_copy(
            src_ref=store.at[:, cols], dst_ref=before.at[k, :, cols], send_sem=send_dn.at[slot],
            recv_sem=recv_bf.at[slot], device_id={"row": me + 1}, device_id_type=MESH)
        up = pltpu.make_async_remote_copy(
            src_ref=store.at[:, cols], dst_ref=after.at[k, :, cols], send_sem=send_up.at[slot],
            recv_sem=recv_af.at[slot], device_id={"row": me - 1}, device_id_type=MESH)
        return down, up

    def start(k, c, store):
        down, up = copies(k, c, store)

        @pl.when(has_dn)
        def _():
            down.start()

        @pl.when(has_up)
        def _():
            up.start()

    def finish(k, store):
        for c in range(CHUNKS):
            down, up = copies(k, c, store)

            @pl.when(has_dn)
            def _():
                down.wait_send()

            @pl.when(has_up)
            def _():
                up.wait_send()

    def halo(k, c, store):
        down, up = copies(k, c, store)
        cols = pl.ds(c * width, width)
        slot = k % 2

        @pl.when(has_up)
        def _():
            down.wait_recv()
            acc_ref[slot, :, cols] += dot3(rband_ref[k, 0], before[k, :, cols])

        @pl.when(has_dn)
        def _():
            up.wait_recv()
            acc_ref[slot, :, cols] += dot3(rband_ref[k, 2], after[k, :, cols])

        return acc_ref[slot, :, cols]

    def emit(k, c, store, value):
        cols = pl.ds(c * width, width)
        store[:, cols] = value
        acc_ref[k % 2, :, cols] = dot3(rband_ref[k, 1], store[:, cols])
        start(k, c, store)

    def write_blocks(c, x):
        high, low = split_bf16(x)
        for b in range(per_chunk):
            bmh_ref[c * per_chunk + b + 1] = high[:, b * LANE:(b + 1) * LANE]
            bml_ref[c * per_chunk + b + 1] = low[:, b * LANE:(b + 1) * LANE]

    def wave(k, store, store_next, finish_chunk, make_chunk):
        for c in range(CHUNKS):
            write_blocks(c, finish_chunk(c, halo(k, c, store)))
            if c >= 1:
                emit(k + 1, c - 1, store_next, make_chunk(c - 1))
        emit(k + 1, CHUNKS - 1, store_next, make_chunk(CHUNKS - 1))
        finish(k, store)

    def col_chunk(c, which):
        total = None
        f32 = jnp.float32
        first = c * per_chunk
        for t in range(3):
            xh = bmh_ref[first + t:first + t + per_chunk].reshape(per_chunk * 2 * height, LANE)
            xl = bml_ref[first + t:first + t + per_chunk].reshape(per_chunk * 2 * height, LANE)
            wh, wl = split_bf16(cband_ref[which, t])
            part = (jnp.dot(xh, wh, preferred_element_type=f32) + jnp.dot(xh, wl, preferred_element_type=f32)
                    + jnp.dot(xl, wh, preferred_element_type=f32))
            total = part if total is None else total + part
        total = total.reshape(per_chunk, 2 * height, 2 * LANE)
        real_part = total[:, :height, :LANE] - total[:, height:, LANE:]
        imag_part = total[:, :height, LANE:] + total[:, height:, :LANE]
        out = jnp.concatenate([real_part, imag_part], axis=1)
        return jnp.concatenate([out[b] for b in range(per_chunk)], axis=1)

    def rotated(s, c, u):
        cols = pl.ds(c * width, width)
        cs = cos_ref[s, :, cols]
        sn = sin_ref[s, :, cols]
        ur = u[:height]
        ui = u[height:]
        return jnp.concatenate([cs * ur - sn * ui, cs * ui + sn * ur], axis=0)

    def adjoint_chunk(s, c, a):
        cols = pl.ds(c * width, width)
        ar = a[:height]
        ai = a[height:]
        y = y_store[s, :, cols]
        terms_ref[s, :, cols] = PHASE_SCALE * (y[:height] * ai - y[height:] * ar)
        cs = cos_ref[s, :, cols]
        sn = sin_ref[s, :, cols]
        return jnp.concatenate([cs * ar + sn * ai, cs * ai - sn * ar], axis=0)

    for c in range(CHUNKS):
        emit(0, c, y_store.at[0], rotated(0, c, u0_ref[:, c * width:(c + 1) * width]))

    def forward(k, carry):
        wave(k, y_store.at[k], y_store.at[k + 1], lambda c, a: a,
             lambda c: rotated(k + 1, c, col_chunk(c, 0)))
        return carry

    lax.fori_loop(0, layers - 1, forward, 0)
    for c in range(CHUNKS):
        write_blocks(c, halo(layers - 1, c, y_store.at[layers - 1]))
    finish(layers - 1, y_store.at[layers - 1])
    for c in range(CHUNKS):
        field_ref[:, c * width:(c + 1) * width] = col_chunk(c, 0)
    u = field_ref[...]
    ur = u[:height]
    ui = u[height:]
    errors = ur * ur + ui * ui - inten_ref[...]
    field_ref[...] = jnp.concatenate([2.0 * errors * ur, 2.0 * errors * ui], axis=0)
    for c in range(CHUNKS):
        write_blocks(c, field_ref[:, c * width:(c + 1) * width])
    for c in range(CHUNKS):
        emit(layers, c, b_store.at[0], col_chunk(c, 1))

    def backward(j, carry):
        s = layers - 1 - j
        wave(layers + j, b_store.at[j], b_store.at[j + 1], lambda c, a: adjoint_chunk(s, c, a),
             lambda c: col_chunk(c, 1))
        return carry

    lax.fori_loop(0, layers - 1, backward, 0)
    last = 2 * layers - 1
    for c in range(CHUNKS):
        adjoint_chunk(0, c, halo(last, c, b_store.at[layers - 1]))
    finish(last, b_store.at[layers - 1])
    own = terms_ref[section]
    exchange = pltpu.make_async_remote_copy(
        src_ref=terms_ref.at[partner], dst_ref=partner_ref, send_sem=send_pair, recv_sem=recv_pair,
        device_id={"depth": partner}, device_id_type=MESH)
    exchange.start()
    exchange.wait_send()
    exchange.wait_recv()
    out_ref[0] = own + partner_ref[...]


def run_chain(u0, cosines, sines, intensity, row_band, col_band, rows):
    layers, height, columns = cosines.shape
    blocks = columns // LANE
    field = (2 * height, columns)
    return pl.pallas_call(
        functools.partial(chain_kernel, rows),
        out_shape=jax.ShapeDtypeStruct((1, height, columns), jnp.float32),
        in_specs=[pl.BlockSpec(memory_space=pltpu.VMEM)] * 6,
        out_specs=pl.BlockSpec(memory_space=pltpu.VMEM),
        scratch_shapes=[
            pltpu.VMEM((layers, height, columns), jnp.float32),
            pltpu.VMEM((height, columns), jnp.float32),
            pltpu.VMEM(field, jnp.float32),
            pltpu.VMEM((2,) + field, jnp.float32),
            pltpu.VMEM((layers,) + field, jnp.float32),
            pltpu.VMEM((layers,) + field, jnp.float32),
            pltpu.VMEM((2 * layers,) + field, jnp.float32),
            pltpu.VMEM((2 * layers,) + field, jnp.float32),
            pltpu.VMEM((blocks + 2, 2 * height, LANE), jnp.bfloat16),
            pltpu.VMEM((blocks + 2, 2 * height, LANE), jnp.bfloat16),
            pltpu.SemaphoreType.DMA((2 * layers * CHUNKS,)),
            pltpu.SemaphoreType.DMA((2 * layers * CHUNKS,)),
            pltpu.SemaphoreType.DMA((2 * layers * CHUNKS,)),
            pltpu.SemaphoreType.DMA((2 * layers * CHUNKS,)),
            pltpu.SemaphoreType.DMA,
            pltpu.SemaphoreType.DMA,
        ],
        compiler_params=pltpu.CompilerParams(
            collective_id=0, has_side_effects=True, vmem_limit_bytes=56 * 1024 * 1024),
    )(u0, cosines, sines, intensity, row_band, col_band)


def gather_kernel(sections, vol_ref, off_ref, vol_out, off_out, vol_slots, off_slots,
                  send_vol, send_off, recv_vol, recv_off):
    me = lax.axis_index("depth")
    barrier = pltpu.get_barrier_semaphore()
    for step in range(1, sections):
        peer = (me + step) % sections
        pl.semaphore_signal(barrier, 1, device_id={"depth": peer}, device_id_type=MESH)
    pl.semaphore_wait(barrier, sections - 1)

    def copies(step):
        peer = (me + step) % sections
        source = (me + sections - step) % sections
        out_vol = pltpu.make_async_remote_copy(
            src_ref=vol_ref.at[0], dst_ref=vol_slots.at[me], send_sem=send_vol.at[step],
            recv_sem=recv_vol.at[me], device_id={"depth": peer}, device_id_type=MESH)
        out_off = pltpu.make_async_remote_copy(
            src_ref=off_ref, dst_ref=off_slots.at[me], send_sem=send_off.at[step],
            recv_sem=recv_off.at[me], device_id={"depth": peer}, device_id_type=MESH)
        in_vol = pltpu.make_async_remote_copy(
            src_ref=vol_ref.at[0], dst_ref=vol_slots.at[source], send_sem=send_vol.at[step],
            recv_sem=recv_vol.at[source], device_id={"depth": peer}, device_id_type=MESH)
        in_off = pltpu.make_async_remote_copy(
            src_ref=off_ref, dst_ref=off_slots.at[source], send_sem=send_off.at[step],
            recv_sem=recv_off.at[source], device_id={"depth": peer}, device_id_type=MESH)
        return out_vol, out_off, in_vol, in_off

    for step in range(1, sections):
        out_vol, out_off, _, _ = copies(step)
        out_vol.start()
        out_off.start()
    vol_slots[me] = vol_ref[0]
    off_slots[me] = off_ref[...]
    for step in range(1, sections):
        out_vol, out_off, in_vol, in_off = copies(step)
        in_vol.wait_recv()
        in_off.wait_recv()
        out_vol.wait_send()
        out_off.wait_send()
    vol_out[...] = vol_slots[...]
    off_out[...] = off_slots[...]


def gather_depth(index_volume, offsets, sections):
    _, height, columns = index_volume.shape
    off_tile = jnp.broadcast_to(offsets.astype(jnp.float32)[:, None], (8, LANE))
    vol_shape = (sections, height, columns)
    off_shape = (sections, 8, LANE)
    return pl.pallas_call(
        functools.partial(gather_kernel, sections),
        out_shape=(jax.ShapeDtypeStruct(vol_shape, index_volume.dtype),
                   jax.ShapeDtypeStruct(off_shape, jnp.float32)),
        in_specs=[pl.BlockSpec(memory_space=pltpu.VMEM)] * 2,
        out_specs=(pl.BlockSpec(memory_space=pltpu.VMEM),) * 2,
        scratch_shapes=[
            pltpu.VMEM(vol_shape, index_volume.dtype),
            pltpu.VMEM(off_shape, jnp.float32),
            pltpu.SemaphoreType.DMA((sections,)),
            pltpu.SemaphoreType.DMA((sections,)),
            pltpu.SemaphoreType.DMA((sections,)),
            pltpu.SemaphoreType.DMA((sections,)),
        ],
        compiler_params=pltpu.CompilerParams(collective_id=1, has_side_effects=True),
    )(index_volume, off_tile)


def plane_wave(angle, row_start, height, columns, total_rows, total_cols):
    across = angle - TILTS // 2
    along = jnp.mod(3 * angle, TILTS) - TILTS // 2
    row_index = row_start + lax.broadcasted_iota(jnp.int32, (height, columns), 0)
    col_index = lax.broadcasted_iota(jnp.int32, (height, columns), 1)
    period = total_cols * total_rows
    cycles_int = jnp.mod(across * col_index * total_rows + along * row_index * total_cols, period)
    phase_arg = 2.0 * math.pi / period * cycles_int.astype(jnp.float32)
    return jnp.concatenate([jnp.cos(phase_arg), jnp.sin(phase_arg)], axis=0)


def body(index_volume, angles, offsets, measured):
    sections = lax.axis_size("depth")
    rows = lax.axis_size("row")
    section_no = lax.axis_index("depth")
    height = index_volume.shape[1]
    columns = index_volume.shape[2]
    row_start = lax.axis_index("row") * height
    total_rows = height * rows
    angle_count = angles.shape[0]
    angle_no = section_no % angle_count
    volume, shift_tiles = gather_depth(index_volume, offsets, sections)
    shifts = shift_tiles[:, 0, 0].astype(jnp.int32)
    intensity = lax.dynamic_index_in_dim(measured, angle_no, 0, keepdims=False).astype(jnp.float32)
    angle = lax.dynamic_index_in_dim(angles, angle_no, 0, keepdims=False)
    incident = plane_wave(angle, row_start, height, columns, total_rows, columns)
    phases = PHASE_SCALE * volume.astype(jnp.float32)
    return run_chain(incident, jnp.cos(phases), jnp.sin(phases), intensity,
                     row_bands(shifts, height), column_bands(), rows)


def solution(mesh):
    in_specs = (P("depth", "row", None), P(), P("depth"), P(None, "row", None))
    out_specs = P("depth", "row", None)
    return jax.shard_map(body, mesh=mesh, in_specs=in_specs, out_specs=out_specs, check_vma=False)
```

```python
import functools
import math

import jax
import numpy as np
import jax.numpy as jnp
from jax import lax
from jax.experimental import pallas as pl
from jax.experimental.pallas import tpu as pltpu
from jax.sharding import PartitionSpec as P

TILTS = 16
HALF = 10
SHIFT = 4
HALFCOL = 64
LANE = 128

PHASE_SCALE = 0.5
CHIRP_ROW = 1.3
CHIRP_COL = 1.7
MESH = pl.DeviceIdType.MESH


def kernel_values(distance, radius, chirp_rate):
    inside = jnp.abs(distance) <= radius
    phase_arg = chirp_rate / radius * distance * distance
    weight = 1.0 / math.sqrt(2 * radius + 1)
    real_part = jnp.where(inside, jnp.cos(phase_arg) * weight, 0.0)
    imag_part = jnp.where(inside, jnp.sin(phase_arg) * weight, 0.0)
    return (real_part, imag_part)


def split_bf16(x):
    high = x.astype(jnp.bfloat16)
    low = (x - high.astype(jnp.float32)).astype(jnp.bfloat16)
    return high, low


def complex_block(real_part, imag_part):
    top = jnp.concatenate([real_part, -imag_part], axis=-1)
    bottom = jnp.concatenate([imag_part, real_part], axis=-1)
    return jnp.concatenate([top, bottom], axis=-2)


def row_bands(shifts, height):
    layers = shifts.shape[0]
    signs = jnp.concatenate([jnp.ones((layers,), jnp.int32), -jnp.ones((layers,), jnp.int32)])
    used = jnp.concatenate([shifts, shifts[::-1]]) * signs
    extent = (2 * layers, 3, height, height)
    part = lax.broadcasted_iota(jnp.int32, extent, 1)
    target = lax.broadcasted_iota(jnp.int32, extent, 2)
    source = lax.broadcasted_iota(jnp.int32, extent, 3) + (part - 1) * height
    distance = (source - target - used[:, None, None, None]).astype(jnp.float32)
    real_part, imag_part = kernel_values(distance, HALF, CHIRP_ROW)
    imag_part = imag_part * signs[:, None, None, None].astype(jnp.float32)
    return complex_block(real_part, imag_part)


def column_bands():
    part = np.arange(3)[:, None, None]
    source = np.arange(LANE)[None, :, None] + (part - 1) * LANE
    target = np.arange(LANE)[None, None, :]
    distance = (source - target).astype(np.float64)
    inside = np.abs(distance) <= HALFCOL
    phase_arg = CHIRP_COL / HALFCOL * distance * distance
    weight = 1.0 / math.sqrt(2 * HALFCOL + 1)
    real_part = np.where(inside, np.cos(phase_arg) * weight, 0.0)
    imag_part = np.where(inside, np.sin(phase_arg) * weight, 0.0)
    forward = np.concatenate([real_part, imag_part], axis=-1)
    adjoint = np.concatenate([real_part, -imag_part], axis=-1)
    return jnp.asarray(np.stack([forward, adjoint], axis=0).astype(np.float32))


def dot3(a, x):
    a_high, a_low = split_bf16(a)
    x_high, x_low = split_bf16(x)
    f32 = jnp.float32
    return (
        jnp.dot(a_high, x_high, preferred_element_type=f32)
        + jnp.dot(a_high, x_low, preferred_element_type=f32)
        + jnp.dot(a_low, x_high, preferred_element_type=f32)
    )


CHUNKS = 4


def chain_kernel(rows, u0_ref, cos_ref, sin_ref, inten_ref, rband_ref, cband_ref,
                 out_ref, terms_ref, partner_ref, field_ref, acc_ref, y_store, b_store, before, after,
                 bmh_ref, bml_ref, send_dn, send_up, recv_bf, recv_af, send_pair, recv_pair):
    me = lax.axis_index("row")
    section = lax.axis_index("depth")
    partner = section + 1 - 2 * (section % 2)
    layers, height, columns = cos_ref.shape
    blocks = columns // LANE
    width = columns // CHUNKS
    per_chunk = blocks // CHUNKS
    has_up = me > 0
    has_dn = me < rows - 1

    barrier = pltpu.get_barrier_semaphore()

    @pl.when(has_up)
    def _():
        pl.semaphore_signal(barrier, 1, device_id={"row": me - 1}, device_id_type=MESH)

    @pl.when(has_dn)
    def _():
        pl.semaphore_signal(barrier, 1, device_id={"row": me + 1}, device_id_type=MESH)

    pl.semaphore_signal(barrier, 1, device_id={"depth": partner}, device_id_type=MESH)
    peers = (me + rows - 1) // rows + (2 * rows - 2 - me) // rows
    pl.semaphore_wait(barrier, peers + 1)

    zero_block = jnp.zeros((2 * height, LANE), jnp.bfloat16)
    for ref in (bmh_ref, bml_ref):
        ref[0] = zero_block
        ref[blocks + 1] = zero_block

    def copies(k, c, store):
        cols = pl.ds(c * width, width)
        slot = k * CHUNKS + c
        down = pltpu.make_async_remote_copy(
            src_ref=store.at[:, cols], dst_ref=before.at[k, :, cols], send_sem=send_dn.at[slot],
            recv_sem=recv_bf.at[slot], device_id={"row": me + 1}, device_id_type=MESH)
        up = pltpu.make_async_remote_copy(
            src_ref=store.at[:, cols], dst_ref=after.at[k, :, cols], send_sem=send_up.at[slot],
            recv_sem=recv_af.at[slot], device_id={"row": me - 1}, device_id_type=MESH)
        return down, up

    def start(k, c, store):
        down, up = copies(k, c, store)

        @pl.when(has_dn)
        def _():
            down.start()

        @pl.when(has_up)
        def _():
            up.start()

    def finish(k, store):
        for c in range(CHUNKS):
            down, up = copies(k, c, store)

            @pl.when(has_dn)
            def _():
                down.wait_send()

            @pl.when(has_up)
            def _():
                up.wait_send()

    def halo(k, c, store):
        down, up = copies(k, c, store)
        cols = pl.ds(c * width, width)
        slot = k % 2

        @pl.when(has_up)
        def _():
            down.wait_recv()
            acc_ref[slot, :, cols] += dot3(rband_ref[k, 0], before[k, :, cols])

        @pl.when(has_dn)
        def _():
            up.wait_recv()
            acc_ref[slot, :, cols] += dot3(rband_ref[k, 2], after[k, :, cols])

        return acc_ref[slot, :, cols]

    def emit(k, c, store, value):
        cols = pl.ds(c * width, width)
        store[:, cols] = value
        acc_ref[k % 2, :, cols] = dot3(rband_ref[k, 1], store[:, cols])
        start(k, c, store)

    def write_blocks(c, x):
        high, low = split_bf16(x)
        for b in range(per_chunk):
            bmh_ref[c * per_chunk + b + 1] = high[:, b * LANE:(b + 1) * LANE]
            bml_ref[c * per_chunk + b + 1] = low[:, b * LANE:(b + 1) * LANE]

    def wave(k, store, store_next, finish_chunk, make_chunk):
        for c in range(CHUNKS):
            write_blocks(c, finish_chunk(c, halo(k, c, store)))
            if c >= 1:
                emit(k + 1, c - 1, store_next, make_chunk(c - 1))
        emit(k + 1, CHUNKS - 1, store_next, make_chunk(CHUNKS - 1))
        finish(k, store)

    def col_chunk(c, which):
        total = None
        f32 = jnp.float32
        first = c * per_chunk
        for t in range(3):
            xh = bmh_ref[first + t:first + t + per_chunk].reshape(per_chunk * 2 * height, LANE)
            xl = bml_ref[first + t:first + t + per_chunk].reshape(per_chunk * 2 * height, LANE)
            wh, wl = split_bf16(cband_ref[which, t])
            part = (jnp.dot(xh, wh, preferred_element_type=f32) + jnp.dot(xh, wl, preferred_element_type=f32)
                    + jnp.dot(xl, wh, preferred_element_type=f32))
            total = part if total is None else total + part
        total = total.reshape(per_chunk, 2 * height, 2 * LANE)
        real_part = total[:, :height, :LANE] - total[:, height:, LANE:]
        imag_part = total[:, :height, LANE:] + total[:, height:, :LANE]
        out = jnp.concatenate([real_part, imag_part], axis=1)
        return jnp.concatenate([out[b] for b in range(per_chunk)], axis=1)

    def rotated(s, c, u):
        cols = pl.ds(c * width, width)
        cs = cos_ref[s, :, cols]
        sn = sin_ref[s, :, cols]
        ur = u[:height]
        ui = u[height:]
        return jnp.concatenate([cs * ur - sn * ui, cs * ui + sn * ur], axis=0)

    def adjoint_chunk(s, c, a):
        cols = pl.ds(c * width, width)
        ar = a[:height]
        ai = a[height:]
        y = y_store[s, :, cols]
        terms_ref[s, :, cols] = PHASE_SCALE * (y[:height] * ai - y[height:] * ar)
        cs = cos_ref[s, :, cols]
        sn = sin_ref[s, :, cols]
        return jnp.concatenate([cs * ar + sn * ai, cs * ai - sn * ar], axis=0)

    for c in range(CHUNKS):
        emit(0, c, y_store.at[0], rotated(0, c, u0_ref[:, c * width:(c + 1) * width]))

    def forward(k, carry):
        wave(k, y_store.at[k], y_store.at[k + 1], lambda c, a: a,
             lambda c: rotated(k + 1, c, col_chunk(c, 0)))
        return carry

    lax.fori_loop(0, layers - 1, forward, 0)
    for c in range(CHUNKS):
        write_blocks(c, halo(layers - 1, c, y_store.at[layers - 1]))
    finish(layers - 1, y_store.at[layers - 1])
    for c in range(CHUNKS):
        field_ref[:, c * width:(c + 1) * width] = col_chunk(c, 0)
    u = field_ref[...]
    ur = u[:height]
    ui = u[height:]
    errors = ur * ur + ui * ui - inten_ref[...]
    field_ref[...] = jnp.concatenate([2.0 * errors * ur, 2.0 * errors * ui], axis=0)
    for c in range(CHUNKS):
        write_blocks(c, field_ref[:, c * width:(c + 1) * width])
    for c in range(CHUNKS):
        emit(layers, c, b_store.at[0], col_chunk(c, 1))

    def backward(j, carry):
        s = layers - 1 - j
        wave(layers + j, b_store.at[j], b_store.at[j + 1], lambda c, a: adjoint_chunk(s, c, a),
             lambda c: col_chunk(c, 1))
        return carry

    lax.fori_loop(0, layers - 1, backward, 0)
    last = 2 * layers - 1
    for c in range(CHUNKS):
        adjoint_chunk(0, c, halo(last, c, b_store.at[layers - 1]))
    finish(last, b_store.at[layers - 1])
    own = terms_ref[section]
    exchange = pltpu.make_async_remote_copy(
        src_ref=terms_ref.at[partner], dst_ref=partner_ref, send_sem=send_pair, recv_sem=recv_pair,
        device_id={"depth": partner}, device_id_type=MESH)
    exchange.start()
    exchange.wait_send()
    exchange.wait_recv()
    out_ref[0] = own + partner_ref[...]


def run_chain(u0, cosines, sines, intensity, row_band, col_band, rows):
    layers, height, columns = cosines.shape
    blocks = columns // LANE
    field = (2 * height, columns)
    return pl.pallas_call(
        functools.partial(chain_kernel, rows),
        out_shape=jax.ShapeDtypeStruct((1, height, columns), jnp.float32),
        in_specs=[pl.BlockSpec(memory_space=pltpu.VMEM)] * 6,
        out_specs=pl.BlockSpec(memory_space=pltpu.VMEM),
        scratch_shapes=[
            pltpu.VMEM((layers, height, columns), jnp.float32),
            pltpu.VMEM((height, columns), jnp.float32),
            pltpu.VMEM(field, jnp.float32),
            pltpu.VMEM((2,) + field, jnp.float32),
            pltpu.VMEM((layers,) + field, jnp.float32),
            pltpu.VMEM((layers,) + field, jnp.float32),
            pltpu.VMEM((2 * layers,) + field, jnp.float32),
            pltpu.VMEM((2 * layers,) + field, jnp.float32),
            pltpu.VMEM((blocks + 2, 2 * height, LANE), jnp.bfloat16),
            pltpu.VMEM((blocks + 2, 2 * height, LANE), jnp.bfloat16),
            pltpu.SemaphoreType.DMA((2 * layers * CHUNKS,)),
            pltpu.SemaphoreType.DMA((2 * layers * CHUNKS,)),
            pltpu.SemaphoreType.DMA((2 * layers * CHUNKS,)),
            pltpu.SemaphoreType.DMA((2 * layers * CHUNKS,)),
            pltpu.SemaphoreType.DMA,
            pltpu.SemaphoreType.DMA,
        ],
        compiler_params=pltpu.CompilerParams(
            collective_id=0, has_side_effects=True, vmem_limit_bytes=56 * 1024 * 1024),
    )(u0, cosines, sines, intensity, row_band, col_band)


def gather_kernel(sections, vol_ref, off_ref, vol_out, off_out, vol_slots, off_slots,
                  send_vol, send_off, recv_vol, recv_off):
    me = lax.axis_index("depth")
    barrier = pltpu.get_barrier_semaphore()
    for step in range(1, sections):
        peer = (me + step) % sections
        pl.semaphore_signal(barrier, 1, device_id={"depth": peer}, device_id_type=MESH)
    pl.semaphore_wait(barrier, sections - 1)

    def copies(step):
        peer = (me + step) % sections
        source = (me + sections - step) % sections
        out_vol = pltpu.make_async_remote_copy(
            src_ref=vol_ref.at[0], dst_ref=vol_slots.at[me], send_sem=send_vol.at[step],
            recv_sem=recv_vol.at[me], device_id={"depth": peer}, device_id_type=MESH)
        out_off = pltpu.make_async_remote_copy(
            src_ref=off_ref, dst_ref=off_slots.at[me], send_sem=send_off.at[step],
            recv_sem=recv_off.at[me], device_id={"depth": peer}, device_id_type=MESH)
        in_vol = pltpu.make_async_remote_copy(
            src_ref=vol_ref.at[0], dst_ref=vol_slots.at[source], send_sem=send_vol.at[step],
            recv_sem=recv_vol.at[source], device_id={"depth": peer}, device_id_type=MESH)
        in_off = pltpu.make_async_remote_copy(
            src_ref=off_ref, dst_ref=off_slots.at[source], send_sem=send_off.at[step],
            recv_sem=recv_off.at[source], device_id={"depth": peer}, device_id_type=MESH)
        return out_vol, out_off, in_vol, in_off

    for step in range(1, sections):
        out_vol, out_off, _, _ = copies(step)
        out_vol.start()
        out_off.start()
    vol_slots[me] = vol_ref[0]
    off_slots[me] = off_ref[...]
    for step in range(1, sections):
        out_vol, out_off, in_vol, in_off = copies(step)
        in_vol.wait_recv()
        in_off.wait_recv()
        out_vol.wait_send()
        out_off.wait_send()
    vol_out[...] = vol_slots[...]
    off_out[...] = off_slots[...]


def gather_depth(index_volume, offsets, sections):
    _, height, columns = index_volume.shape
    off_tile = jnp.broadcast_to(offsets.astype(jnp.float32)[:, None], (8, LANE))
    vol_shape = (sections, height, columns)
    off_shape = (sections, 8, LANE)
    return pl.pallas_call(
        functools.partial(gather_kernel, sections),
        out_shape=(jax.ShapeDtypeStruct(vol_shape, index_volume.dtype),
                   jax.ShapeDtypeStruct(off_shape, jnp.float32)),
        in_specs=[pl.BlockSpec(memory_space=pltpu.VMEM)] * 2,
        out_specs=(pl.BlockSpec(memory_space=pltpu.VMEM),) * 2,
        scratch_shapes=[
            pltpu.VMEM(vol_shape, index_volume.dtype),
            pltpu.VMEM(off_shape, jnp.float32),
            pltpu.SemaphoreType.DMA((sections,)),
            pltpu.SemaphoreType.DMA((sections,)),
            pltpu.SemaphoreType.DMA((sections,)),
            pltpu.SemaphoreType.DMA((sections,)),
        ],
        compiler_params=pltpu.CompilerParams(collective_id=1, has_side_effects=True),
    )(index_volume, off_tile)


def plane_wave(angle, row_start, height, columns, total_rows, total_cols):
    across = angle - TILTS // 2
    along = jnp.mod(3 * angle, TILTS) - TILTS // 2
    row_index = row_start + lax.broadcasted_iota(jnp.int32, (height, columns), 0)
    col_index = lax.broadcasted_iota(jnp.int32, (height, columns), 1)
    period = total_cols * total_rows
    cycles_int = jnp.mod(across * col_index * total_rows + along * row_index * total_cols, period)
    phase_arg = 2.0 * math.pi / period * cycles_int.astype(jnp.float32)
    return jnp.concatenate([jnp.cos(phase_arg), jnp.sin(phase_arg)], axis=0)


def body(index_volume, angles, offsets, measured):
    sections = lax.axis_size("depth")
    rows = lax.axis_size("row")
    section_no = lax.axis_index("depth")
    height = index_volume.shape[1]
    columns = index_volume.shape[2]
    row_start = lax.axis_index("row") * height
    total_rows = height * rows
    angle_count = angles.shape[0]
    angle_no = section_no % angle_count
    volume, shift_tiles = gather_depth(index_volume, offsets, sections)
    shifts = shift_tiles[:, 0, 0].astype(jnp.int32)
    intensity = lax.dynamic_index_in_dim(measured, angle_no, 0, keepdims=False).astype(jnp.float32)
    angle = lax.dynamic_index_in_dim(angles, angle_no, 0, keepdims=False)
    incident = plane_wave(angle, row_start, height, columns, total_rows, columns)
    phases = PHASE_SCALE * volume.astype(jnp.float32)
    return run_chain(incident, jnp.cos(phases), jnp.sin(phases), intensity,
                     row_bands(shifts, height), column_bands(), rows)


def solution(mesh):
    in_specs = (P("depth", "row", None), P(), P("depth"), P(None, "row", None))
    out_specs = P("depth", "row", None)
    return jax.shard_map(body, mesh=mesh, in_specs=in_specs, out_specs=out_specs, check_vma=False)
```

```python
import functools
import math

import jax
import numpy as np
import jax.numpy as jnp
from jax import lax
from jax.experimental import pallas as pl
from jax.experimental.pallas import tpu as pltpu
from jax.sharding import PartitionSpec as P

TILTS = 16
HALF = 10
SHIFT = 4
HALFCOL = 64
LANE = 128

PHASE_SCALE = 0.5
CHIRP_ROW = 1.3
CHIRP_COL = 1.7
MESH = pl.DeviceIdType.MESH


def kernel_values(distance, radius, chirp_rate):
    inside = jnp.abs(distance) <= radius
    phase_arg = chirp_rate / radius * distance * distance
    weight = 1.0 / math.sqrt(2 * radius + 1)
    real_part = jnp.where(inside, jnp.cos(phase_arg) * weight, 0.0)
    imag_part = jnp.where(inside, jnp.sin(phase_arg) * weight, 0.0)
    return (real_part, imag_part)


def split_bf16(x):
    high = x.astype(jnp.bfloat16)
    low = (x - high.astype(jnp.float32)).astype(jnp.bfloat16)
    return high, low


def complex_block(real_part, imag_part):
    top = jnp.concatenate([real_part, -imag_part], axis=-1)
    bottom = jnp.concatenate([imag_part, real_part], axis=-1)
    return jnp.concatenate([top, bottom], axis=-2)


def band_table(height):
    offsets = np.arange(-SHIFT, SHIFT + 1)[:, None, None, None]
    part = np.arange(3)[None, :, None, None]
    target = np.arange(height)[None, None, :, None]
    source = np.arange(height)[None, None, None, :] + (part - 1) * height
    tables = []
    for sign in (1, -1):
        distance = (source - target - sign * offsets).astype(np.float64)
        inside = np.abs(distance) <= HALF
        phase_arg = CHIRP_ROW / HALF * distance * distance
        weight = 1.0 / math.sqrt(2 * HALF + 1)
        real_part = np.where(inside, np.cos(phase_arg) * weight, 0.0)
        imag_part = np.where(inside, np.sin(phase_arg) * weight, 0.0) * sign
        top = np.concatenate([real_part, -imag_part], axis=-1)
        bottom = np.concatenate([imag_part, real_part], axis=-1)
        block = np.concatenate([top, bottom], axis=-2)
        tables.append(block.reshape(2 * SHIFT + 1, 3 * 2 * height, 2 * height))
    return jnp.asarray(np.stack(tables, axis=0).astype(np.float32))


def column_bands():
    part = np.arange(3)[:, None, None]
    source = np.arange(LANE)[None, :, None] + (part - 1) * LANE
    target = np.arange(LANE)[None, None, :]
    distance = (source - target).astype(np.float64)
    inside = np.abs(distance) <= HALFCOL
    phase_arg = CHIRP_COL / HALFCOL * distance * distance
    weight = 1.0 / math.sqrt(2 * HALFCOL + 1)
    real_part = np.where(inside, np.cos(phase_arg) * weight, 0.0)
    imag_part = np.where(inside, np.sin(phase_arg) * weight, 0.0)
    forward = np.concatenate([real_part, imag_part], axis=-1)
    adjoint = np.concatenate([real_part, -imag_part], axis=-1)
    return jnp.asarray(np.stack([forward, adjoint], axis=0).astype(np.float32))


def dot3(a, x):
    a_high, a_low = split_bf16(a)
    x_high, x_low = split_bf16(x)
    f32 = jnp.float32
    return (
        jnp.dot(a_high, x_high, preferred_element_type=f32)
        + jnp.dot(a_high, x_low, preferred_element_type=f32)
        + jnp.dot(a_low, x_high, preferred_element_type=f32)
    )


CHUNKS = 4


def chain_kernel(rows, sections, u0_ref, vol_ref, off_ref, inten_ref, table_ref, cband_ref,
                 out_ref, terms_ref, partner_ref, field_ref, acc_ref, y_store, b_store, before, after,
                 bmh_ref, bml_ref, cos_ref, sin_ref, rband_ref, vol_slots, off_slots,
                 send_dn, send_up, recv_bf, recv_af, send_pair, recv_pair,
                 send_vol, send_off, recv_vol, recv_off):
    me = lax.axis_index("row")
    section = lax.axis_index("depth")
    partner = section + 1 - 2 * (section % 2)
    layers, height, columns = cos_ref.shape
    blocks = columns // LANE
    width = columns // CHUNKS
    per_chunk = blocks // CHUNKS
    has_up = me > 0
    has_dn = me < rows - 1

    barrier = pltpu.get_barrier_semaphore()

    @pl.when(has_up)
    def _():
        pl.semaphore_signal(barrier, 1, device_id={"row": me - 1}, device_id_type=MESH)

    @pl.when(has_dn)
    def _():
        pl.semaphore_signal(barrier, 1, device_id={"row": me + 1}, device_id_type=MESH)

    for step in range(1, sections):
        peer = (section + step) % sections
        pl.semaphore_signal(barrier, 1, device_id={"depth": peer}, device_id_type=MESH)
    peers = (me + rows - 1) // rows + (2 * rows - 2 - me) // rows
    pl.semaphore_wait(barrier, peers + sections - 1)

    def gathers(step, slot):
        peer = (section + step) % sections
        vol_copy = pltpu.make_async_remote_copy(
            src_ref=vol_ref.at[0], dst_ref=vol_slots.at[slot], send_sem=send_vol.at[step],
            recv_sem=recv_vol.at[slot], device_id={"depth": peer}, device_id_type=MESH)
        off_copy = pltpu.make_async_remote_copy(
            src_ref=off_ref, dst_ref=off_slots.at[slot], send_sem=send_off.at[step],
            recv_sem=recv_off.at[slot], device_id={"depth": peer}, device_id_type=MESH)
        return vol_copy, off_copy

    for step in range(1, sections):
        for one in gathers(step, section):
            one.start()
    vol_slots[section] = vol_ref[0]
    off_slots[section] = off_ref[...]
    part_rows = 2 * height

    def prepare(s):
        @pl.when(s != section)
        def _():
            for one in gathers(1, s):
                one.wait_recv()

        phase = PHASE_SCALE * vol_slots[s].astype(jnp.float32)
        cos_ref[s] = jnp.cos(phase)
        sin_ref[s] = jnp.sin(phase)
        shift = off_slots[s][0:1, 0:part_rows]
        forward_band = None
        adjoint_band = None
        for i in range(2 * SHIFT + 1):
            pick = jnp.where(shift == float(i - SHIFT), 1.0, 0.0)
            f_term = pick * table_ref[0, i]
            a_term = pick * table_ref[1, i]
            forward_band = f_term if forward_band is None else forward_band + f_term
            adjoint_band = a_term if adjoint_band is None else adjoint_band + a_term
        rband_ref[s] = forward_band
        rband_ref[2 * layers - 1 - s] = adjoint_band

    zero_block = jnp.zeros((2 * height, LANE), jnp.bfloat16)
    for ref in (bmh_ref, bml_ref):
        ref[0] = zero_block
        ref[blocks + 1] = zero_block

    def copies(k, c, store):
        cols = pl.ds(c * width, width)
        slot = k * CHUNKS + c
        down = pltpu.make_async_remote_copy(
            src_ref=store.at[:, cols], dst_ref=before.at[k, :, cols], send_sem=send_dn.at[slot],
            recv_sem=recv_bf.at[slot], device_id={"row": me + 1}, device_id_type=MESH)
        up = pltpu.make_async_remote_copy(
            src_ref=store.at[:, cols], dst_ref=after.at[k, :, cols], send_sem=send_up.at[slot],
            recv_sem=recv_af.at[slot], device_id={"row": me - 1}, device_id_type=MESH)
        return down, up

    def start(k, c, store):
        down, up = copies(k, c, store)

        @pl.when(has_dn)
        def _():
            down.start()

        @pl.when(has_up)
        def _():
            up.start()

    def finish(k, store):
        for c in range(CHUNKS):
            down, up = copies(k, c, store)

            @pl.when(has_dn)
            def _():
                down.wait_send()

            @pl.when(has_up)
            def _():
                up.wait_send()

    def halo(k, c, store):
        down, up = copies(k, c, store)
        cols = pl.ds(c * width, width)
        slot = k % 2

        @pl.when(has_up)
        def _():
            down.wait_recv()
            acc_ref[slot, :, cols] += dot3(rband_ref[k, 0:part_rows], before[k, :, cols])

        @pl.when(has_dn)
        def _():
            up.wait_recv()
            acc_ref[slot, :, cols] += dot3(rband_ref[k, 2 * part_rows:3 * part_rows], after[k, :, cols])

        return acc_ref[slot, :, cols]

    def emit(k, c, store, value):
        cols = pl.ds(c * width, width)
        store[:, cols] = value
        acc_ref[k % 2, :, cols] = dot3(rband_ref[k, part_rows:2 * part_rows], store[:, cols])
        start(k, c, store)

    def write_blocks(c, x):
        high, low = split_bf16(x)
        for b in range(per_chunk):
            bmh_ref[c * per_chunk + b + 1] = high[:, b * LANE:(b + 1) * LANE]
            bml_ref[c * per_chunk + b + 1] = low[:, b * LANE:(b + 1) * LANE]

    def wave(k, store, store_next, finish_chunk, make_chunk):
        for c in range(CHUNKS):
            write_blocks(c, finish_chunk(c, halo(k, c, store)))
            if c >= 1:
                emit(k + 1, c - 1, store_next, make_chunk(c - 1))
        emit(k + 1, CHUNKS - 1, store_next, make_chunk(CHUNKS - 1))
        finish(k, store)

    def col_chunk(c, which):
        total = None
        f32 = jnp.float32
        first = c * per_chunk
        for t in range(3):
            xh = bmh_ref[first + t:first + t + per_chunk].reshape(per_chunk * 2 * height, LANE)
            xl = bml_ref[first + t:first + t + per_chunk].reshape(per_chunk * 2 * height, LANE)
            wh, wl = split_bf16(cband_ref[which, t])
            part = (jnp.dot(xh, wh, preferred_element_type=f32) + jnp.dot(xh, wl, preferred_element_type=f32)
                    + jnp.dot(xl, wh, preferred_element_type=f32))
            total = part if total is None else total + part
        total = total.reshape(per_chunk, 2 * height, 2 * LANE)
        real_part = total[:, :height, :LANE] - total[:, height:, LANE:]
        imag_part = total[:, :height, LANE:] + total[:, height:, :LANE]
        out = jnp.concatenate([real_part, imag_part], axis=1)
        return jnp.concatenate([out[b] for b in range(per_chunk)], axis=1)

    def rotated(s, c, u):
        cols = pl.ds(c * width, width)
        cs = cos_ref[s, :, cols]
        sn = sin_ref[s, :, cols]
        ur = u[:height]
        ui = u[height:]
        return jnp.concatenate([cs * ur - sn * ui, cs * ui + sn * ur], axis=0)

    def adjoint_chunk(s, c, a):
        cols = pl.ds(c * width, width)
        ar = a[:height]
        ai = a[height:]
        y = y_store[s, :, cols]
        terms_ref[s, :, cols] = PHASE_SCALE * (y[:height] * ai - y[height:] * ar)
        cs = cos_ref[s, :, cols]
        sn = sin_ref[s, :, cols]
        return jnp.concatenate([cs * ar + sn * ai, cs * ai - sn * ar], axis=0)

    prepare(0)
    for c in range(CHUNKS):
        emit(0, c, y_store.at[0], rotated(0, c, u0_ref[:, c * width:(c + 1) * width]))

    def forward(k, carry):
        prepare(k + 1)
        wave(k, y_store.at[k], y_store.at[k + 1], lambda c, a: a,
             lambda c: rotated(k + 1, c, col_chunk(c, 0)))
        return carry

    lax.fori_loop(0, layers - 1, forward, 0)
    for c in range(CHUNKS):
        write_blocks(c, halo(layers - 1, c, y_store.at[layers - 1]))
    finish(layers - 1, y_store.at[layers - 1])
    for c in range(CHUNKS):
        field_ref[:, c * width:(c + 1) * width] = col_chunk(c, 0)
    u = field_ref[...]
    ur = u[:height]
    ui = u[height:]
    errors = ur * ur + ui * ui - inten_ref[...]
    field_ref[...] = jnp.concatenate([2.0 * errors * ur, 2.0 * errors * ui], axis=0)
    for c in range(CHUNKS):
        write_blocks(c, field_ref[:, c * width:(c + 1) * width])
    for c in range(CHUNKS):
        emit(layers, c, b_store.at[0], col_chunk(c, 1))

    def backward(j, carry):
        s = layers - 1 - j
        wave(layers + j, b_store.at[j], b_store.at[j + 1], lambda c, a: adjoint_chunk(s, c, a),
             lambda c: col_chunk(c, 1))
        return carry

    lax.fori_loop(0, layers - 1, backward, 0)
    last = 2 * layers - 1
    for c in range(CHUNKS):
        adjoint_chunk(0, c, halo(last, c, b_store.at[layers - 1]))
    finish(last, b_store.at[layers - 1])
    own = terms_ref[section]
    exchange = pltpu.make_async_remote_copy(
        src_ref=terms_ref.at[partner], dst_ref=partner_ref, send_sem=send_pair, recv_sem=recv_pair,
        device_id={"depth": partner}, device_id_type=MESH)
    exchange.start()
    exchange.wait_send()
    exchange.wait_recv()
    out_ref[0] = own + partner_ref[...]
    for step in range(1, sections):
        for one in gathers(step, section):
            one.wait_send()


def run_chain(u0, index_volume, offsets, intensity, rows, sections):
    _, height, columns = index_volume.shape
    layers = sections
    blocks = columns // LANE
    field = (2 * height, columns)
    off_tile = jnp.broadcast_to(offsets.astype(jnp.float32)[:, None], (8, LANE))
    plane = (layers, height, columns)
    return pl.pallas_call(
        functools.partial(chain_kernel, rows, sections),
        out_shape=jax.ShapeDtypeStruct((1, height, columns), jnp.float32),
        in_specs=[pl.BlockSpec(memory_space=pltpu.VMEM)] * 6,
        out_specs=pl.BlockSpec(memory_space=pltpu.VMEM),
        scratch_shapes=[
            pltpu.VMEM(plane, jnp.float32),
            pltpu.VMEM((height, columns), jnp.float32),
            pltpu.VMEM(field, jnp.float32),
            pltpu.VMEM((2,) + field, jnp.float32),
            pltpu.VMEM((layers,) + field, jnp.float32),
            pltpu.VMEM((layers,) + field, jnp.float32),
            pltpu.VMEM((2 * layers,) + field, jnp.float32),
            pltpu.VMEM((2 * layers,) + field, jnp.float32),
            pltpu.VMEM((blocks + 2, 2 * height, LANE), jnp.bfloat16),
            pltpu.VMEM((blocks + 2, 2 * height, LANE), jnp.bfloat16),
            pltpu.VMEM(plane, jnp.float32),
            pltpu.VMEM(plane, jnp.float32),
            pltpu.VMEM((2 * layers, 3 * 2 * height, 2 * height), jnp.float32),
            pltpu.VMEM(plane, index_volume.dtype),
            pltpu.VMEM((sections, 8, LANE), jnp.float32),
            pltpu.SemaphoreType.DMA((2 * layers * CHUNKS,)),
            pltpu.SemaphoreType.DMA((2 * layers * CHUNKS,)),
            pltpu.SemaphoreType.DMA((2 * layers * CHUNKS,)),
            pltpu.SemaphoreType.DMA((2 * layers * CHUNKS,)),
            pltpu.SemaphoreType.DMA,
            pltpu.SemaphoreType.DMA,
            pltpu.SemaphoreType.DMA((sections,)),
            pltpu.SemaphoreType.DMA((sections,)),
            pltpu.SemaphoreType.DMA((sections,)),
            pltpu.SemaphoreType.DMA((sections,)),
        ],
        compiler_params=pltpu.CompilerParams(
            collective_id=0, has_side_effects=True, vmem_limit_bytes=56 * 1024 * 1024),
    )(u0, index_volume, off_tile, intensity, band_table(height), column_bands())


def gather_kernel(sections, vol_ref, off_ref, vol_out, off_out, vol_slots, off_slots,
                  send_vol, send_off, recv_vol, recv_off):
    me = lax.axis_index("depth")
    barrier = pltpu.get_barrier_semaphore()
    for step in range(1, sections):
        peer = (me + step) % sections
        pl.semaphore_signal(barrier, 1, device_id={"depth": peer}, device_id_type=MESH)
    pl.semaphore_wait(barrier, sections - 1)

    def copies(step):
        peer = (me + step) % sections
        source = (me + sections - step) % sections
        out_vol = pltpu.make_async_remote_copy(
            src_ref=vol_ref.at[0], dst_ref=vol_slots.at[me], send_sem=send_vol.at[step],
            recv_sem=recv_vol.at[me], device_id={"depth": peer}, device_id_type=MESH)
        out_off = pltpu.make_async_remote_copy(
            src_ref=off_ref, dst_ref=off_slots.at[me], send_sem=send_off.at[step],
            recv_sem=recv_off.at[me], device_id={"depth": peer}, device_id_type=MESH)
        in_vol = pltpu.make_async_remote_copy(
            src_ref=vol_ref.at[0], dst_ref=vol_slots.at[source], send_sem=send_vol.at[step],
            recv_sem=recv_vol.at[source], device_id={"depth": peer}, device_id_type=MESH)
        in_off = pltpu.make_async_remote_copy(
            src_ref=off_ref, dst_ref=off_slots.at[source], send_sem=send_off.at[step],
            recv_sem=recv_off.at[source], device_id={"depth": peer}, device_id_type=MESH)
        return out_vol, out_off, in_vol, in_off

    for step in range(1, sections):
        out_vol, out_off, _, _ = copies(step)
        out_vol.start()
        out_off.start()
    vol_slots[me] = vol_ref[0]
    off_slots[me] = off_ref[...]
    for step in range(1, sections):
        out_vol, out_off, in_vol, in_off = copies(step)
        in_vol.wait_recv()
        in_off.wait_recv()
        out_vol.wait_send()
        out_off.wait_send()
    vol_out[...] = vol_slots[...]
    off_out[...] = off_slots[...]


def gather_depth(index_volume, offsets, sections):
    _, height, columns = index_volume.shape
    off_tile = jnp.broadcast_to(offsets.astype(jnp.float32)[:, None], (8, LANE))
    vol_shape = (sections, height, columns)
    off_shape = (sections, 8, LANE)
    return pl.pallas_call(
        functools.partial(gather_kernel, sections),
        out_shape=(jax.ShapeDtypeStruct(vol_shape, index_volume.dtype),
                   jax.ShapeDtypeStruct(off_shape, jnp.float32)),
        in_specs=[pl.BlockSpec(memory_space=pltpu.VMEM)] * 2,
        out_specs=(pl.BlockSpec(memory_space=pltpu.VMEM),) * 2,
        scratch_shapes=[
            pltpu.VMEM(vol_shape, index_volume.dtype),
            pltpu.VMEM(off_shape, jnp.float32),
            pltpu.SemaphoreType.DMA((sections,)),
            pltpu.SemaphoreType.DMA((sections,)),
            pltpu.SemaphoreType.DMA((sections,)),
            pltpu.SemaphoreType.DMA((sections,)),
        ],
        compiler_params=pltpu.CompilerParams(collective_id=1, has_side_effects=True),
    )(index_volume, off_tile)


def plane_wave(angle, row_start, height, columns, total_rows, total_cols):
    across = angle - TILTS // 2
    along = jnp.mod(3 * angle, TILTS) - TILTS // 2
    row_index = row_start + lax.broadcasted_iota(jnp.int32, (height, columns), 0)
    col_index = lax.broadcasted_iota(jnp.int32, (height, columns), 1)
    period = total_cols * total_rows
    cycles_int = jnp.mod(across * col_index * total_rows + along * row_index * total_cols, period)
    phase_arg = 2.0 * math.pi / period * cycles_int.astype(jnp.float32)
    return jnp.concatenate([jnp.cos(phase_arg), jnp.sin(phase_arg)], axis=0)


def body(index_volume, angles, offsets, measured):
    sections = lax.axis_size("depth")
    rows = lax.axis_size("row")
    section_no = lax.axis_index("depth")
    height = index_volume.shape[1]
    columns = index_volume.shape[2]
    row_start = lax.axis_index("row") * height
    total_rows = height * rows
    angle_count = angles.shape[0]
    angle_no = section_no % angle_count
    intensity = lax.dynamic_index_in_dim(measured, angle_no, 0, keepdims=False).astype(jnp.float32)
    angle = lax.dynamic_index_in_dim(angles, angle_no, 0, keepdims=False)
    incident = plane_wave(angle, row_start, height, columns, total_rows, columns)
    return run_chain(incident, index_volume, offsets, intensity, rows, sections)


def solution(mesh):
    in_specs = (P("depth", "row", None), P(), P("depth"), P(None, "row", None))
    out_specs = P("depth", "row", None)
    return jax.shard_map(body, mesh=mesh, in_specs=in_specs, out_specs=out_specs, check_vma=False)
```

```python
import functools
import math

import jax
import numpy as np
import jax.numpy as jnp
from jax import lax
from jax.experimental import pallas as pl
from jax.experimental.pallas import tpu as pltpu
from jax.sharding import PartitionSpec as P

TILTS = 16
HALF = 10
SHIFT = 4
HALFCOL = 64
LANE = 128

PHASE_SCALE = 0.5
CHIRP_ROW = 1.3
CHIRP_COL = 1.7
MESH = pl.DeviceIdType.MESH


def kernel_values(distance, radius, chirp_rate):
    inside = jnp.abs(distance) <= radius
    phase_arg = chirp_rate / radius * distance * distance
    weight = 1.0 / math.sqrt(2 * radius + 1)
    real_part = jnp.where(inside, jnp.cos(phase_arg) * weight, 0.0)
    imag_part = jnp.where(inside, jnp.sin(phase_arg) * weight, 0.0)
    return (real_part, imag_part)


def split_bf16(x):
    high = x.astype(jnp.bfloat16)
    low = (x - high.astype(jnp.float32)).astype(jnp.bfloat16)
    return high, low


def complex_block(real_part, imag_part):
    top = jnp.concatenate([real_part, -imag_part], axis=-1)
    bottom = jnp.concatenate([imag_part, real_part], axis=-1)
    return jnp.concatenate([top, bottom], axis=-2)


def band_table(height):
    offsets = np.arange(-SHIFT, SHIFT + 1)[:, None, None, None]
    part = np.arange(3)[None, :, None, None]
    target = np.arange(height)[None, None, :, None]
    source = np.arange(height)[None, None, None, :] + (part - 1) * height
    tables = []
    for sign in (1, -1):
        distance = (source - target - sign * offsets).astype(np.float64)
        inside = np.abs(distance) <= HALF
        phase_arg = CHIRP_ROW / HALF * distance * distance
        weight = 1.0 / math.sqrt(2 * HALF + 1)
        real_part = np.where(inside, np.cos(phase_arg) * weight, 0.0)
        imag_part = np.where(inside, np.sin(phase_arg) * weight, 0.0) * sign
        top = np.concatenate([real_part, -imag_part], axis=-1)
        bottom = np.concatenate([imag_part, real_part], axis=-1)
        block = np.concatenate([top, bottom], axis=-2)
        tables.append(block.reshape(2 * SHIFT + 1, 3 * 2 * height, 2 * height))
    return jnp.asarray(np.stack(tables, axis=0).astype(np.float32))


def column_bands():
    part = np.arange(3)[:, None, None]
    source = np.arange(LANE)[None, :, None] + (part - 1) * LANE
    target = np.arange(LANE)[None, None, :]
    distance = (source - target).astype(np.float64)
    inside = np.abs(distance) <= HALFCOL
    phase_arg = CHIRP_COL / HALFCOL * distance * distance
    weight = 1.0 / math.sqrt(2 * HALFCOL + 1)
    real_part = np.where(inside, np.cos(phase_arg) * weight, 0.0)
    imag_part = np.where(inside, np.sin(phase_arg) * weight, 0.0)
    forward = np.concatenate([real_part, imag_part], axis=-1)
    adjoint = np.concatenate([real_part, -imag_part], axis=-1)
    return jnp.asarray(np.stack([forward, adjoint], axis=0).astype(np.float32))


def dot3(a, x):
    a_high, a_low = split_bf16(a)
    x_high, x_low = split_bf16(x)
    f32 = jnp.float32
    return (
        jnp.dot(a_high, x_high, preferred_element_type=f32)
        + jnp.dot(a_high, x_low, preferred_element_type=f32)
        + jnp.dot(a_low, x_high, preferred_element_type=f32)
    )


CHUNKS = 4


def chain_kernel(rows, sections, u0_ref, vol_ref, off_ref, inten_ref, table_ref, cband_ref,
                 out_ref, terms_ref, partner_ref, field_ref, acc_ref, y_store, b_store, before, after,
                 bmh_ref, bml_ref, cos_ref, sin_ref, rband_ref, vol_slots, off_slots,
                 send_dn, send_up, recv_bf, recv_af, send_pair, recv_pair,
                 send_vol, send_off, recv_vol, recv_off):
    me = lax.axis_index("row")
    section = lax.axis_index("depth")
    partner = section + 1 - 2 * (section % 2)
    layers, height, columns = cos_ref.shape
    blocks = columns // LANE
    width = columns // CHUNKS
    per_chunk = blocks // CHUNKS
    has_up = me > 0
    has_dn = me < rows - 1

    barrier = pltpu.get_barrier_semaphore()

    @pl.when(has_up)
    def _():
        pl.semaphore_signal(barrier, 1, device_id={"row": me - 1}, device_id_type=MESH)

    @pl.when(has_dn)
    def _():
        pl.semaphore_signal(barrier, 1, device_id={"row": me + 1}, device_id_type=MESH)

    for step in range(1, sections):
        peer = (section + step) % sections
        pl.semaphore_signal(barrier, 1, device_id={"depth": peer}, device_id_type=MESH)
    peers = (me + rows - 1) // rows + (2 * rows - 2 - me) // rows
    pl.semaphore_wait(barrier, peers + sections - 1)

    def gathers(step, slot):
        peer = (section + step) % sections
        vol_copy = pltpu.make_async_remote_copy(
            src_ref=vol_ref.at[0], dst_ref=vol_slots.at[slot], send_sem=send_vol.at[step],
            recv_sem=recv_vol.at[slot], device_id={"depth": peer}, device_id_type=MESH)
        off_copy = pltpu.make_async_remote_copy(
            src_ref=off_ref, dst_ref=off_slots.at[slot], send_sem=send_off.at[step],
            recv_sem=recv_off.at[slot], device_id={"depth": peer}, device_id_type=MESH)
        return vol_copy, off_copy

    for step in range(1, sections):
        for one in gathers(step, section):
            one.start()
    vol_slots[section] = vol_ref[0]
    off_slots[section] = off_ref[...]
    part_rows = 2 * height

    def prepare(s):
        @pl.when(s != section)
        def _():
            for one in gathers(1, s):
                one.wait_recv()

        phase = PHASE_SCALE * vol_slots[s].astype(jnp.float32)
        cos_ref[s] = jnp.cos(phase)
        sin_ref[s] = jnp.sin(phase)
        shift = off_slots[s][0:1, 0:part_rows]
        forward_band = None
        adjoint_band = None
        for i in range(2 * SHIFT + 1):
            pick = jnp.where(shift == float(i - SHIFT), 1.0, 0.0)
            f_term = pick * table_ref[0, i]
            a_term = pick * table_ref[1, i]
            forward_band = f_term if forward_band is None else forward_band + f_term
            adjoint_band = a_term if adjoint_band is None else adjoint_band + a_term
        rband_ref[s] = forward_band
        rband_ref[2 * layers - 1 - s] = adjoint_band

    zero_block = jnp.zeros((2 * height, LANE), jnp.bfloat16)
    for ref in (bmh_ref, bml_ref):
        ref[0] = zero_block
        ref[blocks + 1] = zero_block

    def copies(k, c, store):
        cols = pl.ds(c * width, width)
        slot = k * CHUNKS + c
        down = pltpu.make_async_remote_copy(
            src_ref=store.at[:, cols], dst_ref=before.at[k, :, cols], send_sem=send_dn.at[slot],
            recv_sem=recv_bf.at[slot], device_id={"row": me + 1}, device_id_type=MESH)
        up = pltpu.make_async_remote_copy(
            src_ref=store.at[:, cols], dst_ref=after.at[k, :, cols], send_sem=send_up.at[slot],
            recv_sem=recv_af.at[slot], device_id={"row": me - 1}, device_id_type=MESH)
        return down, up

    def start(k, c, store):
        down, up = copies(k, c, store)

        @pl.when(has_dn)
        def _():
            down.start()

        @pl.when(has_up)
        def _():
            up.start()

    def finish(k, store):
        for c in range(CHUNKS):
            down, up = copies(k, c, store)

            @pl.when(has_dn)
            def _():
                down.wait_send()

            @pl.when(has_up)
            def _():
                up.wait_send()

    def halo(k, c, store):
        down, up = copies(k, c, store)
        cols = pl.ds(c * width, width)
        slot = k % 2

        @pl.when(has_up)
        def _():
            down.wait_recv()
            acc_ref[slot, :, cols] += dot3(rband_ref[k, 0:part_rows], before[k, :, cols])

        @pl.when(has_dn)
        def _():
            up.wait_recv()
            acc_ref[slot, :, cols] += dot3(rband_ref[k, 2 * part_rows:3 * part_rows], after[k, :, cols])

        return acc_ref[slot, :, cols]

    def emit(k, c, store, value):
        cols = pl.ds(c * width, width)
        store[:, cols] = value
        acc_ref[k % 2, :, cols] = dot3(rband_ref[k, part_rows:2 * part_rows], store[:, cols])
        start(k, c, store)

    def write_blocks(c, x):
        high, low = split_bf16(x)
        for b in range(per_chunk):
            bmh_ref[c * per_chunk + b + 1] = high[:, b * LANE:(b + 1) * LANE]
            bml_ref[c * per_chunk + b + 1] = low[:, b * LANE:(b + 1) * LANE]

    def wave(k, store, store_next, finish_chunk, make_chunk, early=None):
        for c in range(CHUNKS):
            if c == CHUNKS - 1 and early is not None:
                early()
            write_blocks(c, finish_chunk(c, halo(k, c, store)))
            if c >= 1:
                emit(k + 1, c - 1, store_next, make_chunk(c - 1))
        emit(k + 1, CHUNKS - 1, store_next, make_chunk(CHUNKS - 1))
        finish(k, store)

    def col_chunk(c, which):
        total = None
        f32 = jnp.float32
        first = c * per_chunk
        for t in range(3):
            xh = bmh_ref[first + t:first + t + per_chunk].reshape(per_chunk * 2 * height, LANE)
            xl = bml_ref[first + t:first + t + per_chunk].reshape(per_chunk * 2 * height, LANE)
            wh, wl = split_bf16(cband_ref[which, t])
            part = (jnp.dot(xh, wh, preferred_element_type=f32) + jnp.dot(xh, wl, preferred_element_type=f32)
                    + jnp.dot(xl, wh, preferred_element_type=f32))
            total = part if total is None else total + part
        total = total.reshape(per_chunk, 2 * height, 2 * LANE)
        real_part = total[:, :height, :LANE] - total[:, height:, LANE:]
        imag_part = total[:, :height, LANE:] + total[:, height:, :LANE]
        out = jnp.concatenate([real_part, imag_part], axis=1)
        return jnp.concatenate([out[b] for b in range(per_chunk)], axis=1)

    def rotated(s, c, u):
        cols = pl.ds(c * width, width)
        cs = cos_ref[s, :, cols]
        sn = sin_ref[s, :, cols]
        ur = u[:height]
        ui = u[height:]
        return jnp.concatenate([cs * ur - sn * ui, cs * ui + sn * ur], axis=0)

    def adjoint_chunk(s, c, a):
        cols = pl.ds(c * width, width)
        ar = a[:height]
        ai = a[height:]
        y = y_store[s, :, cols]
        terms_ref[s, :, cols] = PHASE_SCALE * (y[:height] * ai - y[height:] * ar)
        cs = cos_ref[s, :, cols]
        sn = sin_ref[s, :, cols]
        return jnp.concatenate([cs * ar + sn * ai, cs * ai - sn * ar], axis=0)

    prepare(0)
    for c in range(CHUNKS):
        emit(0, c, y_store.at[0], rotated(0, c, u0_ref[:, c * width:(c + 1) * width]))
    prepare(1)

    def forward(k, carry):
        def early():
            @pl.when(k + 2 < layers)
            def _():
                prepare(k + 2)

        wave(k, y_store.at[k], y_store.at[k + 1], lambda c, a: a,
             lambda c: rotated(k + 1, c, col_chunk(c, 0)), early)
        return carry

    lax.fori_loop(0, layers - 1, forward, 0)
    for c in range(CHUNKS):
        write_blocks(c, halo(layers - 1, c, y_store.at[layers - 1]))
    finish(layers - 1, y_store.at[layers - 1])
    for c in range(CHUNKS):
        field_ref[:, c * width:(c + 1) * width] = col_chunk(c, 0)
    u = field_ref[...]
    ur = u[:height]
    ui = u[height:]
    errors = ur * ur + ui * ui - inten_ref[...]
    field_ref[...] = jnp.concatenate([2.0 * errors * ur, 2.0 * errors * ui], axis=0)
    for c in range(CHUNKS):
        write_blocks(c, field_ref[:, c * width:(c + 1) * width])
    for c in range(CHUNKS):
        emit(layers, c, b_store.at[0], col_chunk(c, 1))

    def backward(j, carry):
        s = layers - 1 - j
        wave(layers + j, b_store.at[j], b_store.at[j + 1], lambda c, a: adjoint_chunk(s, c, a),
             lambda c: col_chunk(c, 1))
        return carry

    lax.fori_loop(0, layers - 1, backward, 0)
    last = 2 * layers - 1
    for c in range(CHUNKS):
        adjoint_chunk(0, c, halo(last, c, b_store.at[layers - 1]))
    finish(last, b_store.at[layers - 1])
    own = terms_ref[section]
    exchange = pltpu.make_async_remote_copy(
        src_ref=terms_ref.at[partner], dst_ref=partner_ref, send_sem=send_pair, recv_sem=recv_pair,
        device_id={"depth": partner}, device_id_type=MESH)
    exchange.start()
    exchange.wait_send()
    exchange.wait_recv()
    out_ref[0] = own + partner_ref[...]
    for step in range(1, sections):
        for one in gathers(step, section):
            one.wait_send()


def run_chain(u0, index_volume, offsets, intensity, rows, sections):
    _, height, columns = index_volume.shape
    layers = sections
    blocks = columns // LANE
    field = (2 * height, columns)
    off_tile = jnp.broadcast_to(offsets.astype(jnp.float32)[:, None], (8, LANE))
    plane = (layers, height, columns)
    return pl.pallas_call(
        functools.partial(chain_kernel, rows, sections),
        out_shape=jax.ShapeDtypeStruct((1, height, columns), jnp.float32),
        in_specs=[pl.BlockSpec(memory_space=pltpu.VMEM)] * 6,
        out_specs=pl.BlockSpec(memory_space=pltpu.VMEM),
        scratch_shapes=[
            pltpu.VMEM(plane, jnp.float32),
            pltpu.VMEM((height, columns), jnp.float32),
            pltpu.VMEM(field, jnp.float32),
            pltpu.VMEM((2,) + field, jnp.float32),
            pltpu.VMEM((layers,) + field, jnp.float32),
            pltpu.VMEM((layers,) + field, jnp.float32),
            pltpu.VMEM((2 * layers,) + field, jnp.float32),
            pltpu.VMEM((2 * layers,) + field, jnp.float32),
            pltpu.VMEM((blocks + 2, 2 * height, LANE), jnp.bfloat16),
            pltpu.VMEM((blocks + 2, 2 * height, LANE), jnp.bfloat16),
            pltpu.VMEM(plane, jnp.float32),
            pltpu.VMEM(plane, jnp.float32),
            pltpu.VMEM((2 * layers, 3 * 2 * height, 2 * height), jnp.float32),
            pltpu.VMEM(plane, index_volume.dtype),
            pltpu.VMEM((sections, 8, LANE), jnp.float32),
            pltpu.SemaphoreType.DMA((2 * layers * CHUNKS,)),
            pltpu.SemaphoreType.DMA((2 * layers * CHUNKS,)),
            pltpu.SemaphoreType.DMA((2 * layers * CHUNKS,)),
            pltpu.SemaphoreType.DMA((2 * layers * CHUNKS,)),
            pltpu.SemaphoreType.DMA,
            pltpu.SemaphoreType.DMA,
            pltpu.SemaphoreType.DMA((sections,)),
            pltpu.SemaphoreType.DMA((sections,)),
            pltpu.SemaphoreType.DMA((sections,)),
            pltpu.SemaphoreType.DMA((sections,)),
        ],
        compiler_params=pltpu.CompilerParams(
            collective_id=0, has_side_effects=True, vmem_limit_bytes=56 * 1024 * 1024),
    )(u0, index_volume, off_tile, intensity, band_table(height), column_bands())


def gather_kernel(sections, vol_ref, off_ref, vol_out, off_out, vol_slots, off_slots,
                  send_vol, send_off, recv_vol, recv_off):
    me = lax.axis_index("depth")
    barrier = pltpu.get_barrier_semaphore()
    for step in range(1, sections):
        peer = (me + step) % sections
        pl.semaphore_signal(barrier, 1, device_id={"depth": peer}, device_id_type=MESH)
    pl.semaphore_wait(barrier, sections - 1)

    def copies(step):
        peer = (me + step) % sections
        source = (me + sections - step) % sections
        out_vol = pltpu.make_async_remote_copy(
            src_ref=vol_ref.at[0], dst_ref=vol_slots.at[me], send_sem=send_vol.at[step],
            recv_sem=recv_vol.at[me], device_id={"depth": peer}, device_id_type=MESH)
        out_off = pltpu.make_async_remote_copy(
            src_ref=off_ref, dst_ref=off_slots.at[me], send_sem=send_off.at[step],
            recv_sem=recv_off.at[me], device_id={"depth": peer}, device_id_type=MESH)
        in_vol = pltpu.make_async_remote_copy(
            src_ref=vol_ref.at[0], dst_ref=vol_slots.at[source], send_sem=send_vol.at[step],
            recv_sem=recv_vol.at[source], device_id={"depth": peer}, device_id_type=MESH)
        in_off = pltpu.make_async_remote_copy(
            src_ref=off_ref, dst_ref=off_slots.at[source], send_sem=send_off.at[step],
            recv_sem=recv_off.at[source], device_id={"depth": peer}, device_id_type=MESH)
        return out_vol, out_off, in_vol, in_off

    for step in range(1, sections):
        out_vol, out_off, _, _ = copies(step)
        out_vol.start()
        out_off.start()
    vol_slots[me] = vol_ref[0]
    off_slots[me] = off_ref[...]
    for step in range(1, sections):
        out_vol, out_off, in_vol, in_off = copies(step)
        in_vol.wait_recv()
        in_off.wait_recv()
        out_vol.wait_send()
        out_off.wait_send()
    vol_out[...] = vol_slots[...]
    off_out[...] = off_slots[...]


def gather_depth(index_volume, offsets, sections):
    _, height, columns = index_volume.shape
    off_tile = jnp.broadcast_to(offsets.astype(jnp.float32)[:, None], (8, LANE))
    vol_shape = (sections, height, columns)
    off_shape = (sections, 8, LANE)
    return pl.pallas_call(
        functools.partial(gather_kernel, sections),
        out_shape=(jax.ShapeDtypeStruct(vol_shape, index_volume.dtype),
                   jax.ShapeDtypeStruct(off_shape, jnp.float32)),
        in_specs=[pl.BlockSpec(memory_space=pltpu.VMEM)] * 2,
        out_specs=(pl.BlockSpec(memory_space=pltpu.VMEM),) * 2,
        scratch_shapes=[
            pltpu.VMEM(vol_shape, index_volume.dtype),
            pltpu.VMEM(off_shape, jnp.float32),
            pltpu.SemaphoreType.DMA((sections,)),
            pltpu.SemaphoreType.DMA((sections,)),
            pltpu.SemaphoreType.DMA((sections,)),
            pltpu.SemaphoreType.DMA((sections,)),
        ],
        compiler_params=pltpu.CompilerParams(collective_id=1, has_side_effects=True),
    )(index_volume, off_tile)


def plane_wave(angle, row_start, height, columns, total_rows, total_cols):
    across = angle - TILTS // 2
    along = jnp.mod(3 * angle, TILTS) - TILTS // 2
    row_index = row_start + lax.broadcasted_iota(jnp.int32, (height, columns), 0)
    col_index = lax.broadcasted_iota(jnp.int32, (height, columns), 1)
    period = total_cols * total_rows
    cycles_int = jnp.mod(across * col_index * total_rows + along * row_index * total_cols, period)
    phase_arg = 2.0 * math.pi / period * cycles_int.astype(jnp.float32)
    return jnp.concatenate([jnp.cos(phase_arg), jnp.sin(phase_arg)], axis=0)


def body(index_volume, angles, offsets, measured):
    sections = lax.axis_size("depth")
    rows = lax.axis_size("row")
    section_no = lax.axis_index("depth")
    height = index_volume.shape[1]
    columns = index_volume.shape[2]
    row_start = lax.axis_index("row") * height
    total_rows = height * rows
    angle_count = angles.shape[0]
    angle_no = section_no % angle_count
    intensity = lax.dynamic_index_in_dim(measured, angle_no, 0, keepdims=False).astype(jnp.float32)
    angle = lax.dynamic_index_in_dim(angles, angle_no, 0, keepdims=False)
    incident = plane_wave(angle, row_start, height, columns, total_rows, columns)
    return run_chain(incident, index_volume, offsets, intensity, rows, sections)


def solution(mesh):
    in_specs = (P("depth", "row", None), P(), P("depth"), P(None, "row", None))
    out_specs = P("depth", "row", None)
    return jax.shard_map(body, mesh=mesh, in_specs=in_specs, out_specs=out_specs, check_vma=False)
```

```python
import functools
import math

import jax
import numpy as np
import jax.numpy as jnp
from jax import lax
from jax.experimental import pallas as pl
from jax.experimental.pallas import tpu as pltpu
from jax.sharding import PartitionSpec as P

TILTS = 16
HALF = 10
SHIFT = 4
HALFCOL = 64
LANE = 128

PHASE_SCALE = 0.5
CHIRP_ROW = 1.3
CHIRP_COL = 1.7
MESH = pl.DeviceIdType.MESH


def kernel_values(distance, radius, chirp_rate):
    inside = jnp.abs(distance) <= radius
    phase_arg = chirp_rate / radius * distance * distance
    weight = 1.0 / math.sqrt(2 * radius + 1)
    real_part = jnp.where(inside, jnp.cos(phase_arg) * weight, 0.0)
    imag_part = jnp.where(inside, jnp.sin(phase_arg) * weight, 0.0)
    return (real_part, imag_part)


def split_bf16(x):
    high = x.astype(jnp.bfloat16)
    low = (x - high.astype(jnp.float32)).astype(jnp.bfloat16)
    return high, low


def complex_block(real_part, imag_part):
    top = jnp.concatenate([real_part, -imag_part], axis=-1)
    bottom = jnp.concatenate([imag_part, real_part], axis=-1)
    return jnp.concatenate([top, bottom], axis=-2)


def band_table(height):
    offsets = np.arange(-SHIFT, SHIFT + 1)[:, None, None, None]
    part = np.arange(3)[None, :, None, None]
    target = np.arange(height)[None, None, :, None]
    source = np.arange(height)[None, None, None, :] + (part - 1) * height
    tables = []
    for sign in (1, -1):
        distance = (source - target - sign * offsets).astype(np.float64)
        inside = np.abs(distance) <= HALF
        phase_arg = CHIRP_ROW / HALF * distance * distance
        weight = 1.0 / math.sqrt(2 * HALF + 1)
        real_part = np.where(inside, np.cos(phase_arg) * weight, 0.0)
        imag_part = np.where(inside, np.sin(phase_arg) * weight, 0.0) * sign
        top = np.concatenate([real_part, -imag_part], axis=-1)
        bottom = np.concatenate([imag_part, real_part], axis=-1)
        block = np.concatenate([top, bottom], axis=-2)
        tables.append(block.reshape(2 * SHIFT + 1, 3 * 2 * height, 2 * height))
    return jnp.asarray(np.stack(tables, axis=0).astype(np.float32))


def column_bands():
    part = np.arange(3)[:, None, None]
    source = np.arange(LANE)[None, :, None] + (part - 1) * LANE
    target = np.arange(LANE)[None, None, :]
    distance = (source - target).astype(np.float64)
    inside = np.abs(distance) <= HALFCOL
    phase_arg = CHIRP_COL / HALFCOL * distance * distance
    weight = 1.0 / math.sqrt(2 * HALFCOL + 1)
    real_part = np.where(inside, np.cos(phase_arg) * weight, 0.0)
    imag_part = np.where(inside, np.sin(phase_arg) * weight, 0.0)
    forward = np.concatenate([real_part, imag_part], axis=-1)
    adjoint = np.concatenate([real_part, -imag_part], axis=-1)
    return jnp.asarray(np.stack([forward, adjoint], axis=0).astype(np.float32))


def dot3(a_high, a_low, x):
    x_high, x_low = split_bf16(x)
    f32 = jnp.float32
    return (
        jnp.dot(a_high, x_high, preferred_element_type=f32)
        + jnp.dot(a_high, x_low, preferred_element_type=f32)
        + jnp.dot(a_low, x_high, preferred_element_type=f32)
    )


CHUNKS = 4


def chain_kernel(rows, sections, u0_ref, vol_ref, off_ref, inten_ref, table_ref, cband_ref,
                 out_ref, terms_ref, partner_ref, field_ref, acc_ref, y_store, b_store, before, after,
                 bmh_ref, bml_ref, cos_ref, sin_ref, rband_ref, vol_slots, off_slots,
                 send_dn, send_up, recv_bf, recv_af, send_pair, recv_pair,
                 send_vol, send_off, recv_vol, recv_off, chb_ref, clb_ref, rbh_ref, rbl_ref):
    me = lax.axis_index("row")
    section = lax.axis_index("depth")
    partner = section + 1 - 2 * (section % 2)
    layers, height, columns = cos_ref.shape
    blocks = columns // LANE
    width = columns // CHUNKS
    per_chunk = blocks // CHUNKS
    has_up = me > 0
    has_dn = me < rows - 1

    barrier = pltpu.get_barrier_semaphore()

    @pl.when(has_up)
    def _():
        pl.semaphore_signal(barrier, 1, device_id={"row": me - 1}, device_id_type=MESH)

    @pl.when(has_dn)
    def _():
        pl.semaphore_signal(barrier, 1, device_id={"row": me + 1}, device_id_type=MESH)

    for step in range(1, sections):
        peer = (section + step) % sections
        pl.semaphore_signal(barrier, 1, device_id={"depth": peer}, device_id_type=MESH)
    peers = (me + rows - 1) // rows + (2 * rows - 2 - me) // rows
    pl.semaphore_wait(barrier, peers + sections - 1)

    def gathers(step, slot):
        peer = (section + step) % sections
        vol_copy = pltpu.make_async_remote_copy(
            src_ref=vol_ref.at[0], dst_ref=vol_slots.at[slot], send_sem=send_vol.at[step],
            recv_sem=recv_vol.at[slot], device_id={"depth": peer}, device_id_type=MESH)
        off_copy = pltpu.make_async_remote_copy(
            src_ref=off_ref, dst_ref=off_slots.at[slot], send_sem=send_off.at[step],
            recv_sem=recv_off.at[slot], device_id={"depth": peer}, device_id_type=MESH)
        return vol_copy, off_copy

    for step in range(1, sections):
        for one in gathers(step, section):
            one.start()
    vol_slots[section] = vol_ref[0]
    off_slots[section] = off_ref[...]
    part_rows = 2 * height

    def prepare(s):
        @pl.when(s != section)
        def _():
            for one in gathers(1, s):
                one.wait_recv()

        phase = PHASE_SCALE * vol_slots[s].astype(jnp.float32)
        cos_ref[s] = jnp.cos(phase)
        sin_ref[s] = jnp.sin(phase)
        shift = off_slots[s][0:1, 0:part_rows]
        forward_band = None
        adjoint_band = None
        for i in range(2 * SHIFT + 1):
            pick = jnp.where(shift == float(i - SHIFT), 1.0, 0.0)
            f_term = pick * table_ref[0, i]
            a_term = pick * table_ref[1, i]
            forward_band = f_term if forward_band is None else forward_band + f_term
            adjoint_band = a_term if adjoint_band is None else adjoint_band + a_term
        high, low = split_bf16(forward_band)
        rbh_ref[s] = high
        rbl_ref[s] = low
        high, low = split_bf16(adjoint_band)
        rbh_ref[2 * layers - 1 - s] = high
        rbl_ref[2 * layers - 1 - s] = low

    high, low = split_bf16(cband_ref[...])
    chb_ref[...] = high
    clb_ref[...] = low
    zero_block = jnp.zeros((2 * height, LANE), jnp.bfloat16)
    for ref in (bmh_ref, bml_ref):
        ref[0] = zero_block
        ref[blocks + 1] = zero_block

    def copies(k, c, store):
        cols = pl.ds(c * width, width)
        slot = k * CHUNKS + c
        down = pltpu.make_async_remote_copy(
            src_ref=store.at[:, cols], dst_ref=before.at[k, :, cols], send_sem=send_dn.at[slot],
            recv_sem=recv_bf.at[slot], device_id={"row": me + 1}, device_id_type=MESH)
        up = pltpu.make_async_remote_copy(
            src_ref=store.at[:, cols], dst_ref=after.at[k, :, cols], send_sem=send_up.at[slot],
            recv_sem=recv_af.at[slot], device_id={"row": me - 1}, device_id_type=MESH)
        return down, up

    def start(k, c, store):
        down, up = copies(k, c, store)

        @pl.when(has_dn)
        def _():
            down.start()

        @pl.when(has_up)
        def _():
            up.start()

    def finish(k, store):
        for c in range(CHUNKS):
            down, up = copies(k, c, store)

            @pl.when(has_dn)
            def _():
                down.wait_send()

            @pl.when(has_up)
            def _():
                up.wait_send()

    def halo(k, c, store):
        down, up = copies(k, c, store)
        cols = pl.ds(c * width, width)
        slot = k % 2

        @pl.when(has_up)
        def _():
            down.wait_recv()
            acc_ref[slot, :, cols] += dot3(rbh_ref[k, 0:part_rows], rbl_ref[k, 0:part_rows], before[k, :, cols])

        @pl.when(has_dn)
        def _():
            up.wait_recv()
            acc_ref[slot, :, cols] += dot3(rbh_ref[k, 2 * part_rows:3 * part_rows], rbl_ref[k, 2 * part_rows:3 * part_rows], after[k, :, cols])

        return acc_ref[slot, :, cols]

    def emit(k, c, store, value):
        cols = pl.ds(c * width, width)
        store[:, cols] = value
        acc_ref[k % 2, :, cols] = dot3(rbh_ref[k, part_rows:2 * part_rows], rbl_ref[k, part_rows:2 * part_rows], store[:, cols])
        start(k, c, store)

    def write_blocks(c, x):
        high, low = split_bf16(x)
        for b in range(per_chunk):
            bmh_ref[c * per_chunk + b + 1] = high[:, b * LANE:(b + 1) * LANE]
            bml_ref[c * per_chunk + b + 1] = low[:, b * LANE:(b + 1) * LANE]

    def wave(k, store, store_next, finish_chunk, make_chunk):
        for c in range(CHUNKS):
            write_blocks(c, finish_chunk(c, halo(k, c, store)))
            if c >= 1:
                emit(k + 1, c - 1, store_next, make_chunk(c - 1))
        emit(k + 1, CHUNKS - 1, store_next, make_chunk(CHUNKS - 1))
        finish(k, store)

    def col_chunk(c, which):
        total = None
        f32 = jnp.float32
        first = c * per_chunk
        for t in range(3):
            xh = bmh_ref[first + t:first + t + per_chunk].reshape(per_chunk * 2 * height, LANE)
            xl = bml_ref[first + t:first + t + per_chunk].reshape(per_chunk * 2 * height, LANE)
            wh = chb_ref[which, t]
            wl = clb_ref[which, t]
            part = (jnp.dot(xh, wh, preferred_element_type=f32) + jnp.dot(xh, wl, preferred_element_type=f32)
                    + jnp.dot(xl, wh, preferred_element_type=f32))
            total = part if total is None else total + part
        total = total.reshape(per_chunk, 2 * height, 2 * LANE)
        real_part = total[:, :height, :LANE] - total[:, height:, LANE:]
        imag_part = total[:, :height, LANE:] + total[:, height:, :LANE]
        out = jnp.concatenate([real_part, imag_part], axis=1)
        return jnp.concatenate([out[b] for b in range(per_chunk)], axis=1)

    def rotated(s, c, u):
        cols = pl.ds(c * width, width)
        cs = cos_ref[s, :, cols]
        sn = sin_ref[s, :, cols]
        ur = u[:height]
        ui = u[height:]
        return jnp.concatenate([cs * ur - sn * ui, cs * ui + sn * ur], axis=0)

    def adjoint_chunk(s, c, a):
        cols = pl.ds(c * width, width)
        ar = a[:height]
        ai = a[height:]
        y = y_store[s, :, cols]
        terms_ref[s, :, cols] = PHASE_SCALE * (y[:height] * ai - y[height:] * ar)
        cs = cos_ref[s, :, cols]
        sn = sin_ref[s, :, cols]
        return jnp.concatenate([cs * ar + sn * ai, cs * ai - sn * ar], axis=0)

    prepare(0)
    for c in range(CHUNKS):
        emit(0, c, y_store.at[0], rotated(0, c, u0_ref[:, c * width:(c + 1) * width]))

    def forward(k, carry):
        prepare(k + 1)
        wave(k, y_store.at[k], y_store.at[k + 1], lambda c, a: a,
             lambda c: rotated(k + 1, c, col_chunk(c, 0)))
        return carry

    lax.fori_loop(0, layers - 1, forward, 0)
    for c in range(CHUNKS):
        write_blocks(c, halo(layers - 1, c, y_store.at[layers - 1]))
    finish(layers - 1, y_store.at[layers - 1])
    for c in range(CHUNKS):
        field_ref[:, c * width:(c + 1) * width] = col_chunk(c, 0)
    u = field_ref[...]
    ur = u[:height]
    ui = u[height:]
    errors = ur * ur + ui * ui - inten_ref[...]
    field_ref[...] = jnp.concatenate([2.0 * errors * ur, 2.0 * errors * ui], axis=0)
    for c in range(CHUNKS):
        write_blocks(c, field_ref[:, c * width:(c + 1) * width])
    for c in range(CHUNKS):
        emit(layers, c, b_store.at[0], col_chunk(c, 1))

    def backward(j, carry):
        s = layers - 1 - j
        wave(layers + j, b_store.at[j], b_store.at[j + 1], lambda c, a: adjoint_chunk(s, c, a),
             lambda c: col_chunk(c, 1))
        return carry

    lax.fori_loop(0, layers - 1, backward, 0)
    last = 2 * layers - 1
    for c in range(CHUNKS):
        adjoint_chunk(0, c, halo(last, c, b_store.at[layers - 1]))
    finish(last, b_store.at[layers - 1])
    own = terms_ref[section]
    exchange = pltpu.make_async_remote_copy(
        src_ref=terms_ref.at[partner], dst_ref=partner_ref, send_sem=send_pair, recv_sem=recv_pair,
        device_id={"depth": partner}, device_id_type=MESH)
    exchange.start()
    exchange.wait_send()
    exchange.wait_recv()
    out_ref[0] = own + partner_ref[...]
    for step in range(1, sections):
        for one in gathers(step, section):
            one.wait_send()


def run_chain(u0, index_volume, offsets, intensity, rows, sections):
    _, height, columns = index_volume.shape
    layers = sections
    blocks = columns // LANE
    field = (2 * height, columns)
    off_tile = jnp.broadcast_to(offsets.astype(jnp.float32)[:, None], (8, LANE))
    plane = (layers, height, columns)
    return pl.pallas_call(
        functools.partial(chain_kernel, rows, sections),
        out_shape=jax.ShapeDtypeStruct((1, height, columns), jnp.float32),
        in_specs=[pl.BlockSpec(memory_space=pltpu.VMEM)] * 6,
        out_specs=pl.BlockSpec(memory_space=pltpu.VMEM),
        scratch_shapes=[
            pltpu.VMEM(plane, jnp.float32),
            pltpu.VMEM((height, columns), jnp.float32),
            pltpu.VMEM(field, jnp.float32),
            pltpu.VMEM((2,) + field, jnp.float32),
            pltpu.VMEM((layers,) + field, jnp.float32),
            pltpu.VMEM((layers,) + field, jnp.float32),
            pltpu.VMEM((2 * layers,) + field, jnp.float32),
            pltpu.VMEM((2 * layers,) + field, jnp.float32),
            pltpu.VMEM((blocks + 2, 2 * height, LANE), jnp.bfloat16),
            pltpu.VMEM((blocks + 2, 2 * height, LANE), jnp.bfloat16),
            pltpu.VMEM(plane, jnp.float32),
            pltpu.VMEM(plane, jnp.float32),
            pltpu.VMEM((2 * layers, 3 * 2 * height, 2 * height), jnp.float32),
            pltpu.VMEM(plane, index_volume.dtype),
            pltpu.VMEM((sections, 8, LANE), jnp.float32),
            pltpu.SemaphoreType.DMA((2 * layers * CHUNKS,)),
            pltpu.SemaphoreType.DMA((2 * layers * CHUNKS,)),
            pltpu.SemaphoreType.DMA((2 * layers * CHUNKS,)),
            pltpu.SemaphoreType.DMA((2 * layers * CHUNKS,)),
            pltpu.SemaphoreType.DMA,
            pltpu.SemaphoreType.DMA,
            pltpu.SemaphoreType.DMA((sections,)),
            pltpu.SemaphoreType.DMA((sections,)),
            pltpu.SemaphoreType.DMA((sections,)),
            pltpu.SemaphoreType.DMA((sections,)),
            pltpu.VMEM((2, 3, LANE, 2 * LANE), jnp.bfloat16),
            pltpu.VMEM((2, 3, LANE, 2 * LANE), jnp.bfloat16),
            pltpu.VMEM((2 * layers, 3 * 2 * height, 2 * height), jnp.bfloat16),
            pltpu.VMEM((2 * layers, 3 * 2 * height, 2 * height), jnp.bfloat16),
        ],
        compiler_params=pltpu.CompilerParams(
            collective_id=0, has_side_effects=True, vmem_limit_bytes=56 * 1024 * 1024),
    )(u0, index_volume, off_tile, intensity, band_table(height), column_bands())


def gather_kernel(sections, vol_ref, off_ref, vol_out, off_out, vol_slots, off_slots,
                  send_vol, send_off, recv_vol, recv_off, chb_ref, clb_ref, rbh_ref, rbl_ref):
    me = lax.axis_index("depth")
    barrier = pltpu.get_barrier_semaphore()
    for step in range(1, sections):
        peer = (me + step) % sections
        pl.semaphore_signal(barrier, 1, device_id={"depth": peer}, device_id_type=MESH)
    pl.semaphore_wait(barrier, sections - 1)

    def copies(step):
        peer = (me + step) % sections
        source = (me + sections - step) % sections
        out_vol = pltpu.make_async_remote_copy(
            src_ref=vol_ref.at[0], dst_ref=vol_slots.at[me], send_sem=send_vol.at[step],
            recv_sem=recv_vol.at[me], device_id={"depth": peer}, device_id_type=MESH)
        out_off = pltpu.make_async_remote_copy(
            src_ref=off_ref, dst_ref=off_slots.at[me], send_sem=send_off.at[step],
            recv_sem=recv_off.at[me], device_id={"depth": peer}, device_id_type=MESH)
        in_vol = pltpu.make_async_remote_copy(
            src_ref=vol_ref.at[0], dst_ref=vol_slots.at[source], send_sem=send_vol.at[step],
            recv_sem=recv_vol.at[source], device_id={"depth": peer}, device_id_type=MESH)
        in_off = pltpu.make_async_remote_copy(
            src_ref=off_ref, dst_ref=off_slots.at[source], send_sem=send_off.at[step],
            recv_sem=recv_off.at[source], device_id={"depth": peer}, device_id_type=MESH)
        return out_vol, out_off, in_vol, in_off

    for step in range(1, sections):
        out_vol, out_off, _, _ = copies(step)
        out_vol.start()
        out_off.start()
    vol_slots[me] = vol_ref[0]
    off_slots[me] = off_ref[...]
    for step in range(1, sections):
        out_vol, out_off, in_vol, in_off = copies(step)
        in_vol.wait_recv()
        in_off.wait_recv()
        out_vol.wait_send()
        out_off.wait_send()
    vol_out[...] = vol_slots[...]
    off_out[...] = off_slots[...]


def gather_depth(index_volume, offsets, sections):
    _, height, columns = index_volume.shape
    off_tile = jnp.broadcast_to(offsets.astype(jnp.float32)[:, None], (8, LANE))
    vol_shape = (sections, height, columns)
    off_shape = (sections, 8, LANE)
    return pl.pallas_call(
        functools.partial(gather_kernel, sections),
        out_shape=(jax.ShapeDtypeStruct(vol_shape, index_volume.dtype),
                   jax.ShapeDtypeStruct(off_shape, jnp.float32)),
        in_specs=[pl.BlockSpec(memory_space=pltpu.VMEM)] * 2,
        out_specs=(pl.BlockSpec(memory_space=pltpu.VMEM),) * 2,
        scratch_shapes=[
            pltpu.VMEM(vol_shape, index_volume.dtype),
            pltpu.VMEM(off_shape, jnp.float32),
            pltpu.SemaphoreType.DMA((sections,)),
            pltpu.SemaphoreType.DMA((sections,)),
            pltpu.SemaphoreType.DMA((sections,)),
            pltpu.SemaphoreType.DMA((sections,)),
            pltpu.VMEM((2, 3, LANE, 2 * LANE), jnp.bfloat16),
            pltpu.VMEM((2, 3, LANE, 2 * LANE), jnp.bfloat16),
            pltpu.VMEM((2 * layers, 3 * 2 * height, 2 * height), jnp.bfloat16),
            pltpu.VMEM((2 * layers, 3 * 2 * height, 2 * height), jnp.bfloat16),
        ],
        compiler_params=pltpu.CompilerParams(collective_id=1, has_side_effects=True),
    )(index_volume, off_tile)


def plane_wave(angle, row_start, height, columns, total_rows, total_cols):
    across = angle - TILTS // 2
    along = jnp.mod(3 * angle, TILTS) - TILTS // 2
    row_index = row_start + lax.broadcasted_iota(jnp.int32, (height, columns), 0)
    col_index = lax.broadcasted_iota(jnp.int32, (height, columns), 1)
    period = total_cols * total_rows
    cycles_int = jnp.mod(across * col_index * total_rows + along * row_index * total_cols, period)
    phase_arg = 2.0 * math.pi / period * cycles_int.astype(jnp.float32)
    return jnp.concatenate([jnp.cos(phase_arg), jnp.sin(phase_arg)], axis=0)


def body(index_volume, angles, offsets, measured):
    sections = lax.axis_size("depth")
    rows = lax.axis_size("row")
    section_no = lax.axis_index("depth")
    height = index_volume.shape[1]
    columns = index_volume.shape[2]
    row_start = lax.axis_index("row") * height
    total_rows = height * rows
    angle_count = angles.shape[0]
    angle_no = section_no % angle_count
    intensity = lax.dynamic_index_in_dim(measured, angle_no, 0, keepdims=False).astype(jnp.float32)
    angle = lax.dynamic_index_in_dim(angles, angle_no, 0, keepdims=False)
    incident = plane_wave(angle, row_start, height, columns, total_rows, columns)
    return run_chain(incident, index_volume, offsets, intensity, rows, sections)


def solution(mesh):
    in_specs = (P("depth", "row", None), P(), P("depth"), P(None, "row", None))
    out_specs = P("depth", "row", None)
    return jax.shard_map(body, mesh=mesh, in_specs=in_specs, out_specs=out_specs, check_vma=False)
```

```python
import functools
import math

import jax
import numpy as np
import jax.numpy as jnp
from jax import lax
from jax.experimental import pallas as pl
from jax.experimental.pallas import tpu as pltpu
from jax.sharding import PartitionSpec as P

TILTS = 16
HALF = 10
SHIFT = 4
HALFCOL = 64
LANE = 128

PHASE_SCALE = 0.5
CHIRP_ROW = 1.3
CHIRP_COL = 1.7
MESH = pl.DeviceIdType.MESH


def kernel_values(distance, radius, chirp_rate):
    inside = jnp.abs(distance) <= radius
    phase_arg = chirp_rate / radius * distance * distance
    weight = 1.0 / math.sqrt(2 * radius + 1)
    real_part = jnp.where(inside, jnp.cos(phase_arg) * weight, 0.0)
    imag_part = jnp.where(inside, jnp.sin(phase_arg) * weight, 0.0)
    return (real_part, imag_part)


def split_bf16(x):
    high = x.astype(jnp.bfloat16)
    low = (x - high.astype(jnp.float32)).astype(jnp.bfloat16)
    return high, low


def complex_block(real_part, imag_part):
    top = jnp.concatenate([real_part, -imag_part], axis=-1)
    bottom = jnp.concatenate([imag_part, real_part], axis=-1)
    return jnp.concatenate([top, bottom], axis=-2)


def band_table(height):
    offsets = np.arange(-SHIFT, SHIFT + 1)[:, None, None, None]
    part = np.arange(3)[None, :, None, None]
    target = np.arange(height)[None, None, :, None]
    source = np.arange(height)[None, None, None, :] + (part - 1) * height
    tables = []
    for sign in (1, -1):
        distance = (source - target - sign * offsets).astype(np.float64)
        inside = np.abs(distance) <= HALF
        phase_arg = CHIRP_ROW / HALF * distance * distance
        weight = 1.0 / math.sqrt(2 * HALF + 1)
        real_part = np.where(inside, np.cos(phase_arg) * weight, 0.0)
        imag_part = np.where(inside, np.sin(phase_arg) * weight, 0.0) * sign
        top = np.concatenate([real_part, -imag_part], axis=-1)
        bottom = np.concatenate([imag_part, real_part], axis=-1)
        block = np.concatenate([top, bottom], axis=-2)
        tables.append(block.reshape(2 * SHIFT + 1, 3 * 2 * height, 2 * height))
    return jnp.asarray(np.stack(tables, axis=0).astype(np.float32))


def column_bands():
    part = np.arange(3)[:, None, None]
    source = np.arange(LANE)[None, :, None] + (part - 1) * LANE
    target = np.arange(LANE)[None, None, :]
    distance = (source - target).astype(np.float64)
    inside = np.abs(distance) <= HALFCOL
    phase_arg = CHIRP_COL / HALFCOL * distance * distance
    weight = 1.0 / math.sqrt(2 * HALFCOL + 1)
    real_part = np.where(inside, np.cos(phase_arg) * weight, 0.0)
    imag_part = np.where(inside, np.sin(phase_arg) * weight, 0.0)
    forward = np.concatenate([real_part, imag_part], axis=-1)
    adjoint = np.concatenate([real_part, -imag_part], axis=-1)
    return jnp.asarray(np.stack([forward, adjoint], axis=0).astype(np.float32))


def dot3(a_high, a_low, x):
    x_high, x_low = split_bf16(x)
    f32 = jnp.float32
    rows = a_high.shape[0]
    both = jnp.dot(jnp.concatenate([a_high, a_low], axis=0), x_high, preferred_element_type=f32)
    return both[:rows] + both[rows:] + jnp.dot(a_high, x_low, preferred_element_type=f32)


CHUNKS = 4


def chain_kernel(rows, sections, u0_ref, vol_ref, off_ref, inten_ref, table_ref, cband_ref,
                 out_ref, terms_ref, partner_ref, field_ref, acc_ref, y_store, b_store, before, after,
                 bmh_ref, bml_ref, cos_ref, sin_ref, rband_ref, vol_slots, off_slots,
                 send_dn, send_up, recv_bf, recv_af, send_pair, recv_pair,
                 send_vol, send_off, recv_vol, recv_off, chb_ref, clb_ref, rbh_ref, rbl_ref):
    me = lax.axis_index("row")
    section = lax.axis_index("depth")
    partner = section + 1 - 2 * (section % 2)
    layers, height, columns = cos_ref.shape
    blocks = columns // LANE
    width = columns // CHUNKS
    per_chunk = blocks // CHUNKS
    has_up = me > 0
    has_dn = me < rows - 1

    barrier = pltpu.get_barrier_semaphore()

    @pl.when(has_up)
    def _():
        pl.semaphore_signal(barrier, 1, device_id={"row": me - 1}, device_id_type=MESH)

    @pl.when(has_dn)
    def _():
        pl.semaphore_signal(barrier, 1, device_id={"row": me + 1}, device_id_type=MESH)

    for step in range(1, sections):
        peer = (section + step) % sections
        pl.semaphore_signal(barrier, 1, device_id={"depth": peer}, device_id_type=MESH)
    peers = (me + rows - 1) // rows + (2 * rows - 2 - me) // rows
    pl.semaphore_wait(barrier, peers + sections - 1)

    def gathers(step, slot):
        peer = (section + step) % sections
        vol_copy = pltpu.make_async_remote_copy(
            src_ref=vol_ref.at[0], dst_ref=vol_slots.at[slot], send_sem=send_vol.at[step],
            recv_sem=recv_vol.at[slot], device_id={"depth": peer}, device_id_type=MESH)
        off_copy = pltpu.make_async_remote_copy(
            src_ref=off_ref, dst_ref=off_slots.at[slot], send_sem=send_off.at[step],
            recv_sem=recv_off.at[slot], device_id={"depth": peer}, device_id_type=MESH)
        return vol_copy, off_copy

    for step in range(1, sections):
        for one in gathers(step, section):
            one.start()
    vol_slots[section] = vol_ref[0]
    off_slots[section] = off_ref[...]
    part_rows = 2 * height

    def prepare(s):
        @pl.when(s != section)
        def _():
            for one in gathers(1, s):
                one.wait_recv()

        phase = PHASE_SCALE * vol_slots[s].astype(jnp.float32)
        cos_ref[s] = jnp.cos(phase)
        sin_ref[s] = jnp.sin(phase)
        shift = off_slots[s][0:1, 0:part_rows]
        forward_band = None
        adjoint_band = None
        for i in range(2 * SHIFT + 1):
            pick = jnp.where(shift == float(i - SHIFT), 1.0, 0.0)
            f_term = pick * table_ref[0, i]
            a_term = pick * table_ref[1, i]
            forward_band = f_term if forward_band is None else forward_band + f_term
            adjoint_band = a_term if adjoint_band is None else adjoint_band + a_term
        high, low = split_bf16(forward_band)
        rbh_ref[s] = high
        rbl_ref[s] = low
        high, low = split_bf16(adjoint_band)
        rbh_ref[2 * layers - 1 - s] = high
        rbl_ref[2 * layers - 1 - s] = low

    high, low = split_bf16(cband_ref[...])
    chb_ref[...] = high
    clb_ref[...] = low
    zero_block = jnp.zeros((2 * height, LANE), jnp.bfloat16)
    for ref in (bmh_ref, bml_ref):
        ref[0] = zero_block
        ref[blocks + 1] = zero_block

    def copies(k, c, store):
        cols = pl.ds(c * width, width)
        slot = k * CHUNKS + c
        down = pltpu.make_async_remote_copy(
            src_ref=store.at[:, cols], dst_ref=before.at[k, :, cols], send_sem=send_dn.at[slot],
            recv_sem=recv_bf.at[slot], device_id={"row": me + 1}, device_id_type=MESH)
        up = pltpu.make_async_remote_copy(
            src_ref=store.at[:, cols], dst_ref=after.at[k, :, cols], send_sem=send_up.at[slot],
            recv_sem=recv_af.at[slot], device_id={"row": me - 1}, device_id_type=MESH)
        return down, up

    def start(k, c, store):
        down, up = copies(k, c, store)

        @pl.when(has_dn)
        def _():
            down.start()

        @pl.when(has_up)
        def _():
            up.start()

    def finish(k, store):
        for c in range(CHUNKS):
            down, up = copies(k, c, store)

            @pl.when(has_dn)
            def _():
                down.wait_send()

            @pl.when(has_up)
            def _():
                up.wait_send()

    def halo(k, c, store):
        down, up = copies(k, c, store)
        cols = pl.ds(c * width, width)
        slot = k % 2

        @pl.when(has_up)
        def _():
            down.wait_recv()
            acc_ref[slot, :, cols] += dot3(rbh_ref[k, 0:part_rows], rbl_ref[k, 0:part_rows], before[k, :, cols])

        @pl.when(has_dn)
        def _():
            up.wait_recv()
            acc_ref[slot, :, cols] += dot3(rbh_ref[k, 2 * part_rows:3 * part_rows], rbl_ref[k, 2 * part_rows:3 * part_rows], after[k, :, cols])

        return acc_ref[slot, :, cols]

    def emit(k, c, store, value):
        cols = pl.ds(c * width, width)
        store[:, cols] = value
        acc_ref[k % 2, :, cols] = dot3(rbh_ref[k, part_rows:2 * part_rows], rbl_ref[k, part_rows:2 * part_rows], store[:, cols])
        start(k, c, store)

    def write_blocks(c, x):
        high, low = split_bf16(x)
        for b in range(per_chunk):
            bmh_ref[c * per_chunk + b + 1] = high[:, b * LANE:(b + 1) * LANE]
            bml_ref[c * per_chunk + b + 1] = low[:, b * LANE:(b + 1) * LANE]

    def wave(k, store, store_next, finish_chunk, make_chunk):
        for c in range(CHUNKS):
            write_blocks(c, finish_chunk(c, halo(k, c, store)))
            if c >= 1:
                emit(k + 1, c - 1, store_next, make_chunk(c - 1))
        emit(k + 1, CHUNKS - 1, store_next, make_chunk(CHUNKS - 1))
        finish(k, store)

    def col_chunk(c, which):
        total = None
        f32 = jnp.float32
        first = c * per_chunk
        for t in range(3):
            xh = bmh_ref[first + t:first + t + per_chunk].reshape(per_chunk * 2 * height, LANE)
            xl = bml_ref[first + t:first + t + per_chunk].reshape(per_chunk * 2 * height, LANE)
            wh = chb_ref[which, t]
            wl = clb_ref[which, t]
            count = xh.shape[0]
            both = jnp.dot(jnp.concatenate([xh, xl], axis=0), wh, preferred_element_type=f32)
            part = both[:count] + both[count:] + jnp.dot(xh, wl, preferred_element_type=f32)
            total = part if total is None else total + part
        total = total.reshape(per_chunk, 2 * height, 2 * LANE)
        real_part = total[:, :height, :LANE] - total[:, height:, LANE:]
        imag_part = total[:, :height, LANE:] + total[:, height:, :LANE]
        out = jnp.concatenate([real_part, imag_part], axis=1)
        return jnp.concatenate([out[b] for b in range(per_chunk)], axis=1)

    def rotated(s, c, u):
        cols = pl.ds(c * width, width)
        cs = cos_ref[s, :, cols]
        sn = sin_ref[s, :, cols]
        ur = u[:height]
        ui = u[height:]
        return jnp.concatenate([cs * ur - sn * ui, cs * ui + sn * ur], axis=0)

    def adjoint_chunk(s, c, a):
        cols = pl.ds(c * width, width)
        ar = a[:height]
        ai = a[height:]
        y = y_store[s, :, cols]
        terms_ref[s, :, cols] = PHASE_SCALE * (y[:height] * ai - y[height:] * ar)
        cs = cos_ref[s, :, cols]
        sn = sin_ref[s, :, cols]
        return jnp.concatenate([cs * ar + sn * ai, cs * ai - sn * ar], axis=0)

    prepare(0)
    for c in range(CHUNKS):
        emit(0, c, y_store.at[0], rotated(0, c, u0_ref[:, c * width:(c + 1) * width]))

    def forward(k, carry):
        prepare(k + 1)
        wave(k, y_store.at[k], y_store.at[k + 1], lambda c, a: a,
             lambda c: rotated(k + 1, c, col_chunk(c, 0)))
        return carry

    lax.fori_loop(0, layers - 1, forward, 0)
    for c in range(CHUNKS):
        write_blocks(c, halo(layers - 1, c, y_store.at[layers - 1]))
    finish(layers - 1, y_store.at[layers - 1])
    for c in range(CHUNKS):
        field_ref[:, c * width:(c + 1) * width] = col_chunk(c, 0)
    u = field_ref[...]
    ur = u[:height]
    ui = u[height:]
    errors = ur * ur + ui * ui - inten_ref[...]
    field_ref[...] = jnp.concatenate([2.0 * errors * ur, 2.0 * errors * ui], axis=0)
    for c in range(CHUNKS):
        write_blocks(c, field_ref[:, c * width:(c + 1) * width])
    for c in range(CHUNKS):
        emit(layers, c, b_store.at[0], col_chunk(c, 1))

    def backward(j, carry):
        s = layers - 1 - j
        wave(layers + j, b_store.at[j], b_store.at[j + 1], lambda c, a: adjoint_chunk(s, c, a),
             lambda c: col_chunk(c, 1))
        return carry

    lax.fori_loop(0, layers - 1, backward, 0)
    last = 2 * layers - 1
    for c in range(CHUNKS):
        adjoint_chunk(0, c, halo(last, c, b_store.at[layers - 1]))
    finish(last, b_store.at[layers - 1])
    own = terms_ref[section]
    exchange = pltpu.make_async_remote_copy(
        src_ref=terms_ref.at[partner], dst_ref=partner_ref, send_sem=send_pair, recv_sem=recv_pair,
        device_id={"depth": partner}, device_id_type=MESH)
    exchange.start()
    exchange.wait_send()
    exchange.wait_recv()
    out_ref[0] = own + partner_ref[...]
    for step in range(1, sections):
        for one in gathers(step, section):
            one.wait_send()


def run_chain(u0, index_volume, offsets, intensity, rows, sections):
    _, height, columns = index_volume.shape
    layers = sections
    blocks = columns // LANE
    field = (2 * height, columns)
    off_tile = jnp.broadcast_to(offsets.astype(jnp.float32)[:, None], (8, LANE))
    plane = (layers, height, columns)
    return pl.pallas_call(
        functools.partial(chain_kernel, rows, sections),
        out_shape=jax.ShapeDtypeStruct((1, height, columns), jnp.float32),
        in_specs=[pl.BlockSpec(memory_space=pltpu.VMEM)] * 6,
        out_specs=pl.BlockSpec(memory_space=pltpu.VMEM),
        scratch_shapes=[
            pltpu.VMEM(plane, jnp.float32),
            pltpu.VMEM((height, columns), jnp.float32),
            pltpu.VMEM(field, jnp.float32),
            pltpu.VMEM((2,) + field, jnp.float32),
            pltpu.VMEM((layers,) + field, jnp.float32),
            pltpu.VMEM((layers,) + field, jnp.float32),
            pltpu.VMEM((2 * layers,) + field, jnp.float32),
            pltpu.VMEM((2 * layers,) + field, jnp.float32),
            pltpu.VMEM((blocks + 2, 2 * height, LANE), jnp.bfloat16),
            pltpu.VMEM((blocks + 2, 2 * height, LANE), jnp.bfloat16),
            pltpu.VMEM(plane, jnp.float32),
            pltpu.VMEM(plane, jnp.float32),
            pltpu.VMEM((2 * layers, 3 * 2 * height, 2 * height), jnp.float32),
            pltpu.VMEM(plane, index_volume.dtype),
            pltpu.VMEM((sections, 8, LANE), jnp.float32),
            pltpu.SemaphoreType.DMA((2 * layers * CHUNKS,)),
            pltpu.SemaphoreType.DMA((2 * layers * CHUNKS,)),
            pltpu.SemaphoreType.DMA((2 * layers * CHUNKS,)),
            pltpu.SemaphoreType.DMA((2 * layers * CHUNKS,)),
            pltpu.SemaphoreType.DMA,
            pltpu.SemaphoreType.DMA,
            pltpu.SemaphoreType.DMA((sections,)),
            pltpu.SemaphoreType.DMA((sections,)),
            pltpu.SemaphoreType.DMA((sections,)),
            pltpu.SemaphoreType.DMA((sections,)),
            pltpu.VMEM((2, 3, LANE, 2 * LANE), jnp.bfloat16),
            pltpu.VMEM((2, 3, LANE, 2 * LANE), jnp.bfloat16),
            pltpu.VMEM((2 * layers, 3 * 2 * height, 2 * height), jnp.bfloat16),
            pltpu.VMEM((2 * layers, 3 * 2 * height, 2 * height), jnp.bfloat16),
        ],
        compiler_params=pltpu.CompilerParams(
            collective_id=0, has_side_effects=True, vmem_limit_bytes=56 * 1024 * 1024),
    )(u0, index_volume, off_tile, intensity, band_table(height), column_bands())


def gather_kernel(sections, vol_ref, off_ref, vol_out, off_out, vol_slots, off_slots,
                  send_vol, send_off, recv_vol, recv_off, chb_ref, clb_ref, rbh_ref, rbl_ref):
    me = lax.axis_index("depth")
    barrier = pltpu.get_barrier_semaphore()
    for step in range(1, sections):
        peer = (me + step) % sections
        pl.semaphore_signal(barrier, 1, device_id={"depth": peer}, device_id_type=MESH)
    pl.semaphore_wait(barrier, sections - 1)

    def copies(step):
        peer = (me + step) % sections
        source = (me + sections - step) % sections
        out_vol = pltpu.make_async_remote_copy(
            src_ref=vol_ref.at[0], dst_ref=vol_slots.at[me], send_sem=send_vol.at[step],
            recv_sem=recv_vol.at[me], device_id={"depth": peer}, device_id_type=MESH)
        out_off = pltpu.make_async_remote_copy(
            src_ref=off_ref, dst_ref=off_slots.at[me], send_sem=send_off.at[step],
            recv_sem=recv_off.at[me], device_id={"depth": peer}, device_id_type=MESH)
        in_vol = pltpu.make_async_remote_copy(
            src_ref=vol_ref.at[0], dst_ref=vol_slots.at[source], send_sem=send_vol.at[step],
            recv_sem=recv_vol.at[source], device_id={"depth": peer}, device_id_type=MESH)
        in_off = pltpu.make_async_remote_copy(
            src_ref=off_ref, dst_ref=off_slots.at[source], send_sem=send_off.at[step],
            recv_sem=recv_off.at[source], device_id={"depth": peer}, device_id_type=MESH)
        return out_vol, out_off, in_vol, in_off

    for step in range(1, sections):
        out_vol, out_off, _, _ = copies(step)
        out_vol.start()
        out_off.start()
    vol_slots[me] = vol_ref[0]
    off_slots[me] = off_ref[...]
    for step in range(1, sections):
        out_vol, out_off, in_vol, in_off = copies(step)
        in_vol.wait_recv()
        in_off.wait_recv()
        out_vol.wait_send()
        out_off.wait_send()
    vol_out[...] = vol_slots[...]
    off_out[...] = off_slots[...]


def gather_depth(index_volume, offsets, sections):
    _, height, columns = index_volume.shape
    off_tile = jnp.broadcast_to(offsets.astype(jnp.float32)[:, None], (8, LANE))
    vol_shape = (sections, height, columns)
    off_shape = (sections, 8, LANE)
    return pl.pallas_call(
        functools.partial(gather_kernel, sections),
        out_shape=(jax.ShapeDtypeStruct(vol_shape, index_volume.dtype),
                   jax.ShapeDtypeStruct(off_shape, jnp.float32)),
        in_specs=[pl.BlockSpec(memory_space=pltpu.VMEM)] * 2,
        out_specs=(pl.BlockSpec(memory_space=pltpu.VMEM),) * 2,
        scratch_shapes=[
            pltpu.VMEM(vol_shape, index_volume.dtype),
            pltpu.VMEM(off_shape, jnp.float32),
            pltpu.SemaphoreType.DMA((sections,)),
            pltpu.SemaphoreType.DMA((sections,)),
            pltpu.SemaphoreType.DMA((sections,)),
            pltpu.SemaphoreType.DMA((sections,)),
            pltpu.VMEM((2, 3, LANE, 2 * LANE), jnp.bfloat16),
            pltpu.VMEM((2, 3, LANE, 2 * LANE), jnp.bfloat16),
            pltpu.VMEM((2 * layers, 3 * 2 * height, 2 * height), jnp.bfloat16),
            pltpu.VMEM((2 * layers, 3 * 2 * height, 2 * height), jnp.bfloat16),
        ],
        compiler_params=pltpu.CompilerParams(collective_id=1, has_side_effects=True),
    )(index_volume, off_tile)


def plane_wave(angle, row_start, height, columns, total_rows, total_cols):
    across = angle - TILTS // 2
    along = jnp.mod(3 * angle, TILTS) - TILTS // 2
    row_index = row_start + lax.broadcasted_iota(jnp.int32, (height, columns), 0)
    col_index = lax.broadcasted_iota(jnp.int32, (height, columns), 1)
    period = total_cols * total_rows
    cycles_int = jnp.mod(across * col_index * total_rows + along * row_index * total_cols, period)
    phase_arg = 2.0 * math.pi / period * cycles_int.astype(jnp.float32)
    return jnp.concatenate([jnp.cos(phase_arg), jnp.sin(phase_arg)], axis=0)


def body(index_volume, angles, offsets, measured):
    sections = lax.axis_size("depth")
    rows = lax.axis_size("row")
    section_no = lax.axis_index("depth")
    height = index_volume.shape[1]
    columns = index_volume.shape[2]
    row_start = lax.axis_index("row") * height
    total_rows = height * rows
    angle_count = angles.shape[0]
    angle_no = section_no % angle_count
    intensity = lax.dynamic_index_in_dim(measured, angle_no, 0, keepdims=False).astype(jnp.float32)
    angle = lax.dynamic_index_in_dim(angles, angle_no, 0, keepdims=False)
    incident = plane_wave(angle, row_start, height, columns, total_rows, columns)
    return run_chain(incident, index_volume, offsets, intensity, rows, sections)


def solution(mesh):
    in_specs = (P("depth", "row", None), P(), P("depth"), P(None, "row", None))
    out_specs = P("depth", "row", None)
    return jax.shard_map(body, mesh=mesh, in_specs=in_specs, out_specs=out_specs, check_vma=False)
```

```python
import functools
import math

import jax
import numpy as np
import jax.numpy as jnp
from jax import lax
from jax.experimental import pallas as pl
from jax.experimental.pallas import tpu as pltpu
from jax.sharding import PartitionSpec as P

TILTS = 16
HALF = 10
SHIFT = 4
HALFCOL = 64
LANE = 128

PHASE_SCALE = 0.5
CHIRP_ROW = 1.3
CHIRP_COL = 1.7
MESH = pl.DeviceIdType.MESH


def kernel_values(distance, radius, chirp_rate):
    inside = jnp.abs(distance) <= radius
    phase_arg = chirp_rate / radius * distance * distance
    weight = 1.0 / math.sqrt(2 * radius + 1)
    real_part = jnp.where(inside, jnp.cos(phase_arg) * weight, 0.0)
    imag_part = jnp.where(inside, jnp.sin(phase_arg) * weight, 0.0)
    return (real_part, imag_part)


def split_bf16(x):
    high = x.astype(jnp.bfloat16)
    low = (x - high.astype(jnp.float32)).astype(jnp.bfloat16)
    return high, low


def complex_block(real_part, imag_part):
    top = jnp.concatenate([real_part, -imag_part], axis=-1)
    bottom = jnp.concatenate([imag_part, real_part], axis=-1)
    return jnp.concatenate([top, bottom], axis=-2)


def band_table(height):
    offsets = np.arange(-SHIFT, SHIFT + 1)[:, None, None, None]
    part = np.arange(3)[None, :, None, None]
    target = np.arange(height)[None, None, :, None]
    source = np.arange(height)[None, None, None, :] + (part - 1) * height
    tables = []
    for sign in (1, -1):
        distance = (source - target - sign * offsets).astype(np.float64)
        inside = np.abs(distance) <= HALF
        phase_arg = CHIRP_ROW / HALF * distance * distance
        weight = 1.0 / math.sqrt(2 * HALF + 1)
        real_part = np.where(inside, np.cos(phase_arg) * weight, 0.0)
        imag_part = np.where(inside, np.sin(phase_arg) * weight, 0.0) * sign
        top = np.concatenate([real_part, -imag_part], axis=-1)
        bottom = np.concatenate([imag_part, real_part], axis=-1)
        block = np.concatenate([top, bottom], axis=-2)
        tables.append(block.reshape(2 * SHIFT + 1, 3 * 2 * height, 2 * height))
    return jnp.asarray(np.stack(tables, axis=0).astype(np.float32))


def column_bands():
    part = np.arange(3)[:, None, None]
    source = np.arange(LANE)[None, :, None] + (part - 1) * LANE
    target = np.arange(LANE)[None, None, :]
    distance = (source - target).astype(np.float64)
    inside = np.abs(distance) <= HALFCOL
    phase_arg = CHIRP_COL / HALFCOL * distance * distance
    weight = 1.0 / math.sqrt(2 * HALFCOL + 1)
    real_part = np.where(inside, np.cos(phase_arg) * weight, 0.0)
    imag_part = np.where(inside, np.sin(phase_arg) * weight, 0.0)
    forward = np.concatenate([real_part, imag_part], axis=-1)
    adjoint = np.concatenate([real_part, -imag_part], axis=-1)
    return jnp.asarray(np.stack([forward, adjoint], axis=0).astype(np.float32))


def dot3(a_high, a_low, x):
    x_high, x_low = split_bf16(x)
    f32 = jnp.float32
    rows = a_high.shape[0]
    both = jnp.dot(jnp.concatenate([a_high, a_low], axis=0), x_high, preferred_element_type=f32)
    return both[:rows] + both[rows:] + jnp.dot(a_high, x_low, preferred_element_type=f32)


CHUNKS = 4


def chain_kernel(rows, sections, u0_ref, vol_ref, off_ref, inten_ref, table_ref, cband_ref,
                 out_ref, terms_ref, partner_ref, field_ref, acc_ref, y_store, b_store, before, after,
                 bmh_ref, bml_ref, cos_ref, sin_ref, rband_ref, vol_slots, off_slots,
                 send_dn, send_up, recv_bf, recv_af, send_pair, recv_pair,
                 send_vol, send_off, recv_vol, recv_off, chb_ref, clb_ref, rbh_ref, rbl_ref):
    me = lax.axis_index("row")
    section = lax.axis_index("depth")
    partner = section + 1 - 2 * (section % 2)
    layers, height, columns = cos_ref.shape
    blocks = columns // LANE
    width = columns // CHUNKS
    per_chunk = blocks // CHUNKS
    has_up = me > 0
    has_dn = me < rows - 1

    barrier = pltpu.get_barrier_semaphore()

    @pl.when(has_up)
    def _():
        pl.semaphore_signal(barrier, 1, device_id={"row": me - 1}, device_id_type=MESH)

    @pl.when(has_dn)
    def _():
        pl.semaphore_signal(barrier, 1, device_id={"row": me + 1}, device_id_type=MESH)

    for step in range(1, sections):
        peer = (section + step) % sections
        pl.semaphore_signal(barrier, 1, device_id={"depth": peer}, device_id_type=MESH)
    peers = (me + rows - 1) // rows + (2 * rows - 2 - me) // rows
    pl.semaphore_wait(barrier, peers + sections - 1)

    def gathers(step, slot):
        peer = (section + step) % sections
        vol_copy = pltpu.make_async_remote_copy(
            src_ref=vol_ref.at[0], dst_ref=vol_slots.at[slot], send_sem=send_vol.at[step],
            recv_sem=recv_vol.at[slot], device_id={"depth": peer}, device_id_type=MESH)
        off_copy = pltpu.make_async_remote_copy(
            src_ref=off_ref, dst_ref=off_slots.at[slot], send_sem=send_off.at[step],
            recv_sem=recv_off.at[slot], device_id={"depth": peer}, device_id_type=MESH)
        return vol_copy, off_copy

    for step in range(1, sections):
        for one in gathers(step, section):
            one.start()
    vol_slots[section] = vol_ref[0]
    off_slots[section] = off_ref[...]
    part_rows = 2 * height

    def prepare(s):
        @pl.when(s != section)
        def _():
            for one in gathers(1, s):
                one.wait_recv()

        phase = PHASE_SCALE * vol_slots[s].astype(jnp.float32)
        cos_ref[s] = jnp.cos(phase)
        sin_ref[s] = jnp.sin(phase)
        shift = off_slots[s][0:1, 0:part_rows]
        forward_band = None
        adjoint_band = None
        for i in range(2 * SHIFT + 1):
            pick = jnp.where(shift == float(i - SHIFT), 1.0, 0.0)
            f_term = pick * table_ref[0, i]
            a_term = pick * table_ref[1, i]
            forward_band = f_term if forward_band is None else forward_band + f_term
            adjoint_band = a_term if adjoint_band is None else adjoint_band + a_term
        high, low = split_bf16(forward_band)
        rbh_ref[s] = high
        rbl_ref[s] = low
        high, low = split_bf16(adjoint_band)
        rbh_ref[2 * layers - 1 - s] = high
        rbl_ref[2 * layers - 1 - s] = low

    high, low = split_bf16(cband_ref[...])
    chb_ref[...] = high
    clb_ref[...] = low
    zero_block = jnp.zeros((2 * height, LANE), jnp.bfloat16)
    for ref in (bmh_ref, bml_ref):
        ref[0] = zero_block
        ref[blocks + 1] = zero_block

    def copies(k, c, store):
        cols = pl.ds(c * width, width)
        slot = k * CHUNKS + c
        down = pltpu.make_async_remote_copy(
            src_ref=store.at[:, cols], dst_ref=before.at[k, :, cols], send_sem=send_dn.at[slot],
            recv_sem=recv_bf.at[slot], device_id={"row": me + 1}, device_id_type=MESH)
        up = pltpu.make_async_remote_copy(
            src_ref=store.at[:, cols], dst_ref=after.at[k, :, cols], send_sem=send_up.at[slot],
            recv_sem=recv_af.at[slot], device_id={"row": me - 1}, device_id_type=MESH)
        return down, up

    def start(k, c, store):
        down, up = copies(k, c, store)

        @pl.when(has_dn)
        def _():
            down.start()

        @pl.when(has_up)
        def _():
            up.start()

    def finish(k, store):
        for c in range(CHUNKS):
            down, up = copies(k, c, store)

            @pl.when(has_dn)
            def _():
                down.wait_send()

            @pl.when(has_up)
            def _():
                up.wait_send()

    def halo(k, c, store):
        down, up = copies(k, c, store)
        cols = pl.ds(c * width, width)
        slot = k % 2

        @pl.when(has_up)
        def _():
            down.wait_recv()
            acc_ref[slot, :, cols] += dot3(rbh_ref[k, 0:part_rows], rbl_ref[k, 0:part_rows], before[k, :, cols])

        @pl.when(has_dn)
        def _():
            up.wait_recv()
            acc_ref[slot, :, cols] += dot3(rbh_ref[k, 2 * part_rows:3 * part_rows], rbl_ref[k, 2 * part_rows:3 * part_rows], after[k, :, cols])

        return acc_ref[slot, :, cols]

    def emit(k, c, store, value):
        cols = pl.ds(c * width, width)
        store[:, cols] = value
        acc_ref[k % 2, :, cols] = dot3(rbh_ref[k, part_rows:2 * part_rows], rbl_ref[k, part_rows:2 * part_rows], store[:, cols])
        start(k, c, store)

    def write_blocks(c, x):
        high, low = split_bf16(x)
        for b in range(per_chunk):
            bmh_ref[c * per_chunk + b + 1] = high[:, b * LANE:(b + 1) * LANE]
            bml_ref[c * per_chunk + b + 1] = low[:, b * LANE:(b + 1) * LANE]

    def wave(k, store, store_next, finish_chunk, make_chunk):
        for c in range(CHUNKS):
            write_blocks(c, finish_chunk(c, halo(k, c, store)))
            if c >= 1:
                emit(k + 1, c - 1, store_next, make_chunk(c - 1))
        emit(k + 1, CHUNKS - 1, store_next, make_chunk(CHUNKS - 1))
        finish(k, store)

    def col_chunk(c, which):
        total = None
        f32 = jnp.float32
        first = c * per_chunk
        for t in range(3):
            xh = bmh_ref[first + t:first + t + per_chunk].reshape(per_chunk * 2 * height, LANE)
            xl = bml_ref[first + t:first + t + per_chunk].reshape(per_chunk * 2 * height, LANE)
            wh = chb_ref[which, t]
            wl = clb_ref[which, t]
            count = xh.shape[0]
            both = jnp.dot(jnp.concatenate([xh, xl], axis=0), wh, preferred_element_type=f32)
            part = both[:count] + both[count:] + jnp.dot(xh, wl, preferred_element_type=f32)
            total = part if total is None else total + part
        total = total.reshape(per_chunk, 2 * height, 2 * LANE)
        real_part = total[:, :height, :LANE] - total[:, height:, LANE:]
        imag_part = total[:, :height, LANE:] + total[:, height:, :LANE]
        out = jnp.concatenate([real_part, imag_part], axis=1)
        return jnp.concatenate([out[b] for b in range(per_chunk)], axis=1)

    def rotated(s, c, u):
        cols = pl.ds(c * width, width)
        cs = cos_ref[s, :, cols]
        sn = sin_ref[s, :, cols]
        ur = u[:height]
        ui = u[height:]
        return jnp.concatenate([cs * ur - sn * ui, cs * ui + sn * ur], axis=0)

    def adjoint_chunk(s, c, a):
        cols = pl.ds(c * width, width)
        ar = a[:height]
        ai = a[height:]
        y = y_store[s, :, cols]
        terms_ref[s, :, cols] = PHASE_SCALE * (y[:height] * ai - y[height:] * ar)
        cs = cos_ref[s, :, cols]
        sn = sin_ref[s, :, cols]
        return jnp.concatenate([cs * ar + sn * ai, cs * ai - sn * ar], axis=0)

    prepare(0)
    for c in range(CHUNKS):
        emit(0, c, y_store.at[0], rotated(0, c, u0_ref[:, c * width:(c + 1) * width]))

    def forward(k, carry):
        prepare(k + 1)
        wave(k, y_store.at[k], y_store.at[k + 1], lambda c, a: a,
             lambda c: rotated(k + 1, c, col_chunk(c, 0)))
        return carry

    lax.fori_loop(0, layers - 1, forward, 0)
    for c in range(CHUNKS):
        write_blocks(c, halo(layers - 1, c, y_store.at[layers - 1]))
    finish(layers - 1, y_store.at[layers - 1])
    for c in range(CHUNKS):
        field_ref[:, c * width:(c + 1) * width] = col_chunk(c, 0)
    u = field_ref[...]
    ur = u[:height]
    ui = u[height:]
    errors = ur * ur + ui * ui - inten_ref[section % inten_ref.shape[0]].astype(jnp.float32)
    field_ref[...] = jnp.concatenate([2.0 * errors * ur, 2.0 * errors * ui], axis=0)
    for c in range(CHUNKS):
        write_blocks(c, field_ref[:, c * width:(c + 1) * width])
    for c in range(CHUNKS):
        emit(layers, c, b_store.at[0], col_chunk(c, 1))

    def backward(j, carry):
        s = layers - 1 - j
        wave(layers + j, b_store.at[j], b_store.at[j + 1], lambda c, a: adjoint_chunk(s, c, a),
             lambda c: col_chunk(c, 1))
        return carry

    lax.fori_loop(0, layers - 1, backward, 0)
    last = 2 * layers - 1
    for c in range(CHUNKS):
        adjoint_chunk(0, c, halo(last, c, b_store.at[layers - 1]))
    finish(last, b_store.at[layers - 1])
    own = terms_ref[section]
    exchange = pltpu.make_async_remote_copy(
        src_ref=terms_ref.at[partner], dst_ref=partner_ref, send_sem=send_pair, recv_sem=recv_pair,
        device_id={"depth": partner}, device_id_type=MESH)
    exchange.start()
    exchange.wait_send()
    exchange.wait_recv()
    out_ref[0] = own + partner_ref[...]
    for step in range(1, sections):
        for one in gathers(step, section):
            one.wait_send()


def run_chain(u0, index_volume, offsets, intensity, rows, sections):
    _, height, columns = index_volume.shape
    layers = sections
    blocks = columns // LANE
    field = (2 * height, columns)
    off_tile = jnp.broadcast_to(offsets.astype(jnp.float32)[:, None], (8, LANE))
    plane = (layers, height, columns)
    return pl.pallas_call(
        functools.partial(chain_kernel, rows, sections),
        out_shape=jax.ShapeDtypeStruct((1, height, columns), jnp.float32),
        in_specs=[pl.BlockSpec(memory_space=pltpu.VMEM)] * 6,
        out_specs=pl.BlockSpec(memory_space=pltpu.VMEM),
        scratch_shapes=[
            pltpu.VMEM(plane, jnp.float32),
            pltpu.VMEM((height, columns), jnp.float32),
            pltpu.VMEM(field, jnp.float32),
            pltpu.VMEM((2,) + field, jnp.float32),
            pltpu.VMEM((layers,) + field, jnp.float32),
            pltpu.VMEM((layers,) + field, jnp.float32),
            pltpu.VMEM((2 * layers,) + field, jnp.float32),
            pltpu.VMEM((2 * layers,) + field, jnp.float32),
            pltpu.VMEM((blocks + 2, 2 * height, LANE), jnp.bfloat16),
            pltpu.VMEM((blocks + 2, 2 * height, LANE), jnp.bfloat16),
            pltpu.VMEM(plane, jnp.float32),
            pltpu.VMEM(plane, jnp.float32),
            pltpu.VMEM((2 * layers, 3 * 2 * height, 2 * height), jnp.float32),
            pltpu.VMEM(plane, index_volume.dtype),
            pltpu.VMEM((sections, 8, LANE), jnp.float32),
            pltpu.SemaphoreType.DMA((2 * layers * CHUNKS,)),
            pltpu.SemaphoreType.DMA((2 * layers * CHUNKS,)),
            pltpu.SemaphoreType.DMA((2 * layers * CHUNKS,)),
            pltpu.SemaphoreType.DMA((2 * layers * CHUNKS,)),
            pltpu.SemaphoreType.DMA,
            pltpu.SemaphoreType.DMA,
            pltpu.SemaphoreType.DMA((sections,)),
            pltpu.SemaphoreType.DMA((sections,)),
            pltpu.SemaphoreType.DMA((sections,)),
            pltpu.SemaphoreType.DMA((sections,)),
            pltpu.VMEM((2, 3, LANE, 2 * LANE), jnp.bfloat16),
            pltpu.VMEM((2, 3, LANE, 2 * LANE), jnp.bfloat16),
            pltpu.VMEM((2 * layers, 3 * 2 * height, 2 * height), jnp.bfloat16),
            pltpu.VMEM((2 * layers, 3 * 2 * height, 2 * height), jnp.bfloat16),
        ],
        compiler_params=pltpu.CompilerParams(
            collective_id=0, has_side_effects=True, vmem_limit_bytes=56 * 1024 * 1024),
    )(u0, index_volume, off_tile, intensity, band_table(height), column_bands())


def gather_kernel(sections, vol_ref, off_ref, vol_out, off_out, vol_slots, off_slots,
                  send_vol, send_off, recv_vol, recv_off, chb_ref, clb_ref, rbh_ref, rbl_ref):
    me = lax.axis_index("depth")
    barrier = pltpu.get_barrier_semaphore()
    for step in range(1, sections):
        peer = (me + step) % sections
        pl.semaphore_signal(barrier, 1, device_id={"depth": peer}, device_id_type=MESH)
    pl.semaphore_wait(barrier, sections - 1)

    def copies(step):
        peer = (me + step) % sections
        source = (me + sections - step) % sections
        out_vol = pltpu.make_async_remote_copy(
            src_ref=vol_ref.at[0], dst_ref=vol_slots.at[me], send_sem=send_vol.at[step],
            recv_sem=recv_vol.at[me], device_id={"depth": peer}, device_id_type=MESH)
        out_off = pltpu.make_async_remote_copy(
            src_ref=off_ref, dst_ref=off_slots.at[me], send_sem=send_off.at[step],
            recv_sem=recv_off.at[me], device_id={"depth": peer}, device_id_type=MESH)
        in_vol = pltpu.make_async_remote_copy(
            src_ref=vol_ref.at[0], dst_ref=vol_slots.at[source], send_sem=send_vol.at[step],
            recv_sem=recv_vol.at[source], device_id={"depth": peer}, device_id_type=MESH)
        in_off = pltpu.make_async_remote_copy(
            src_ref=off_ref, dst_ref=off_slots.at[source], send_sem=send_off.at[step],
            recv_sem=recv_off.at[source], device_id={"depth": peer}, device_id_type=MESH)
        return out_vol, out_off, in_vol, in_off

    for step in range(1, sections):
        out_vol, out_off, _, _ = copies(step)
        out_vol.start()
        out_off.start()
    vol_slots[me] = vol_ref[0]
    off_slots[me] = off_ref[...]
    for step in range(1, sections):
        out_vol, out_off, in_vol, in_off = copies(step)
        in_vol.wait_recv()
        in_off.wait_recv()
        out_vol.wait_send()
        out_off.wait_send()
    vol_out[...] = vol_slots[...]
    off_out[...] = off_slots[...]


def gather_depth(index_volume, offsets, sections):
    _, height, columns = index_volume.shape
    off_tile = jnp.broadcast_to(offsets.astype(jnp.float32)[:, None], (8, LANE))
    vol_shape = (sections, height, columns)
    off_shape = (sections, 8, LANE)
    return pl.pallas_call(
        functools.partial(gather_kernel, sections),
        out_shape=(jax.ShapeDtypeStruct(vol_shape, index_volume.dtype),
                   jax.ShapeDtypeStruct(off_shape, jnp.float32)),
        in_specs=[pl.BlockSpec(memory_space=pltpu.VMEM)] * 2,
        out_specs=(pl.BlockSpec(memory_space=pltpu.VMEM),) * 2,
        scratch_shapes=[
            pltpu.VMEM(vol_shape, index_volume.dtype),
            pltpu.VMEM(off_shape, jnp.float32),
            pltpu.SemaphoreType.DMA((sections,)),
            pltpu.SemaphoreType.DMA((sections,)),
            pltpu.SemaphoreType.DMA((sections,)),
            pltpu.SemaphoreType.DMA((sections,)),
            pltpu.VMEM((2, 3, LANE, 2 * LANE), jnp.bfloat16),
            pltpu.VMEM((2, 3, LANE, 2 * LANE), jnp.bfloat16),
            pltpu.VMEM((2 * layers, 3 * 2 * height, 2 * height), jnp.bfloat16),
            pltpu.VMEM((2 * layers, 3 * 2 * height, 2 * height), jnp.bfloat16),
        ],
        compiler_params=pltpu.CompilerParams(collective_id=1, has_side_effects=True),
    )(index_volume, off_tile)


def plane_wave(angle, row_start, height, columns, total_rows, total_cols):
    across = angle - TILTS // 2
    along = jnp.mod(3 * angle, TILTS) - TILTS // 2
    row_index = row_start + lax.broadcasted_iota(jnp.int32, (height, columns), 0)
    col_index = lax.broadcasted_iota(jnp.int32, (height, columns), 1)
    period = total_cols * total_rows
    cycles_int = jnp.mod(across * col_index * total_rows + along * row_index * total_cols, period)
    phase_arg = 2.0 * math.pi / period * cycles_int.astype(jnp.float32)
    return jnp.concatenate([jnp.cos(phase_arg), jnp.sin(phase_arg)], axis=0)


def body(index_volume, angles, offsets, measured):
    sections = lax.axis_size("depth")
    rows = lax.axis_size("row")
    section_no = lax.axis_index("depth")
    height = index_volume.shape[1]
    columns = index_volume.shape[2]
    row_start = lax.axis_index("row") * height
    total_rows = height * rows
    angle_count = angles.shape[0]
    angle_no = section_no % angle_count
    angle = lax.dynamic_index_in_dim(angles, angle_no, 0, keepdims=False)
    incident = plane_wave(angle, row_start, height, columns, total_rows, columns)
    return run_chain(incident, index_volume, offsets, measured, rows, sections)


def solution(mesh):
    in_specs = (P("depth", "row", None), P(), P("depth"), P(None, "row", None))
    out_specs = P("depth", "row", None)
    return jax.shard_map(body, mesh=mesh, in_specs=in_specs, out_specs=out_specs, check_vma=False)
```

```python
import functools
import math

import jax
import numpy as np
import jax.numpy as jnp
from jax import lax
from jax.experimental import pallas as pl
from jax.experimental.pallas import tpu as pltpu
from jax.sharding import PartitionSpec as P

TILTS = 16
HALF = 10
SHIFT = 4
HALFCOL = 64
LANE = 128

PHASE_SCALE = 0.5
CHIRP_ROW = 1.3
CHIRP_COL = 1.7
MESH = pl.DeviceIdType.MESH


def kernel_values(distance, radius, chirp_rate):
    inside = jnp.abs(distance) <= radius
    phase_arg = chirp_rate / radius * distance * distance
    weight = 1.0 / math.sqrt(2 * radius + 1)
    real_part = jnp.where(inside, jnp.cos(phase_arg) * weight, 0.0)
    imag_part = jnp.where(inside, jnp.sin(phase_arg) * weight, 0.0)
    return (real_part, imag_part)


def split_bf16(x):
    high = x.astype(jnp.bfloat16)
    low = (x - high.astype(jnp.float32)).astype(jnp.bfloat16)
    return high, low


def complex_block(real_part, imag_part):
    top = jnp.concatenate([real_part, -imag_part], axis=-1)
    bottom = jnp.concatenate([imag_part, real_part], axis=-1)
    return jnp.concatenate([top, bottom], axis=-2)


def band_table(height):
    offsets = np.arange(-SHIFT, SHIFT + 1)[:, None, None, None]
    part = np.arange(3)[None, :, None, None]
    target = np.arange(height)[None, None, :, None]
    source = np.arange(height)[None, None, None, :] + (part - 1) * height
    tables = []
    for sign in (1, -1):
        distance = (source - target - sign * offsets).astype(np.float64)
        inside = np.abs(distance) <= HALF
        phase_arg = CHIRP_ROW / HALF * distance * distance
        weight = 1.0 / math.sqrt(2 * HALF + 1)
        real_part = np.where(inside, np.cos(phase_arg) * weight, 0.0)
        imag_part = np.where(inside, np.sin(phase_arg) * weight, 0.0) * sign
        top = np.concatenate([real_part, -imag_part], axis=-1)
        bottom = np.concatenate([imag_part, real_part], axis=-1)
        block = np.concatenate([top, bottom], axis=-2)
        tables.append(block.reshape(2 * SHIFT + 1, 3 * 2 * height, 2 * height))
    return jnp.asarray(np.stack(tables, axis=0).astype(np.float32))


def column_bands():
    part = np.arange(3)[:, None, None]
    source = np.arange(LANE)[None, :, None] + (part - 1) * LANE
    target = np.arange(LANE)[None, None, :]
    distance = (source - target).astype(np.float64)
    inside = np.abs(distance) <= HALFCOL
    phase_arg = CHIRP_COL / HALFCOL * distance * distance
    weight = 1.0 / math.sqrt(2 * HALFCOL + 1)
    real_part = np.where(inside, np.cos(phase_arg) * weight, 0.0)
    imag_part = np.where(inside, np.sin(phase_arg) * weight, 0.0)
    forward = np.concatenate([real_part, imag_part], axis=-1)
    adjoint = np.concatenate([real_part, -imag_part], axis=-1)
    return jnp.asarray(np.stack([forward, adjoint], axis=0).astype(np.float32))


def dot3(a_high, a_low, x):
    x_high, x_low = split_bf16(x)
    f32 = jnp.float32
    rows = a_high.shape[0]
    both = jnp.dot(jnp.concatenate([a_high, a_low], axis=0), x_high, preferred_element_type=f32)
    return both[:rows] + both[rows:] + jnp.dot(a_high, x_low, preferred_element_type=f32)


CHUNKS = 4


def chain_kernel(rows, sections, u0_ref, vol_ref, off_ref, inten_ref, table_ref, cband_ref,
                 out_ref, terms_ref, partner_ref, field_ref, acc_ref, y_store, b_store, before, after,
                 bmh_ref, bml_ref, cos_ref, sin_ref, rband_ref, vol_slots, off_slots,
                 send_dn, send_up, recv_bf, recv_af, send_pair, recv_pair,
                 send_vol, send_off, recv_vol, recv_off, chb_ref, clb_ref, rbh_ref, rbl_ref, own_off):
    me = lax.axis_index("row")
    section = lax.axis_index("depth")
    partner = section + 1 - 2 * (section % 2)
    layers, height, columns = cos_ref.shape
    blocks = columns // LANE
    width = columns // CHUNKS
    per_chunk = blocks // CHUNKS
    has_up = me > 0
    has_dn = me < rows - 1

    own_off[...] = jnp.full(own_off.shape, off_ref[0].astype(jnp.float32), jnp.float32)
    barrier = pltpu.get_barrier_semaphore()

    @pl.when(has_up)
    def _():
        pl.semaphore_signal(barrier, 1, device_id={"row": me - 1}, device_id_type=MESH)

    @pl.when(has_dn)
    def _():
        pl.semaphore_signal(barrier, 1, device_id={"row": me + 1}, device_id_type=MESH)

    for step in range(1, sections):
        peer = (section + step) % sections
        pl.semaphore_signal(barrier, 1, device_id={"depth": peer}, device_id_type=MESH)
    peers = (me + rows - 1) // rows + (2 * rows - 2 - me) // rows
    pl.semaphore_wait(barrier, peers + sections - 1)

    def gathers(step, slot):
        peer = (section + step) % sections
        vol_copy = pltpu.make_async_remote_copy(
            src_ref=vol_ref.at[0], dst_ref=vol_slots.at[slot], send_sem=send_vol.at[step],
            recv_sem=recv_vol.at[slot], device_id={"depth": peer}, device_id_type=MESH)
        off_copy = pltpu.make_async_remote_copy(
            src_ref=own_off, dst_ref=off_slots.at[slot], send_sem=send_off.at[step],
            recv_sem=recv_off.at[slot], device_id={"depth": peer}, device_id_type=MESH)
        return vol_copy, off_copy

    for step in range(1, sections):
        for one in gathers(step, section):
            one.start()
    vol_slots[section] = vol_ref[0]
    off_slots[section] = own_off[...]
    part_rows = 2 * height

    def prepare(s):
        @pl.when(s != section)
        def _():
            for one in gathers(1, s):
                one.wait_recv()

        phase = PHASE_SCALE * vol_slots[s].astype(jnp.float32)
        cos_ref[s] = jnp.cos(phase)
        sin_ref[s] = jnp.sin(phase)
        shift = off_slots[s][0:1, 0:part_rows]
        forward_band = None
        adjoint_band = None
        for i in range(2 * SHIFT + 1):
            pick = jnp.where(shift == float(i - SHIFT), 1.0, 0.0)
            f_term = pick * table_ref[0, i]
            a_term = pick * table_ref[1, i]
            forward_band = f_term if forward_band is None else forward_band + f_term
            adjoint_band = a_term if adjoint_band is None else adjoint_band + a_term
        high, low = split_bf16(forward_band)
        rbh_ref[s] = high
        rbl_ref[s] = low
        high, low = split_bf16(adjoint_band)
        rbh_ref[2 * layers - 1 - s] = high
        rbl_ref[2 * layers - 1 - s] = low

    high, low = split_bf16(cband_ref[...])
    chb_ref[...] = high
    clb_ref[...] = low
    zero_block = jnp.zeros((2 * height, LANE), jnp.bfloat16)
    for ref in (bmh_ref, bml_ref):
        ref[0] = zero_block
        ref[blocks + 1] = zero_block

    def copies(k, c, store):
        cols = pl.ds(c * width, width)
        slot = k * CHUNKS + c
        down = pltpu.make_async_remote_copy(
            src_ref=store.at[:, cols], dst_ref=before.at[k, :, cols], send_sem=send_dn.at[slot],
            recv_sem=recv_bf.at[slot], device_id={"row": me + 1}, device_id_type=MESH)
        up = pltpu.make_async_remote_copy(
            src_ref=store.at[:, cols], dst_ref=after.at[k, :, cols], send_sem=send_up.at[slot],
            recv_sem=recv_af.at[slot], device_id={"row": me - 1}, device_id_type=MESH)
        return down, up

    def start(k, c, store):
        down, up = copies(k, c, store)

        @pl.when(has_dn)
        def _():
            down.start()

        @pl.when(has_up)
        def _():
            up.start()

    def finish(k, store):
        for c in range(CHUNKS):
            down, up = copies(k, c, store)

            @pl.when(has_dn)
            def _():
                down.wait_send()

            @pl.when(has_up)
            def _():
                up.wait_send()

    def halo(k, c, store):
        down, up = copies(k, c, store)
        cols = pl.ds(c * width, width)
        slot = k % 2

        @pl.when(has_up)
        def _():
            down.wait_recv()
            acc_ref[slot, :, cols] += dot3(rbh_ref[k, 0:part_rows], rbl_ref[k, 0:part_rows], before[k, :, cols])

        @pl.when(has_dn)
        def _():
            up.wait_recv()
            acc_ref[slot, :, cols] += dot3(rbh_ref[k, 2 * part_rows:3 * part_rows], rbl_ref[k, 2 * part_rows:3 * part_rows], after[k, :, cols])

        return acc_ref[slot, :, cols]

    def emit(k, c, store, value):
        cols = pl.ds(c * width, width)
        store[:, cols] = value
        acc_ref[k % 2, :, cols] = dot3(rbh_ref[k, part_rows:2 * part_rows], rbl_ref[k, part_rows:2 * part_rows], store[:, cols])
        start(k, c, store)

    def write_blocks(c, x):
        high, low = split_bf16(x)
        for b in range(per_chunk):
            bmh_ref[c * per_chunk + b + 1] = high[:, b * LANE:(b + 1) * LANE]
            bml_ref[c * per_chunk + b + 1] = low[:, b * LANE:(b + 1) * LANE]

    def wave(k, store, store_next, finish_chunk, make_chunk):
        for c in range(CHUNKS):
            write_blocks(c, finish_chunk(c, halo(k, c, store)))
            if c >= 1:
                emit(k + 1, c - 1, store_next, make_chunk(c - 1))
        emit(k + 1, CHUNKS - 1, store_next, make_chunk(CHUNKS - 1))
        finish(k, store)

    def col_chunk(c, which):
        total = None
        f32 = jnp.float32
        first = c * per_chunk
        for t in range(3):
            xh = bmh_ref[first + t:first + t + per_chunk].reshape(per_chunk * 2 * height, LANE)
            xl = bml_ref[first + t:first + t + per_chunk].reshape(per_chunk * 2 * height, LANE)
            wh = chb_ref[which, t]
            wl = clb_ref[which, t]
            count = xh.shape[0]
            both = jnp.dot(jnp.concatenate([xh, xl], axis=0), wh, preferred_element_type=f32)
            part = both[:count] + both[count:] + jnp.dot(xh, wl, preferred_element_type=f32)
            total = part if total is None else total + part
        total = total.reshape(per_chunk, 2 * height, 2 * LANE)
        real_part = total[:, :height, :LANE] - total[:, height:, LANE:]
        imag_part = total[:, :height, LANE:] + total[:, height:, :LANE]
        out = jnp.concatenate([real_part, imag_part], axis=1)
        return jnp.concatenate([out[b] for b in range(per_chunk)], axis=1)

    def rotated(s, c, u):
        cols = pl.ds(c * width, width)
        cs = cos_ref[s, :, cols]
        sn = sin_ref[s, :, cols]
        ur = u[:height]
        ui = u[height:]
        return jnp.concatenate([cs * ur - sn * ui, cs * ui + sn * ur], axis=0)

    def adjoint_chunk(s, c, a):
        cols = pl.ds(c * width, width)
        ar = a[:height]
        ai = a[height:]
        y = y_store[s, :, cols]
        terms_ref[s, :, cols] = PHASE_SCALE * (y[:height] * ai - y[height:] * ar)
        cs = cos_ref[s, :, cols]
        sn = sin_ref[s, :, cols]
        return jnp.concatenate([cs * ar + sn * ai, cs * ai - sn * ar], axis=0)

    prepare(0)
    for c in range(CHUNKS):
        emit(0, c, y_store.at[0], rotated(0, c, u0_ref[:, c * width:(c + 1) * width]))

    def forward(k, carry):
        prepare(k + 1)
        wave(k, y_store.at[k], y_store.at[k + 1], lambda c, a: a,
             lambda c: rotated(k + 1, c, col_chunk(c, 0)))
        return carry

    lax.fori_loop(0, layers - 1, forward, 0)
    for c in range(CHUNKS):
        write_blocks(c, halo(layers - 1, c, y_store.at[layers - 1]))
    finish(layers - 1, y_store.at[layers - 1])
    for c in range(CHUNKS):
        field_ref[:, c * width:(c + 1) * width] = col_chunk(c, 0)
    u = field_ref[...]
    ur = u[:height]
    ui = u[height:]
    errors = ur * ur + ui * ui - inten_ref[section % inten_ref.shape[0]].astype(jnp.float32)
    field_ref[...] = jnp.concatenate([2.0 * errors * ur, 2.0 * errors * ui], axis=0)
    for c in range(CHUNKS):
        write_blocks(c, field_ref[:, c * width:(c + 1) * width])
    for c in range(CHUNKS):
        emit(layers, c, b_store.at[0], col_chunk(c, 1))

    def backward(j, carry):
        s = layers - 1 - j
        wave(layers + j, b_store.at[j], b_store.at[j + 1], lambda c, a: adjoint_chunk(s, c, a),
             lambda c: col_chunk(c, 1))
        return carry

    lax.fori_loop(0, layers - 1, backward, 0)
    last = 2 * layers - 1
    for c in range(CHUNKS):
        adjoint_chunk(0, c, halo(last, c, b_store.at[layers - 1]))
    finish(last, b_store.at[layers - 1])
    own = terms_ref[section]
    exchange = pltpu.make_async_remote_copy(
        src_ref=terms_ref.at[partner], dst_ref=partner_ref, send_sem=send_pair, recv_sem=recv_pair,
        device_id={"depth": partner}, device_id_type=MESH)
    exchange.start()
    exchange.wait_send()
    exchange.wait_recv()
    out_ref[0] = own + partner_ref[...]
    for step in range(1, sections):
        for one in gathers(step, section):
            one.wait_send()


def run_chain(u0, index_volume, offsets, intensity, rows, sections):
    _, height, columns = index_volume.shape
    layers = sections
    blocks = columns // LANE
    field = (2 * height, columns)
    plane = (layers, height, columns)
    return pl.pallas_call(
        functools.partial(chain_kernel, rows, sections),
        out_shape=jax.ShapeDtypeStruct((1, height, columns), jnp.float32),
        in_specs=[pl.BlockSpec(memory_space=pltpu.VMEM)] * 2 + [pl.BlockSpec(memory_space=pltpu.SMEM)]
        + [pl.BlockSpec(memory_space=pltpu.VMEM)] * 3,
        out_specs=pl.BlockSpec(memory_space=pltpu.VMEM),
        scratch_shapes=[
            pltpu.VMEM(plane, jnp.float32),
            pltpu.VMEM((height, columns), jnp.float32),
            pltpu.VMEM(field, jnp.float32),
            pltpu.VMEM((2,) + field, jnp.float32),
            pltpu.VMEM((layers,) + field, jnp.float32),
            pltpu.VMEM((layers,) + field, jnp.float32),
            pltpu.VMEM((2 * layers,) + field, jnp.float32),
            pltpu.VMEM((2 * layers,) + field, jnp.float32),
            pltpu.VMEM((blocks + 2, 2 * height, LANE), jnp.bfloat16),
            pltpu.VMEM((blocks + 2, 2 * height, LANE), jnp.bfloat16),
            pltpu.VMEM(plane, jnp.float32),
            pltpu.VMEM(plane, jnp.float32),
            pltpu.VMEM((2 * layers, 3 * 2 * height, 2 * height), jnp.float32),
            pltpu.VMEM(plane, index_volume.dtype),
            pltpu.VMEM((sections, 8, LANE), jnp.float32),
            pltpu.SemaphoreType.DMA((2 * layers * CHUNKS,)),
            pltpu.SemaphoreType.DMA((2 * layers * CHUNKS,)),
            pltpu.SemaphoreType.DMA((2 * layers * CHUNKS,)),
            pltpu.SemaphoreType.DMA((2 * layers * CHUNKS,)),
            pltpu.SemaphoreType.DMA,
            pltpu.SemaphoreType.DMA,
            pltpu.SemaphoreType.DMA((sections,)),
            pltpu.SemaphoreType.DMA((sections,)),
            pltpu.SemaphoreType.DMA((sections,)),
            pltpu.SemaphoreType.DMA((sections,)),
            pltpu.VMEM((2, 3, LANE, 2 * LANE), jnp.bfloat16),
            pltpu.VMEM((2, 3, LANE, 2 * LANE), jnp.bfloat16),
            pltpu.VMEM((2 * layers, 3 * 2 * height, 2 * height), jnp.bfloat16),
            pltpu.VMEM((2 * layers, 3 * 2 * height, 2 * height), jnp.bfloat16),
            pltpu.VMEM((8, LANE), jnp.float32),
        ],
        compiler_params=pltpu.CompilerParams(
            collective_id=0, has_side_effects=True, vmem_limit_bytes=56 * 1024 * 1024),
    )(u0, index_volume, offsets, intensity, band_table(height), column_bands())


def plane_wave(angle, row_start, height, columns, total_rows, total_cols):
    across = angle - TILTS // 2
    along = jnp.mod(3 * angle, TILTS) - TILTS // 2
    row_index = row_start + lax.broadcasted_iota(jnp.int32, (height, columns), 0)
    col_index = lax.broadcasted_iota(jnp.int32, (height, columns), 1)
    period = total_cols * total_rows
    cycles_int = jnp.mod(across * col_index * total_rows + along * row_index * total_cols, period)
    phase_arg = 2.0 * math.pi / period * cycles_int.astype(jnp.float32)
    return jnp.concatenate([jnp.cos(phase_arg), jnp.sin(phase_arg)], axis=0)


def body(index_volume, angles, offsets, measured):
    sections = lax.axis_size("depth")
    rows = lax.axis_size("row")
    section_no = lax.axis_index("depth")
    height = index_volume.shape[1]
    columns = index_volume.shape[2]
    row_start = lax.axis_index("row") * height
    total_rows = height * rows
    angle_count = angles.shape[0]
    angle_no = section_no % angle_count
    angle = lax.dynamic_index_in_dim(angles, angle_no, 0, keepdims=False)
    incident = plane_wave(angle, row_start, height, columns, total_rows, columns)
    return run_chain(incident, index_volume, offsets, measured, rows, sections)


def solution(mesh):
    in_specs = (P("depth", "row", None), P(), P("depth"), P(None, "row", None))
    out_specs = P("depth", "row", None)
    return jax.shard_map(body, mesh=mesh, in_specs=in_specs, out_specs=out_specs, check_vma=False)
```

```python
import functools
import math

import jax
import numpy as np
import jax.numpy as jnp
from jax import lax
from jax.experimental import pallas as pl
from jax.experimental.pallas import tpu as pltpu
from jax.sharding import PartitionSpec as P

TILTS = 16
HALF = 10
SHIFT = 4
HALFCOL = 64
LANE = 128

PHASE_SCALE = 0.5
CHIRP_ROW = 1.3
CHIRP_COL = 1.7
MESH = pl.DeviceIdType.MESH


def kernel_values(distance, radius, chirp_rate):
    inside = jnp.abs(distance) <= radius
    phase_arg = chirp_rate / radius * distance * distance
    weight = 1.0 / math.sqrt(2 * radius + 1)
    real_part = jnp.where(inside, jnp.cos(phase_arg) * weight, 0.0)
    imag_part = jnp.where(inside, jnp.sin(phase_arg) * weight, 0.0)
    return (real_part, imag_part)


def split_bf16(x):
    high = x.astype(jnp.bfloat16)
    low = (x - high.astype(jnp.float32)).astype(jnp.bfloat16)
    return high, low


def complex_block(real_part, imag_part):
    top = jnp.concatenate([real_part, -imag_part], axis=-1)
    bottom = jnp.concatenate([imag_part, real_part], axis=-1)
    return jnp.concatenate([top, bottom], axis=-2)


def band_table(height):
    offsets = np.arange(-SHIFT, SHIFT + 1)[:, None, None, None]
    part = np.arange(3)[None, :, None, None]
    target = np.arange(height)[None, None, :, None]
    source = np.arange(height)[None, None, None, :] + (part - 1) * height
    tables = []
    for sign in (1, -1):
        distance = (source - target - sign * offsets).astype(np.float64)
        inside = np.abs(distance) <= HALF
        phase_arg = CHIRP_ROW / HALF * distance * distance
        weight = 1.0 / math.sqrt(2 * HALF + 1)
        real_part = np.where(inside, np.cos(phase_arg) * weight, 0.0)
        imag_part = np.where(inside, np.sin(phase_arg) * weight, 0.0) * sign
        top = np.concatenate([real_part, -imag_part], axis=-1)
        bottom = np.concatenate([imag_part, real_part], axis=-1)
        block = np.concatenate([top, bottom], axis=-2)
        tables.append(block.reshape(2 * SHIFT + 1, 3 * 2 * height, 2 * height))
    return jnp.asarray(np.stack(tables, axis=0).astype(np.float32))


def column_bands():
    part = np.arange(3)[:, None, None]
    source = np.arange(LANE)[None, :, None] + (part - 1) * LANE
    target = np.arange(LANE)[None, None, :]
    distance = (source - target).astype(np.float64)
    inside = np.abs(distance) <= HALFCOL
    phase_arg = CHIRP_COL / HALFCOL * distance * distance
    weight = 1.0 / math.sqrt(2 * HALFCOL + 1)
    real_part = np.where(inside, np.cos(phase_arg) * weight, 0.0)
    imag_part = np.where(inside, np.sin(phase_arg) * weight, 0.0)
    forward = np.concatenate([real_part, imag_part], axis=-1)
    adjoint = np.concatenate([real_part, -imag_part], axis=-1)
    return jnp.asarray(np.stack([forward, adjoint], axis=0).astype(np.float32))


def dot3(a_high, a_low, x):
    x_high, x_low = split_bf16(x)
    f32 = jnp.float32
    rows = a_high.shape[0]
    both = jnp.dot(jnp.concatenate([a_high, a_low], axis=0), x_high, preferred_element_type=f32)
    return both[:rows] + both[rows:] + jnp.dot(a_high, x_low, preferred_element_type=f32)


CHUNKS = 4


def chain_kernel(rows, sections, angle_ref, vol_ref, off_ref, inten_ref, table_ref, cband_ref,
                 out_ref, terms_ref, partner_ref, field_ref, acc_ref, y_store, b_store, before, after,
                 bmh_ref, bml_ref, cos_ref, sin_ref, rband_ref, vol_slots, off_slots,
                 send_dn, send_up, recv_bf, recv_af, send_pair, recv_pair,
                 send_vol, send_off, recv_vol, recv_off, chb_ref, clb_ref, rbh_ref, rbl_ref, own_off):
    me = lax.axis_index("row")
    section = lax.axis_index("depth")
    partner = section + 1 - 2 * (section % 2)
    layers, height, columns = cos_ref.shape
    blocks = columns // LANE
    width = columns // CHUNKS
    per_chunk = blocks // CHUNKS
    has_up = me > 0
    has_dn = me < rows - 1

    own_off[...] = jnp.full(own_off.shape, off_ref[0].astype(jnp.float32), jnp.float32)
    angle = angle_ref[section % angle_ref.shape[0]]
    across = angle - TILTS // 2
    along = lax.rem(3 * angle, TILTS) - TILTS // 2
    shape2 = (cos_ref.shape[1], cos_ref.shape[2])
    period = shape2[0] * rows * shape2[1]
    row_index = me * shape2[0] + lax.broadcasted_iota(jnp.int32, shape2, 0)
    col_index = lax.broadcasted_iota(jnp.int32, shape2, 1)
    cycles = lax.rem(across * col_index * (shape2[0] * rows) + along * row_index * shape2[1], period)
    cycles = jnp.where(cycles < 0, cycles + period, cycles)
    wave_arg = 2.0 * math.pi / period * cycles.astype(jnp.float32)
    field_ref[...] = jnp.concatenate([jnp.cos(wave_arg), jnp.sin(wave_arg)], axis=0)
    barrier = pltpu.get_barrier_semaphore()

    @pl.when(has_up)
    def _():
        pl.semaphore_signal(barrier, 1, device_id={"row": me - 1}, device_id_type=MESH)

    @pl.when(has_dn)
    def _():
        pl.semaphore_signal(barrier, 1, device_id={"row": me + 1}, device_id_type=MESH)

    for step in range(1, sections):
        peer = (section + step) % sections
        pl.semaphore_signal(barrier, 1, device_id={"depth": peer}, device_id_type=MESH)
    peers = (me + rows - 1) // rows + (2 * rows - 2 - me) // rows
    pl.semaphore_wait(barrier, peers + sections - 1)

    def gathers(step, slot):
        peer = (section + step) % sections
        vol_copy = pltpu.make_async_remote_copy(
            src_ref=vol_ref.at[0], dst_ref=vol_slots.at[slot], send_sem=send_vol.at[step],
            recv_sem=recv_vol.at[slot], device_id={"depth": peer}, device_id_type=MESH)
        off_copy = pltpu.make_async_remote_copy(
            src_ref=own_off, dst_ref=off_slots.at[slot], send_sem=send_off.at[step],
            recv_sem=recv_off.at[slot], device_id={"depth": peer}, device_id_type=MESH)
        return vol_copy, off_copy

    for step in range(1, sections):
        for one in gathers(step, section):
            one.start()
    vol_slots[section] = vol_ref[0]
    off_slots[section] = own_off[...]
    part_rows = 2 * height

    def prepare(s):
        @pl.when(s != section)
        def _():
            for one in gathers(1, s):
                one.wait_recv()

        phase = PHASE_SCALE * vol_slots[s].astype(jnp.float32)
        cos_ref[s] = jnp.cos(phase)
        sin_ref[s] = jnp.sin(phase)
        shift = off_slots[s][0:1, 0:part_rows]
        forward_band = None
        adjoint_band = None
        for i in range(2 * SHIFT + 1):
            pick = jnp.where(shift == float(i - SHIFT), 1.0, 0.0)
            f_term = pick * table_ref[0, i]
            a_term = pick * table_ref[1, i]
            forward_band = f_term if forward_band is None else forward_band + f_term
            adjoint_band = a_term if adjoint_band is None else adjoint_band + a_term
        high, low = split_bf16(forward_band)
        rbh_ref[s] = high
        rbl_ref[s] = low
        high, low = split_bf16(adjoint_band)
        rbh_ref[2 * layers - 1 - s] = high
        rbl_ref[2 * layers - 1 - s] = low

    high, low = split_bf16(cband_ref[...])
    chb_ref[...] = high
    clb_ref[...] = low
    zero_block = jnp.zeros((2 * height, LANE), jnp.bfloat16)
    for ref in (bmh_ref, bml_ref):
        ref[0] = zero_block
        ref[blocks + 1] = zero_block

    def copies(k, c, store):
        cols = pl.ds(c * width, width)
        slot = k * CHUNKS + c
        down = pltpu.make_async_remote_copy(
            src_ref=store.at[:, cols], dst_ref=before.at[k, :, cols], send_sem=send_dn.at[slot],
            recv_sem=recv_bf.at[slot], device_id={"row": me + 1}, device_id_type=MESH)
        up = pltpu.make_async_remote_copy(
            src_ref=store.at[:, cols], dst_ref=after.at[k, :, cols], send_sem=send_up.at[slot],
            recv_sem=recv_af.at[slot], device_id={"row": me - 1}, device_id_type=MESH)
        return down, up

    def start(k, c, store):
        down, up = copies(k, c, store)

        @pl.when(has_dn)
        def _():
            down.start()

        @pl.when(has_up)
        def _():
            up.start()

    def finish(k, store):
        for c in range(CHUNKS):
            down, up = copies(k, c, store)

            @pl.when(has_dn)
            def _():
                down.wait_send()

            @pl.when(has_up)
            def _():
                up.wait_send()

    def halo(k, c, store):
        down, up = copies(k, c, store)
        cols = pl.ds(c * width, width)
        slot = k % 2

        @pl.when(has_up)
        def _():
            down.wait_recv()
            acc_ref[slot, :, cols] += dot3(rbh_ref[k, 0:part_rows], rbl_ref[k, 0:part_rows], before[k, :, cols])

        @pl.when(has_dn)
        def _():
            up.wait_recv()
            acc_ref[slot, :, cols] += dot3(rbh_ref[k, 2 * part_rows:3 * part_rows], rbl_ref[k, 2 * part_rows:3 * part_rows], after[k, :, cols])

        return acc_ref[slot, :, cols]

    def emit(k, c, store, value):
        cols = pl.ds(c * width, width)
        store[:, cols] = value
        acc_ref[k % 2, :, cols] = dot3(rbh_ref[k, part_rows:2 * part_rows], rbl_ref[k, part_rows:2 * part_rows], store[:, cols])
        start(k, c, store)

    def write_blocks(c, x):
        high, low = split_bf16(x)
        for b in range(per_chunk):
            bmh_ref[c * per_chunk + b + 1] = high[:, b * LANE:(b + 1) * LANE]
            bml_ref[c * per_chunk + b + 1] = low[:, b * LANE:(b + 1) * LANE]

    def wave(k, store, store_next, finish_chunk, make_chunk):
        for c in range(CHUNKS):
            write_blocks(c, finish_chunk(c, halo(k, c, store)))
            if c >= 1:
                emit(k + 1, c - 1, store_next, make_chunk(c - 1))
        emit(k + 1, CHUNKS - 1, store_next, make_chunk(CHUNKS - 1))
        finish(k, store)

    def col_chunk(c, which):
        total = None
        f32 = jnp.float32
        first = c * per_chunk
        for t in range(3):
            xh = bmh_ref[first + t:first + t + per_chunk].reshape(per_chunk * 2 * height, LANE)
            xl = bml_ref[first + t:first + t + per_chunk].reshape(per_chunk * 2 * height, LANE)
            wh = chb_ref[which, t]
            wl = clb_ref[which, t]
            count = xh.shape[0]
            both = jnp.dot(jnp.concatenate([xh, xl], axis=0), wh, preferred_element_type=f32)
            part = both[:count] + both[count:] + jnp.dot(xh, wl, preferred_element_type=f32)
            total = part if total is None else total + part
        total = total.reshape(per_chunk, 2 * height, 2 * LANE)
        real_part = total[:, :height, :LANE] - total[:, height:, LANE:]
        imag_part = total[:, :height, LANE:] + total[:, height:, :LANE]
        out = jnp.concatenate([real_part, imag_part], axis=1)
        return jnp.concatenate([out[b] for b in range(per_chunk)], axis=1)

    def rotated(s, c, u):
        cols = pl.ds(c * width, width)
        cs = cos_ref[s, :, cols]
        sn = sin_ref[s, :, cols]
        ur = u[:height]
        ui = u[height:]
        return jnp.concatenate([cs * ur - sn * ui, cs * ui + sn * ur], axis=0)

    def adjoint_chunk(s, c, a):
        cols = pl.ds(c * width, width)
        ar = a[:height]
        ai = a[height:]
        y = y_store[s, :, cols]
        terms_ref[s, :, cols] = PHASE_SCALE * (y[:height] * ai - y[height:] * ar)
        cs = cos_ref[s, :, cols]
        sn = sin_ref[s, :, cols]
        return jnp.concatenate([cs * ar + sn * ai, cs * ai - sn * ar], axis=0)

    prepare(0)
    for c in range(CHUNKS):
        emit(0, c, y_store.at[0], rotated(0, c, field_ref[:, c * width:(c + 1) * width]))

    def forward(k, carry):
        prepare(k + 1)
        wave(k, y_store.at[k], y_store.at[k + 1], lambda c, a: a,
             lambda c: rotated(k + 1, c, col_chunk(c, 0)))
        return carry

    lax.fori_loop(0, layers - 1, forward, 0)
    for c in range(CHUNKS):
        write_blocks(c, halo(layers - 1, c, y_store.at[layers - 1]))
    finish(layers - 1, y_store.at[layers - 1])
    for c in range(CHUNKS):
        field_ref[:, c * width:(c + 1) * width] = col_chunk(c, 0)
    u = field_ref[...]
    ur = u[:height]
    ui = u[height:]
    errors = ur * ur + ui * ui - inten_ref[section % inten_ref.shape[0]].astype(jnp.float32)
    field_ref[...] = jnp.concatenate([2.0 * errors * ur, 2.0 * errors * ui], axis=0)
    for c in range(CHUNKS):
        write_blocks(c, field_ref[:, c * width:(c + 1) * width])
    for c in range(CHUNKS):
        emit(layers, c, b_store.at[0], col_chunk(c, 1))

    def backward(j, carry):
        s = layers - 1 - j
        wave(layers + j, b_store.at[j], b_store.at[j + 1], lambda c, a: adjoint_chunk(s, c, a),
             lambda c: col_chunk(c, 1))
        return carry

    lax.fori_loop(0, layers - 1, backward, 0)
    last = 2 * layers - 1
    for c in range(CHUNKS):
        adjoint_chunk(0, c, halo(last, c, b_store.at[layers - 1]))
    finish(last, b_store.at[layers - 1])
    own = terms_ref[section]
    exchange = pltpu.make_async_remote_copy(
        src_ref=terms_ref.at[partner], dst_ref=partner_ref, send_sem=send_pair, recv_sem=recv_pair,
        device_id={"depth": partner}, device_id_type=MESH)
    exchange.start()
    exchange.wait_send()
    exchange.wait_recv()
    out_ref[0] = own + partner_ref[...]
    for step in range(1, sections):
        for one in gathers(step, section):
            one.wait_send()


def run_chain(angles, index_volume, offsets, intensity, rows, sections):
    _, height, columns = index_volume.shape
    layers = sections
    blocks = columns // LANE
    field = (2 * height, columns)
    plane = (layers, height, columns)
    return pl.pallas_call(
        functools.partial(chain_kernel, rows, sections),
        out_shape=jax.ShapeDtypeStruct((1, height, columns), jnp.float32),
        in_specs=[pl.BlockSpec(memory_space=pltpu.SMEM), pl.BlockSpec(memory_space=pltpu.VMEM),
                  pl.BlockSpec(memory_space=pltpu.SMEM)] + [pl.BlockSpec(memory_space=pltpu.VMEM)] * 3,
        out_specs=pl.BlockSpec(memory_space=pltpu.VMEM),
        scratch_shapes=[
            pltpu.VMEM(plane, jnp.float32),
            pltpu.VMEM((height, columns), jnp.float32),
            pltpu.VMEM(field, jnp.float32),
            pltpu.VMEM((2,) + field, jnp.float32),
            pltpu.VMEM((layers,) + field, jnp.float32),
            pltpu.VMEM((layers,) + field, jnp.float32),
            pltpu.VMEM((2 * layers,) + field, jnp.float32),
            pltpu.VMEM((2 * layers,) + field, jnp.float32),
            pltpu.VMEM((blocks + 2, 2 * height, LANE), jnp.bfloat16),
            pltpu.VMEM((blocks + 2, 2 * height, LANE), jnp.bfloat16),
            pltpu.VMEM(plane, jnp.float32),
            pltpu.VMEM(plane, jnp.float32),
            pltpu.VMEM((2 * layers, 3 * 2 * height, 2 * height), jnp.float32),
            pltpu.VMEM(plane, index_volume.dtype),
            pltpu.VMEM((sections, 8, LANE), jnp.float32),
            pltpu.SemaphoreType.DMA((2 * layers * CHUNKS,)),
            pltpu.SemaphoreType.DMA((2 * layers * CHUNKS,)),
            pltpu.SemaphoreType.DMA((2 * layers * CHUNKS,)),
            pltpu.SemaphoreType.DMA((2 * layers * CHUNKS,)),
            pltpu.SemaphoreType.DMA,
            pltpu.SemaphoreType.DMA,
            pltpu.SemaphoreType.DMA((sections,)),
            pltpu.SemaphoreType.DMA((sections,)),
            pltpu.SemaphoreType.DMA((sections,)),
            pltpu.SemaphoreType.DMA((sections,)),
            pltpu.VMEM((2, 3, LANE, 2 * LANE), jnp.bfloat16),
            pltpu.VMEM((2, 3, LANE, 2 * LANE), jnp.bfloat16),
            pltpu.VMEM((2 * layers, 3 * 2 * height, 2 * height), jnp.bfloat16),
            pltpu.VMEM((2 * layers, 3 * 2 * height, 2 * height), jnp.bfloat16),
            pltpu.VMEM((8, LANE), jnp.float32),
        ],
        compiler_params=pltpu.CompilerParams(
            collective_id=0, has_side_effects=True, vmem_limit_bytes=56 * 1024 * 1024),
    )(angles, index_volume, offsets, intensity, band_table(height), column_bands())


def plane_wave(angle, row_start, height, columns, total_rows, total_cols):
    across = angle - TILTS // 2
    along = jnp.mod(3 * angle, TILTS) - TILTS // 2
    row_index = row_start + lax.broadcasted_iota(jnp.int32, (height, columns), 0)
    col_index = lax.broadcasted_iota(jnp.int32, (height, columns), 1)
    period = total_cols * total_rows
    cycles_int = jnp.mod(across * col_index * total_rows + along * row_index * total_cols, period)
    phase_arg = 2.0 * math.pi / period * cycles_int.astype(jnp.float32)
    return jnp.concatenate([jnp.cos(phase_arg), jnp.sin(phase_arg)], axis=0)


def body(index_volume, angles, offsets, measured):
    sections = lax.axis_size("depth")
    rows = lax.axis_size("row")
    section_no = lax.axis_index("depth")
    height = index_volume.shape[1]
    columns = index_volume.shape[2]
    row_start = lax.axis_index("row") * height
    total_rows = height * rows
    angle_count = angles.shape[0]
    angle_no = section_no % angle_count
    return run_chain(angles, index_volume, offsets, measured, rows, sections)


def solution(mesh):
    in_specs = (P("depth", "row", None), P(), P("depth"), P(None, "row", None))
    out_specs = P("depth", "row", None)
    return jax.shard_map(body, mesh=mesh, in_specs=in_specs, out_specs=out_specs, check_vma=False)
```

```python
import functools
import math

import jax
import numpy as np
import jax.numpy as jnp
from jax import lax
from jax.experimental import pallas as pl
from jax.experimental.pallas import tpu as pltpu
from jax.sharding import PartitionSpec as P

TILTS = 16
HALF = 10
SHIFT = 4
HALFCOL = 64
LANE = 128

PHASE_SCALE = 0.5
CHIRP_ROW = 1.3
CHIRP_COL = 1.7
MESH = pl.DeviceIdType.MESH


def kernel_values(distance, radius, chirp_rate):
    inside = jnp.abs(distance) <= radius
    phase_arg = chirp_rate / radius * distance * distance
    weight = 1.0 / math.sqrt(2 * radius + 1)
    real_part = jnp.where(inside, jnp.cos(phase_arg) * weight, 0.0)
    imag_part = jnp.where(inside, jnp.sin(phase_arg) * weight, 0.0)
    return (real_part, imag_part)


def split_bf16(x):
    high = x.astype(jnp.bfloat16)
    low = (x - high.astype(jnp.float32)).astype(jnp.bfloat16)
    return high, low


def complex_block(real_part, imag_part):
    top = jnp.concatenate([real_part, -imag_part], axis=-1)
    bottom = jnp.concatenate([imag_part, real_part], axis=-1)
    return jnp.concatenate([top, bottom], axis=-2)


def band_table(height):
    offsets = np.arange(-SHIFT, SHIFT + 1)[:, None, None, None]
    part = np.arange(3)[None, :, None, None]
    target = np.arange(height)[None, None, :, None]
    source = np.arange(height)[None, None, None, :] + (part - 1) * height
    tables = []
    for sign in (1, -1):
        distance = (source - target - sign * offsets).astype(np.float64)
        inside = np.abs(distance) <= HALF
        phase_arg = CHIRP_ROW / HALF * distance * distance
        weight = 1.0 / math.sqrt(2 * HALF + 1)
        real_part = np.where(inside, np.cos(phase_arg) * weight, 0.0)
        imag_part = np.where(inside, np.sin(phase_arg) * weight, 0.0) * sign
        top = np.concatenate([real_part, -imag_part], axis=-1)
        bottom = np.concatenate([imag_part, real_part], axis=-1)
        block = np.concatenate([top, bottom], axis=-2)
        tables.append(block.reshape(2 * SHIFT + 1, 3 * 2 * height, 2 * height))
    return jnp.asarray(np.stack(tables, axis=0).astype(np.float32))


def column_bands():
    part = np.arange(3)[:, None, None]
    source = np.arange(LANE)[None, :, None] + (part - 1) * LANE
    target = np.arange(LANE)[None, None, :]
    distance = (source - target).astype(np.float64)
    inside = np.abs(distance) <= HALFCOL
    phase_arg = CHIRP_COL / HALFCOL * distance * distance
    weight = 1.0 / math.sqrt(2 * HALFCOL + 1)
    real_part = np.where(inside, np.cos(phase_arg) * weight, 0.0)
    imag_part = np.where(inside, np.sin(phase_arg) * weight, 0.0)
    forward = np.concatenate([real_part, imag_part], axis=-1)
    adjoint = np.concatenate([real_part, -imag_part], axis=-1)
    return jnp.asarray(np.stack([forward, adjoint], axis=0).astype(np.float32))


def dot3(a_high, a_low, x):
    x_high, x_low = split_bf16(x)
    f32 = jnp.float32
    rows = a_high.shape[0]
    both = jnp.dot(jnp.concatenate([a_high, a_low], axis=0), x_high, preferred_element_type=f32)
    return both[:rows] + both[rows:] + jnp.dot(a_high, x_low, preferred_element_type=f32)


CHUNKS = 4


def chain_kernel(rows, sections, angle_ref, vol_ref, off_ref, inten_ref, table_ref, cband_ref,
                 out_ref, terms_ref, partner_ref, field_ref, acc_ref, y_store, b_store, before, after,
                 bmh_ref, bml_ref, cos_ref, sin_ref, rband_ref, vol_slots, off_slots,
                 send_dn, send_up, recv_bf, recv_af, send_pair, recv_pair,
                 send_vol, send_off, recv_vol, recv_off, chb_ref, clb_ref, rbh_ref, rbl_ref, own_off):
    me = lax.axis_index("row")
    section = lax.axis_index("depth")
    partner = section + 1 - 2 * (section % 2)
    layers, height, columns = cos_ref.shape
    blocks = columns // LANE
    width = columns // CHUNKS
    per_chunk = blocks // CHUNKS
    has_up = me > 0
    has_dn = me < rows - 1

    own_off[...] = jnp.full(own_off.shape, off_ref[0].astype(jnp.float32), jnp.float32)
    barrier = pltpu.get_barrier_semaphore()

    @pl.when(has_up)
    def _():
        pl.semaphore_signal(barrier, 1, device_id={"row": me - 1}, device_id_type=MESH)

    @pl.when(has_dn)
    def _():
        pl.semaphore_signal(barrier, 1, device_id={"row": me + 1}, device_id_type=MESH)

    for step in range(1, sections):
        peer = (section + step) % sections
        pl.semaphore_signal(barrier, 1, device_id={"depth": peer}, device_id_type=MESH)
    angle = angle_ref[section % angle_ref.shape[0]]
    across = angle - TILTS // 2
    along = lax.rem(3 * angle, TILTS) - TILTS // 2
    shape2 = (cos_ref.shape[1], cos_ref.shape[2])
    period = shape2[0] * rows * shape2[1]
    row_index = me * shape2[0] + lax.broadcasted_iota(jnp.int32, shape2, 0)
    col_index = lax.broadcasted_iota(jnp.int32, shape2, 1)
    cycles = lax.rem(across * col_index * (shape2[0] * rows) + along * row_index * shape2[1], period)
    cycles = jnp.where(cycles < 0, cycles + period, cycles)
    wave_arg = 2.0 * math.pi / period * cycles.astype(jnp.float32)
    field_ref[...] = jnp.concatenate([jnp.cos(wave_arg), jnp.sin(wave_arg)], axis=0)
    high, low = split_bf16(cband_ref[...])
    chb_ref[...] = high
    clb_ref[...] = low
    zero_block = jnp.zeros((2 * height, LANE), jnp.bfloat16)
    for ref in (bmh_ref, bml_ref):
        ref[0] = zero_block
        ref[blocks + 1] = zero_block
    peers = (me + rows - 1) // rows + (2 * rows - 2 - me) // rows
    pl.semaphore_wait(barrier, peers + sections - 1)

    def gathers(step, slot):
        peer = (section + step) % sections
        vol_copy = pltpu.make_async_remote_copy(
            src_ref=vol_ref.at[0], dst_ref=vol_slots.at[slot], send_sem=send_vol.at[step],
            recv_sem=recv_vol.at[slot], device_id={"depth": peer}, device_id_type=MESH)
        off_copy = pltpu.make_async_remote_copy(
            src_ref=own_off, dst_ref=off_slots.at[slot], send_sem=send_off.at[step],
            recv_sem=recv_off.at[slot], device_id={"depth": peer}, device_id_type=MESH)
        return vol_copy, off_copy

    for step in range(1, sections):
        for one in gathers(step, section):
            one.start()
    vol_slots[section] = vol_ref[0]
    off_slots[section] = own_off[...]
    part_rows = 2 * height

    def prepare(s):
        @pl.when(s != section)
        def _():
            for one in gathers(1, s):
                one.wait_recv()

        phase = PHASE_SCALE * vol_slots[s].astype(jnp.float32)
        cos_ref[s] = jnp.cos(phase)
        sin_ref[s] = jnp.sin(phase)
        shift = off_slots[s][0:1, 0:part_rows]
        forward_band = None
        adjoint_band = None
        for i in range(2 * SHIFT + 1):
            pick = jnp.where(shift == float(i - SHIFT), 1.0, 0.0)
            f_term = pick * table_ref[0, i]
            a_term = pick * table_ref[1, i]
            forward_band = f_term if forward_band is None else forward_band + f_term
            adjoint_band = a_term if adjoint_band is None else adjoint_band + a_term
        high, low = split_bf16(forward_band)
        rbh_ref[s] = high
        rbl_ref[s] = low
        high, low = split_bf16(adjoint_band)
        rbh_ref[2 * layers - 1 - s] = high
        rbl_ref[2 * layers - 1 - s] = low


    def copies(k, c, store):
        cols = pl.ds(c * width, width)
        slot = k * CHUNKS + c
        down = pltpu.make_async_remote_copy(
            src_ref=store.at[:, cols], dst_ref=before.at[k, :, cols], send_sem=send_dn.at[slot],
            recv_sem=recv_bf.at[slot], device_id={"row": me + 1}, device_id_type=MESH)
        up = pltpu.make_async_remote_copy(
            src_ref=store.at[:, cols], dst_ref=after.at[k, :, cols], send_sem=send_up.at[slot],
            recv_sem=recv_af.at[slot], device_id={"row": me - 1}, device_id_type=MESH)
        return down, up

    def start(k, c, store):
        down, up = copies(k, c, store)

        @pl.when(has_dn)
        def _():
            down.start()

        @pl.when(has_up)
        def _():
            up.start()

    def finish(k, store):
        for c in range(CHUNKS):
            down, up = copies(k, c, store)

            @pl.when(has_dn)
            def _():
                down.wait_send()

            @pl.when(has_up)
            def _():
                up.wait_send()

    def halo(k, c, store):
        down, up = copies(k, c, store)
        cols = pl.ds(c * width, width)
        slot = k % 2

        @pl.when(has_up)
        def _():
            down.wait_recv()
            acc_ref[slot, :, cols] += dot3(rbh_ref[k, 0:part_rows], rbl_ref[k, 0:part_rows], before[k, :, cols])

        @pl.when(has_dn)
        def _():
            up.wait_recv()
            acc_ref[slot, :, cols] += dot3(rbh_ref[k, 2 * part_rows:3 * part_rows], rbl_ref[k, 2 * part_rows:3 * part_rows], after[k, :, cols])

        return acc_ref[slot, :, cols]

    def emit(k, c, store, value):
        cols = pl.ds(c * width, width)
        store[:, cols] = value
        acc_ref[k % 2, :, cols] = dot3(rbh_ref[k, part_rows:2 * part_rows], rbl_ref[k, part_rows:2 * part_rows], store[:, cols])
        start(k, c, store)

    def write_blocks(c, x):
        high, low = split_bf16(x)
        for b in range(per_chunk):
            bmh_ref[c * per_chunk + b + 1] = high[:, b * LANE:(b + 1) * LANE]
            bml_ref[c * per_chunk + b + 1] = low[:, b * LANE:(b + 1) * LANE]

    def wave(k, store, store_next, finish_chunk, make_chunk):
        for c in range(CHUNKS):
            write_blocks(c, finish_chunk(c, halo(k, c, store)))
            if c >= 1:
                emit(k + 1, c - 1, store_next, make_chunk(c - 1))
        emit(k + 1, CHUNKS - 1, store_next, make_chunk(CHUNKS - 1))
        finish(k, store)

    def col_chunk(c, which):
        total = None
        f32 = jnp.float32
        first = c * per_chunk
        for t in range(3):
            xh = bmh_ref[first + t:first + t + per_chunk].reshape(per_chunk * 2 * height, LANE)
            xl = bml_ref[first + t:first + t + per_chunk].reshape(per_chunk * 2 * height, LANE)
            wh = chb_ref[which, t]
            wl = clb_ref[which, t]
            count = xh.shape[0]
            both = jnp.dot(jnp.concatenate([xh, xl], axis=0), wh, preferred_element_type=f32)
            part = both[:count] + both[count:] + jnp.dot(xh, wl, preferred_element_type=f32)
            total = part if total is None else total + part
        total = total.reshape(per_chunk, 2 * height, 2 * LANE)
        real_part = total[:, :height, :LANE] - total[:, height:, LANE:]
        imag_part = total[:, :height, LANE:] + total[:, height:, :LANE]
        out = jnp.concatenate([real_part, imag_part], axis=1)
        return jnp.concatenate([out[b] for b in range(per_chunk)], axis=1)

    def rotated(s, c, u):
        cols = pl.ds(c * width, width)
        cs = cos_ref[s, :, cols]
        sn = sin_ref[s, :, cols]
        ur = u[:height]
        ui = u[height:]
        return jnp.concatenate([cs * ur - sn * ui, cs * ui + sn * ur], axis=0)

    def adjoint_chunk(s, c, a):
        cols = pl.ds(c * width, width)
        ar = a[:height]
        ai = a[height:]
        y = y_store[s, :, cols]
        terms_ref[s, :, cols] = PHASE_SCALE * (y[:height] * ai - y[height:] * ar)
        cs = cos_ref[s, :, cols]
        sn = sin_ref[s, :, cols]
        return jnp.concatenate([cs * ar + sn * ai, cs * ai - sn * ar], axis=0)

    prepare(0)
    for c in range(CHUNKS):
        emit(0, c, y_store.at[0], rotated(0, c, field_ref[:, c * width:(c + 1) * width]))

    def forward(k, carry):
        prepare(k + 1)
        wave(k, y_store.at[k], y_store.at[k + 1], lambda c, a: a,
             lambda c: rotated(k + 1, c, col_chunk(c, 0)))
        return carry

    lax.fori_loop(0, layers - 1, forward, 0)
    for c in range(CHUNKS):
        write_blocks(c, halo(layers - 1, c, y_store.at[layers - 1]))
    finish(layers - 1, y_store.at[layers - 1])
    for c in range(CHUNKS):
        field_ref[:, c * width:(c + 1) * width] = col_chunk(c, 0)
    u = field_ref[...]
    ur = u[:height]
    ui = u[height:]
    errors = ur * ur + ui * ui - inten_ref[section % inten_ref.shape[0]].astype(jnp.float32)
    field_ref[...] = jnp.concatenate([2.0 * errors * ur, 2.0 * errors * ui], axis=0)
    for c in range(CHUNKS):
        write_blocks(c, field_ref[:, c * width:(c + 1) * width])
    for c in range(CHUNKS):
        emit(layers, c, b_store.at[0], col_chunk(c, 1))

    def backward(j, carry):
        s = layers - 1 - j
        wave(layers + j, b_store.at[j], b_store.at[j + 1], lambda c, a: adjoint_chunk(s, c, a),
             lambda c: col_chunk(c, 1))
        return carry

    lax.fori_loop(0, layers - 1, backward, 0)
    last = 2 * layers - 1
    for c in range(CHUNKS):
        adjoint_chunk(0, c, halo(last, c, b_store.at[layers - 1]))
    finish(last, b_store.at[layers - 1])
    own = terms_ref[section]
    exchange = pltpu.make_async_remote_copy(
        src_ref=terms_ref.at[partner], dst_ref=partner_ref, send_sem=send_pair, recv_sem=recv_pair,
        device_id={"depth": partner}, device_id_type=MESH)
    exchange.start()
    exchange.wait_send()
    exchange.wait_recv()
    out_ref[0] = own + partner_ref[...]
    for step in range(1, sections):
        for one in gathers(step, section):
            one.wait_send()


def run_chain(angles, index_volume, offsets, intensity, rows, sections):
    _, height, columns = index_volume.shape
    layers = sections
    blocks = columns // LANE
    field = (2 * height, columns)
    plane = (layers, height, columns)
    return pl.pallas_call(
        functools.partial(chain_kernel, rows, sections),
        out_shape=jax.ShapeDtypeStruct((1, height, columns), jnp.float32),
        in_specs=[pl.BlockSpec(memory_space=pltpu.SMEM), pl.BlockSpec(memory_space=pltpu.VMEM),
                  pl.BlockSpec(memory_space=pltpu.SMEM)] + [pl.BlockSpec(memory_space=pltpu.VMEM)] * 3,
        out_specs=pl.BlockSpec(memory_space=pltpu.VMEM),
        scratch_shapes=[
            pltpu.VMEM(plane, jnp.float32),
            pltpu.VMEM((height, columns), jnp.float32),
            pltpu.VMEM(field, jnp.float32),
            pltpu.VMEM((2,) + field, jnp.float32),
            pltpu.VMEM((layers,) + field, jnp.float32),
            pltpu.VMEM((layers,) + field, jnp.float32),
            pltpu.VMEM((2 * layers,) + field, jnp.float32),
            pltpu.VMEM((2 * layers,) + field, jnp.float32),
            pltpu.VMEM((blocks + 2, 2 * height, LANE), jnp.bfloat16),
            pltpu.VMEM((blocks + 2, 2 * height, LANE), jnp.bfloat16),
            pltpu.VMEM(plane, jnp.float32),
            pltpu.VMEM(plane, jnp.float32),
            pltpu.VMEM((2 * layers, 3 * 2 * height, 2 * height), jnp.float32),
            pltpu.VMEM(plane, index_volume.dtype),
            pltpu.VMEM((sections, 8, LANE), jnp.float32),
            pltpu.SemaphoreType.DMA((2 * layers * CHUNKS,)),
            pltpu.SemaphoreType.DMA((2 * layers * CHUNKS,)),
            pltpu.SemaphoreType.DMA((2 * layers * CHUNKS,)),
            pltpu.SemaphoreType.DMA((2 * layers * CHUNKS,)),
            pltpu.SemaphoreType.DMA,
            pltpu.SemaphoreType.DMA,
            pltpu.SemaphoreType.DMA((sections,)),
            pltpu.SemaphoreType.DMA((sections,)),
            pltpu.SemaphoreType.DMA((sections,)),
            pltpu.SemaphoreType.DMA((sections,)),
            pltpu.VMEM((2, 3, LANE, 2 * LANE), jnp.bfloat16),
            pltpu.VMEM((2, 3, LANE, 2 * LANE), jnp.bfloat16),
            pltpu.VMEM((2 * layers, 3 * 2 * height, 2 * height), jnp.bfloat16),
            pltpu.VMEM((2 * layers, 3 * 2 * height, 2 * height), jnp.bfloat16),
            pltpu.VMEM((8, LANE), jnp.float32),
        ],
        compiler_params=pltpu.CompilerParams(
            collective_id=0, has_side_effects=True, vmem_limit_bytes=56 * 1024 * 1024),
    )(angles, index_volume, offsets, intensity, band_table(height), column_bands())


def plane_wave(angle, row_start, height, columns, total_rows, total_cols):
    across = angle - TILTS // 2
    along = jnp.mod(3 * angle, TILTS) - TILTS // 2
    row_index = row_start + lax.broadcasted_iota(jnp.int32, (height, columns), 0)
    col_index = lax.broadcasted_iota(jnp.int32, (height, columns), 1)
    period = total_cols * total_rows
    cycles_int = jnp.mod(across * col_index * total_rows + along * row_index * total_cols, period)
    phase_arg = 2.0 * math.pi / period * cycles_int.astype(jnp.float32)
    return jnp.concatenate([jnp.cos(phase_arg), jnp.sin(phase_arg)], axis=0)


def body(index_volume, angles, offsets, measured):
    sections = lax.axis_size("depth")
    rows = lax.axis_size("row")
    section_no = lax.axis_index("depth")
    height = index_volume.shape[1]
    columns = index_volume.shape[2]
    row_start = lax.axis_index("row") * height
    total_rows = height * rows
    angle_count = angles.shape[0]
    angle_no = section_no % angle_count
    return run_chain(angles, index_volume, offsets, measured, rows, sections)


def solution(mesh):
    in_specs = (P("depth", "row", None), P(), P("depth"), P(None, "row", None))
    out_specs = P("depth", "row", None)
    return jax.shard_map(body, mesh=mesh, in_specs=in_specs, out_specs=out_specs, check_vma=False)
```

```python
import functools
import math

import jax
import numpy as np
import jax.numpy as jnp
from jax import lax
from jax.experimental import pallas as pl
from jax.experimental.pallas import tpu as pltpu
from jax.sharding import PartitionSpec as P

TILTS = 16
HALF = 10
SHIFT = 4
HALFCOL = 64
LANE = 128

PHASE_SCALE = 0.5
CHIRP_ROW = 1.3
CHIRP_COL = 1.7
MESH = pl.DeviceIdType.MESH


def kernel_values(distance, radius, chirp_rate):
    inside = jnp.abs(distance) <= radius
    phase_arg = chirp_rate / radius * distance * distance
    weight = 1.0 / math.sqrt(2 * radius + 1)
    real_part = jnp.where(inside, jnp.cos(phase_arg) * weight, 0.0)
    imag_part = jnp.where(inside, jnp.sin(phase_arg) * weight, 0.0)
    return (real_part, imag_part)


def split_bf16(x):
    high = x.astype(jnp.bfloat16)
    low = (x - high.astype(jnp.float32)).astype(jnp.bfloat16)
    return high, low


def complex_block(real_part, imag_part):
    top = jnp.concatenate([real_part, -imag_part], axis=-1)
    bottom = jnp.concatenate([imag_part, real_part], axis=-1)
    return jnp.concatenate([top, bottom], axis=-2)


def band_table(height):
    offsets = np.arange(-SHIFT, SHIFT + 1)[:, None, None, None]
    part = np.arange(3)[None, :, None, None]
    target = np.arange(height)[None, None, :, None]
    source = np.arange(height)[None, None, None, :] + (part - 1) * height
    tables = []
    for sign in (1, -1):
        distance = (source - target - sign * offsets).astype(np.float64)
        inside = np.abs(distance) <= HALF
        phase_arg = CHIRP_ROW / HALF * distance * distance
        weight = 1.0 / math.sqrt(2 * HALF + 1)
        real_part = np.where(inside, np.cos(phase_arg) * weight, 0.0)
        imag_part = np.where(inside, np.sin(phase_arg) * weight, 0.0) * sign
        top = np.concatenate([real_part, -imag_part], axis=-1)
        bottom = np.concatenate([imag_part, real_part], axis=-1)
        block = np.concatenate([top, bottom], axis=-2)
        tables.append(block.reshape(2 * SHIFT + 1, 3 * 2 * height, 2 * height))
    return jnp.asarray(np.stack(tables, axis=0).astype(np.float32))


def column_bands():
    part = np.arange(3)[:, None, None]
    source = np.arange(LANE)[None, :, None] + (part - 1) * LANE
    target = np.arange(LANE)[None, None, :]
    distance = (source - target).astype(np.float64)
    inside = np.abs(distance) <= HALFCOL
    phase_arg = CHIRP_COL / HALFCOL * distance * distance
    weight = 1.0 / math.sqrt(2 * HALFCOL + 1)
    real_part = np.where(inside, np.cos(phase_arg) * weight, 0.0)
    imag_part = np.where(inside, np.sin(phase_arg) * weight, 0.0)
    forward = np.concatenate([real_part, imag_part], axis=-1)
    adjoint = np.concatenate([real_part, -imag_part], axis=-1)
    return jnp.asarray(np.stack([forward, adjoint], axis=0).astype(np.float32))


def dot3(a_high, a_low, x):
    x_high, x_low = split_bf16(x)
    f32 = jnp.float32
    rows = a_high.shape[0]
    both = jnp.dot(jnp.concatenate([a_high, a_low], axis=0), x_high, preferred_element_type=f32)
    return both[:rows] + both[rows:] + jnp.dot(a_high, x_low, preferred_element_type=f32)


CHUNKS = 4


def chain_kernel(rows, sections, angle_ref, vol_ref, off_ref, inten_ref, table_ref, cband_ref,
                 out_ref, terms_ref, partner_ref, field_ref, acc_ref, y_store, b_store, before, after,
                 bmh_ref, bml_ref, cos_ref, sin_ref, rband_ref, vol_slots, off_slots,
                 send_dn, send_up, recv_bf, recv_af, send_pair, recv_pair,
                 send_vol, send_off, recv_vol, recv_off, chb_ref, clb_ref, rbh_ref, rbl_ref, own_off):
    me = lax.axis_index("row")
    section = lax.axis_index("depth")
    partner = section + 1 - 2 * (section % 2)
    layers, height, columns = cos_ref.shape
    blocks = columns // LANE
    width = columns // CHUNKS
    per_chunk = blocks // CHUNKS
    has_up = me > 0
    has_dn = me < rows - 1

    own_off[...] = jnp.full(own_off.shape, off_ref[0].astype(jnp.float32), jnp.float32)
    barrier = pltpu.get_barrier_semaphore()

    @pl.when(has_up)
    def _():
        pl.semaphore_signal(barrier, 1, device_id={"row": me - 1}, device_id_type=MESH)

    @pl.when(has_dn)
    def _():
        pl.semaphore_signal(barrier, 1, device_id={"row": me + 1}, device_id_type=MESH)

    for step in range(1, sections):
        peer = (section + step) % sections
        pl.semaphore_signal(barrier, 1, device_id={"depth": peer}, device_id_type=MESH)
    angle = angle_ref[section % angle_ref.shape[0]]
    across = angle - TILTS // 2
    along = lax.rem(3 * angle, TILTS) - TILTS // 2
    shape2 = (cos_ref.shape[1], cos_ref.shape[2])
    period = shape2[0] * rows * shape2[1]
    row_index = me * shape2[0] + lax.broadcasted_iota(jnp.int32, shape2, 0)
    col_index = lax.broadcasted_iota(jnp.int32, shape2, 1)
    cycles = lax.rem(across * col_index * (shape2[0] * rows) + along * row_index * shape2[1], period)
    cycles = jnp.where(cycles < 0, cycles + period, cycles)
    wave_arg = 2.0 * math.pi / period * cycles.astype(jnp.float32)
    field_ref[...] = jnp.concatenate([jnp.cos(wave_arg), jnp.sin(wave_arg)], axis=0)
    high, low = split_bf16(cband_ref[...])
    chb_ref[...] = high
    clb_ref[...] = low
    zero_block = jnp.zeros((2 * height, LANE), jnp.bfloat16)
    for ref in (bmh_ref, bml_ref):
        ref[0] = zero_block
        ref[blocks + 1] = zero_block
    peers = (me + rows - 1) // rows + (2 * rows - 2 - me) // rows
    vol_slots[section] = vol_ref[0]
    off_slots[section] = own_off[...]
    part_rows = 2 * height
    def compute(s):
        phase = PHASE_SCALE * vol_slots[s].astype(jnp.float32)
        cos_ref[s] = jnp.cos(phase)
        sin_ref[s] = jnp.sin(phase)
        shift = off_slots[s][0:1, 0:part_rows]
        forward_band = None
        adjoint_band = None
        for i in range(2 * SHIFT + 1):
            pick = jnp.where(shift == float(i - SHIFT), 1.0, 0.0)
            f_term = pick * table_ref[0, i]
            a_term = pick * table_ref[1, i]
            forward_band = f_term if forward_band is None else forward_band + f_term
            adjoint_band = a_term if adjoint_band is None else adjoint_band + a_term
        high, low = split_bf16(forward_band)
        rbh_ref[s] = high
        rbl_ref[s] = low
        high, low = split_bf16(adjoint_band)
        rbh_ref[2 * layers - 1 - s] = high
        rbl_ref[2 * layers - 1 - s] = low

    compute(section)
    pl.semaphore_wait(barrier, peers + sections - 1)

    def gathers(step, slot):
        peer = (section + step) % sections
        vol_copy = pltpu.make_async_remote_copy(
            src_ref=vol_ref.at[0], dst_ref=vol_slots.at[slot], send_sem=send_vol.at[step],
            recv_sem=recv_vol.at[slot], device_id={"depth": peer}, device_id_type=MESH)
        off_copy = pltpu.make_async_remote_copy(
            src_ref=own_off, dst_ref=off_slots.at[slot], send_sem=send_off.at[step],
            recv_sem=recv_off.at[slot], device_id={"depth": peer}, device_id_type=MESH)
        return vol_copy, off_copy

    for step in range(1, sections):
        for one in gathers(step, section):
            one.start()

    def prepare(s):
        @pl.when(s != section)
        def _():
            for one in gathers(1, s):
                one.wait_recv()
            compute(s)


    def copies(k, c, store):
        cols = pl.ds(c * width, width)
        slot = k * CHUNKS + c
        down = pltpu.make_async_remote_copy(
            src_ref=store.at[:, cols], dst_ref=before.at[k, :, cols], send_sem=send_dn.at[slot],
            recv_sem=recv_bf.at[slot], device_id={"row": me + 1}, device_id_type=MESH)
        up = pltpu.make_async_remote_copy(
            src_ref=store.at[:, cols], dst_ref=after.at[k, :, cols], send_sem=send_up.at[slot],
            recv_sem=recv_af.at[slot], device_id={"row": me - 1}, device_id_type=MESH)
        return down, up

    def start(k, c, store):
        down, up = copies(k, c, store)

        @pl.when(has_dn)
        def _():
            down.start()

        @pl.when(has_up)
        def _():
            up.start()

    def finish(k, store):
        for c in range(CHUNKS):
            down, up = copies(k, c, store)

            @pl.when(has_dn)
            def _():
                down.wait_send()

            @pl.when(has_up)
            def _():
                up.wait_send()

    def halo(k, c, store):
        down, up = copies(k, c, store)
        cols = pl.ds(c * width, width)
        slot = k % 2

        @pl.when(has_up)
        def _():
            down.wait_recv()
            acc_ref[slot, :, cols] += dot3(rbh_ref[k, 0:part_rows], rbl_ref[k, 0:part_rows], before[k, :, cols])

        @pl.when(has_dn)
        def _():
            up.wait_recv()
            acc_ref[slot, :, cols] += dot3(rbh_ref[k, 2 * part_rows:3 * part_rows], rbl_ref[k, 2 * part_rows:3 * part_rows], after[k, :, cols])

        return acc_ref[slot, :, cols]

    def emit(k, c, store, value):
        cols = pl.ds(c * width, width)
        store[:, cols] = value
        acc_ref[k % 2, :, cols] = dot3(rbh_ref[k, part_rows:2 * part_rows], rbl_ref[k, part_rows:2 * part_rows], store[:, cols])
        start(k, c, store)

    def write_blocks(c, x):
        high, low = split_bf16(x)
        for b in range(per_chunk):
            bmh_ref[c * per_chunk + b + 1] = high[:, b * LANE:(b + 1) * LANE]
            bml_ref[c * per_chunk + b + 1] = low[:, b * LANE:(b + 1) * LANE]

    def wave(k, store, store_next, finish_chunk, make_chunk):
        for c in range(CHUNKS):
            write_blocks(c, finish_chunk(c, halo(k, c, store)))
            if c >= 1:
                emit(k + 1, c - 1, store_next, make_chunk(c - 1))
        emit(k + 1, CHUNKS - 1, store_next, make_chunk(CHUNKS - 1))
        finish(k, store)

    def col_chunk(c, which):
        total = None
        f32 = jnp.float32
        first = c * per_chunk
        for t in range(3):
            xh = bmh_ref[first + t:first + t + per_chunk].reshape(per_chunk * 2 * height, LANE)
            xl = bml_ref[first + t:first + t + per_chunk].reshape(per_chunk * 2 * height, LANE)
            wh = chb_ref[which, t]
            wl = clb_ref[which, t]
            count = xh.shape[0]
            both = jnp.dot(jnp.concatenate([xh, xl], axis=0), wh, preferred_element_type=f32)
            part = both[:count] + both[count:] + jnp.dot(xh, wl, preferred_element_type=f32)
            total = part if total is None else total + part
        total = total.reshape(per_chunk, 2 * height, 2 * LANE)
        real_part = total[:, :height, :LANE] - total[:, height:, LANE:]
        imag_part = total[:, :height, LANE:] + total[:, height:, :LANE]
        out = jnp.concatenate([real_part, imag_part], axis=1)
        return jnp.concatenate([out[b] for b in range(per_chunk)], axis=1)

    def rotated(s, c, u):
        cols = pl.ds(c * width, width)
        cs = cos_ref[s, :, cols]
        sn = sin_ref[s, :, cols]
        ur = u[:height]
        ui = u[height:]
        return jnp.concatenate([cs * ur - sn * ui, cs * ui + sn * ur], axis=0)

    def adjoint_chunk(s, c, a):
        cols = pl.ds(c * width, width)
        ar = a[:height]
        ai = a[height:]
        y = y_store[s, :, cols]
        terms_ref[s, :, cols] = PHASE_SCALE * (y[:height] * ai - y[height:] * ar)
        cs = cos_ref[s, :, cols]
        sn = sin_ref[s, :, cols]
        return jnp.concatenate([cs * ar + sn * ai, cs * ai - sn * ar], axis=0)

    prepare(0)
    for c in range(CHUNKS):
        emit(0, c, y_store.at[0], rotated(0, c, field_ref[:, c * width:(c + 1) * width]))

    def forward(k, carry):
        prepare(k + 1)
        wave(k, y_store.at[k], y_store.at[k + 1], lambda c, a: a,
             lambda c: rotated(k + 1, c, col_chunk(c, 0)))
        return carry

    lax.fori_loop(0, layers - 1, forward, 0)
    for c in range(CHUNKS):
        write_blocks(c, halo(layers - 1, c, y_store.at[layers - 1]))
    finish(layers - 1, y_store.at[layers - 1])
    for c in range(CHUNKS):
        field_ref[:, c * width:(c + 1) * width] = col_chunk(c, 0)
    u = field_ref[...]
    ur = u[:height]
    ui = u[height:]
    errors = ur * ur + ui * ui - inten_ref[section % inten_ref.shape[0]].astype(jnp.float32)
    field_ref[...] = jnp.concatenate([2.0 * errors * ur, 2.0 * errors * ui], axis=0)
    for c in range(CHUNKS):
        write_blocks(c, field_ref[:, c * width:(c + 1) * width])
    for c in range(CHUNKS):
        emit(layers, c, b_store.at[0], col_chunk(c, 1))

    def backward(j, carry):
        s = layers - 1 - j
        wave(layers + j, b_store.at[j], b_store.at[j + 1], lambda c, a: adjoint_chunk(s, c, a),
             lambda c: col_chunk(c, 1))
        return carry

    lax.fori_loop(0, layers - 1, backward, 0)
    last = 2 * layers - 1
    for c in range(CHUNKS):
        adjoint_chunk(0, c, halo(last, c, b_store.at[layers - 1]))
    finish(last, b_store.at[layers - 1])
    own = terms_ref[section]
    exchange = pltpu.make_async_remote_copy(
        src_ref=terms_ref.at[partner], dst_ref=partner_ref, send_sem=send_pair, recv_sem=recv_pair,
        device_id={"depth": partner}, device_id_type=MESH)
    exchange.start()
    exchange.wait_send()
    exchange.wait_recv()
    out_ref[0] = own + partner_ref[...]
    for step in range(1, sections):
        for one in gathers(step, section):
            one.wait_send()


def run_chain(angles, index_volume, offsets, intensity, rows, sections):
    _, height, columns = index_volume.shape
    layers = sections
    blocks = columns // LANE
    field = (2 * height, columns)
    plane = (layers, height, columns)
    return pl.pallas_call(
        functools.partial(chain_kernel, rows, sections),
        out_shape=jax.ShapeDtypeStruct((1, height, columns), jnp.float32),
        in_specs=[pl.BlockSpec(memory_space=pltpu.SMEM), pl.BlockSpec(memory_space=pltpu.VMEM),
                  pl.BlockSpec(memory_space=pltpu.SMEM)] + [pl.BlockSpec(memory_space=pltpu.VMEM)] * 3,
        out_specs=pl.BlockSpec(memory_space=pltpu.VMEM),
        scratch_shapes=[
            pltpu.VMEM(plane, jnp.float32),
            pltpu.VMEM((height, columns), jnp.float32),
            pltpu.VMEM(field, jnp.float32),
            pltpu.VMEM((2,) + field, jnp.float32),
            pltpu.VMEM((layers,) + field, jnp.float32),
            pltpu.VMEM((layers,) + field, jnp.float32),
            pltpu.VMEM((2 * layers,) + field, jnp.float32),
            pltpu.VMEM((2 * layers,) + field, jnp.float32),
            pltpu.VMEM((blocks + 2, 2 * height, LANE), jnp.bfloat16),
            pltpu.VMEM((blocks + 2, 2 * height, LANE), jnp.bfloat16),
            pltpu.VMEM(plane, jnp.float32),
            pltpu.VMEM(plane, jnp.float32),
            pltpu.VMEM((2 * layers, 3 * 2 * height, 2 * height), jnp.float32),
            pltpu.VMEM(plane, index_volume.dtype),
            pltpu.VMEM((sections, 8, LANE), jnp.float32),
            pltpu.SemaphoreType.DMA((2 * layers * CHUNKS,)),
            pltpu.SemaphoreType.DMA((2 * layers * CHUNKS,)),
            pltpu.SemaphoreType.DMA((2 * layers * CHUNKS,)),
            pltpu.SemaphoreType.DMA((2 * layers * CHUNKS,)),
            pltpu.SemaphoreType.DMA,
            pltpu.SemaphoreType.DMA,
            pltpu.SemaphoreType.DMA((sections,)),
            pltpu.SemaphoreType.DMA((sections,)),
            pltpu.SemaphoreType.DMA((sections,)),
            pltpu.SemaphoreType.DMA((sections,)),
            pltpu.VMEM((2, 3, LANE, 2 * LANE), jnp.bfloat16),
            pltpu.VMEM((2, 3, LANE, 2 * LANE), jnp.bfloat16),
            pltpu.VMEM((2 * layers, 3 * 2 * height, 2 * height), jnp.bfloat16),
            pltpu.VMEM((2 * layers, 3 * 2 * height, 2 * height), jnp.bfloat16),
            pltpu.VMEM((8, LANE), jnp.float32),
        ],
        compiler_params=pltpu.CompilerParams(
            collective_id=0, has_side_effects=True, vmem_limit_bytes=56 * 1024 * 1024),
    )(angles, index_volume, offsets, intensity, band_table(height), column_bands())


def plane_wave(angle, row_start, height, columns, total_rows, total_cols):
    across = angle - TILTS // 2
    along = jnp.mod(3 * angle, TILTS) - TILTS // 2
    row_index = row_start + lax.broadcasted_iota(jnp.int32, (height, columns), 0)
    col_index = lax.broadcasted_iota(jnp.int32, (height, columns), 1)
    period = total_cols * total_rows
    cycles_int = jnp.mod(across * col_index * total_rows + along * row_index * total_cols, period)
    phase_arg = 2.0 * math.pi / period * cycles_int.astype(jnp.float32)
    return jnp.concatenate([jnp.cos(phase_arg), jnp.sin(phase_arg)], axis=0)


def body(index_volume, angles, offsets, measured):
    sections = lax.axis_size("depth")
    rows = lax.axis_size("row")
    section_no = lax.axis_index("depth")
    height = index_volume.shape[1]
    columns = index_volume.shape[2]
    row_start = lax.axis_index("row") * height
    total_rows = height * rows
    angle_count = angles.shape[0]
    angle_no = section_no % angle_count
    return run_chain(angles, index_volume, offsets, measured, rows, sections)


def solution(mesh):
    in_specs = (P("depth", "row", None), P(), P("depth"), P(None, "row", None))
    out_specs = P("depth", "row", None)
    return jax.shard_map(body, mesh=mesh, in_specs=in_specs, out_specs=out_specs, check_vma=False)
```

```python
import functools
import math

import jax
import numpy as np
import jax.numpy as jnp
from jax import lax
from jax.experimental import pallas as pl
from jax.experimental.pallas import tpu as pltpu
from jax.sharding import PartitionSpec as P

TILTS = 16
HALF = 10
SHIFT = 4
HALFCOL = 64
LANE = 128

PHASE_SCALE = 0.5
CHIRP_ROW = 1.3
CHIRP_COL = 1.7
MESH = pl.DeviceIdType.MESH


def kernel_values(distance, radius, chirp_rate):
    inside = jnp.abs(distance) <= radius
    phase_arg = chirp_rate / radius * distance * distance
    weight = 1.0 / math.sqrt(2 * radius + 1)
    real_part = jnp.where(inside, jnp.cos(phase_arg) * weight, 0.0)
    imag_part = jnp.where(inside, jnp.sin(phase_arg) * weight, 0.0)
    return (real_part, imag_part)


def split_bf16(x):
    high = x.astype(jnp.bfloat16)
    low = (x - high.astype(jnp.float32)).astype(jnp.bfloat16)
    return high, low


def complex_block(real_part, imag_part):
    top = jnp.concatenate([real_part, -imag_part], axis=-1)
    bottom = jnp.concatenate([imag_part, real_part], axis=-1)
    return jnp.concatenate([top, bottom], axis=-2)


def band_table(height):
    offsets = np.arange(-SHIFT, SHIFT + 1)[:, None, None, None]
    part = np.arange(3)[None, :, None, None]
    target = np.arange(height)[None, None, :, None]
    source = np.arange(height)[None, None, None, :] + (part - 1) * height
    tables = []
    for sign in (1, -1):
        distance = (source - target - sign * offsets).astype(np.float64)
        inside = np.abs(distance) <= HALF
        phase_arg = CHIRP_ROW / HALF * distance * distance
        weight = 1.0 / math.sqrt(2 * HALF + 1)
        real_part = np.where(inside, np.cos(phase_arg) * weight, 0.0)
        imag_part = np.where(inside, np.sin(phase_arg) * weight, 0.0) * sign
        top = np.concatenate([real_part, -imag_part], axis=-1)
        bottom = np.concatenate([imag_part, real_part], axis=-1)
        block = np.concatenate([top, bottom], axis=-2)
        tables.append(block.reshape(2 * SHIFT + 1, 3 * 2 * height, 2 * height))
    return jnp.asarray(np.stack(tables, axis=0).astype(np.float32))


def column_bands():
    part = np.arange(3)[:, None, None]
    source = np.arange(LANE)[None, :, None] + (part - 1) * LANE
    target = np.arange(LANE)[None, None, :]
    distance = (source - target).astype(np.float64)
    inside = np.abs(distance) <= HALFCOL
    phase_arg = CHIRP_COL / HALFCOL * distance * distance
    weight = 1.0 / math.sqrt(2 * HALFCOL + 1)
    real_part = np.where(inside, np.cos(phase_arg) * weight, 0.0)
    imag_part = np.where(inside, np.sin(phase_arg) * weight, 0.0)
    forward = np.concatenate([real_part, imag_part], axis=-1)
    adjoint = np.concatenate([real_part, -imag_part], axis=-1)
    return jnp.asarray(np.stack([forward, adjoint], axis=0).astype(np.float32))


def dot3(a_high, a_low, x):
    x_high, x_low = split_bf16(x)
    f32 = jnp.float32
    rows = a_high.shape[0]
    both = jnp.dot(jnp.concatenate([a_high, a_low], axis=0), x_high, preferred_element_type=f32)
    return both[:rows] + both[rows:] + jnp.dot(a_high, x_low, preferred_element_type=f32)


CHUNKS = 2


def chain_kernel(rows, sections, angle_ref, vol_ref, off_ref, inten_ref, table_ref, cband_ref,
                 out_ref, terms_ref, partner_ref, field_ref, acc_ref, y_store, b_store, before, after,
                 bmh_ref, bml_ref, cos_ref, sin_ref, rband_ref, vol_slots, off_slots,
                 send_dn, send_up, recv_bf, recv_af, send_pair, recv_pair,
                 send_vol, send_off, recv_vol, recv_off, chb_ref, clb_ref, rbh_ref, rbl_ref, own_off):
    me = lax.axis_index("row")
    section = lax.axis_index("depth")
    partner = section + 1 - 2 * (section % 2)
    layers, height, columns = cos_ref.shape
    blocks = columns // LANE
    width = columns // CHUNKS
    per_chunk = blocks // CHUNKS
    has_up = me > 0
    has_dn = me < rows - 1

    own_off[...] = jnp.full(own_off.shape, off_ref[0].astype(jnp.float32), jnp.float32)
    barrier = pltpu.get_barrier_semaphore()

    @pl.when(has_up)
    def _():
        pl.semaphore_signal(barrier, 1, device_id={"row": me - 1}, device_id_type=MESH)

    @pl.when(has_dn)
    def _():
        pl.semaphore_signal(barrier, 1, device_id={"row": me + 1}, device_id_type=MESH)

    for step in range(1, sections):
        peer = (section + step) % sections
        pl.semaphore_signal(barrier, 1, device_id={"depth": peer}, device_id_type=MESH)
    angle = angle_ref[section % angle_ref.shape[0]]
    across = angle - TILTS // 2
    along = lax.rem(3 * angle, TILTS) - TILTS // 2
    shape2 = (cos_ref.shape[1], cos_ref.shape[2])
    period = shape2[0] * rows * shape2[1]
    row_index = me * shape2[0] + lax.broadcasted_iota(jnp.int32, shape2, 0)
    col_index = lax.broadcasted_iota(jnp.int32, shape2, 1)
    cycles = lax.rem(across * col_index * (shape2[0] * rows) + along * row_index * shape2[1], period)
    cycles = jnp.where(cycles < 0, cycles + period, cycles)
    wave_arg = 2.0 * math.pi / period * cycles.astype(jnp.float32)
    field_ref[...] = jnp.concatenate([jnp.cos(wave_arg), jnp.sin(wave_arg)], axis=0)
    high, low = split_bf16(cband_ref[...])
    chb_ref[...] = high
    clb_ref[...] = low
    zero_block = jnp.zeros((2 * height, LANE), jnp.bfloat16)
    for ref in (bmh_ref, bml_ref):
        ref[0] = zero_block
        ref[blocks + 1] = zero_block
    peers = (me + rows - 1) // rows + (2 * rows - 2 - me) // rows
    vol_slots[section] = vol_ref[0]
    off_slots[section] = own_off[...]
    part_rows = 2 * height
    def compute(s):
        phase = PHASE_SCALE * vol_slots[s].astype(jnp.float32)
        cos_ref[s] = jnp.cos(phase)
        sin_ref[s] = jnp.sin(phase)
        shift = off_slots[s][0:1, 0:part_rows]
        forward_band = None
        adjoint_band = None
        for i in range(2 * SHIFT + 1):
            pick = jnp.where(shift == float(i - SHIFT), 1.0, 0.0)
            f_term = pick * table_ref[0, i]
            a_term = pick * table_ref[1, i]
            forward_band = f_term if forward_band is None else forward_band + f_term
            adjoint_band = a_term if adjoint_band is None else adjoint_band + a_term
        high, low = split_bf16(forward_band)
        rbh_ref[s] = high
        rbl_ref[s] = low
        high, low = split_bf16(adjoint_band)
        rbh_ref[2 * layers - 1 - s] = high
        rbl_ref[2 * layers - 1 - s] = low

    compute(section)
    pl.semaphore_wait(barrier, peers + sections - 1)

    def gathers(step, slot):
        peer = (section + step) % sections
        vol_copy = pltpu.make_async_remote_copy(
            src_ref=vol_ref.at[0], dst_ref=vol_slots.at[slot], send_sem=send_vol.at[step],
            recv_sem=recv_vol.at[slot], device_id={"depth": peer}, device_id_type=MESH)
        off_copy = pltpu.make_async_remote_copy(
            src_ref=own_off, dst_ref=off_slots.at[slot], send_sem=send_off.at[step],
            recv_sem=recv_off.at[slot], device_id={"depth": peer}, device_id_type=MESH)
        return vol_copy, off_copy

    for step in range(1, sections):
        for one in gathers(step, section):
            one.start()

    def prepare(s):
        @pl.when(s != section)
        def _():
            for one in gathers(1, s):
                one.wait_recv()
            compute(s)


    def copies(k, c, store):
        cols = pl.ds(c * width, width)
        slot = k * CHUNKS + c
        down = pltpu.make_async_remote_copy(
            src_ref=store.at[:, cols], dst_ref=before.at[k, :, cols], send_sem=send_dn.at[slot],
            recv_sem=recv_bf.at[slot], device_id={"row": me + 1}, device_id_type=MESH)
        up = pltpu.make_async_remote_copy(
            src_ref=store.at[:, cols], dst_ref=after.at[k, :, cols], send_sem=send_up.at[slot],
            recv_sem=recv_af.at[slot], device_id={"row": me - 1}, device_id_type=MESH)
        return down, up

    def start(k, c, store):
        down, up = copies(k, c, store)

        @pl.when(has_dn)
        def _():
            down.start()

        @pl.when(has_up)
        def _():
            up.start()

    def finish(k, store):
        for c in range(CHUNKS):
            down, up = copies(k, c, store)

            @pl.when(has_dn)
            def _():
                down.wait_send()

            @pl.when(has_up)
            def _():
                up.wait_send()

    def halo(k, c, store):
        down, up = copies(k, c, store)
        cols = pl.ds(c * width, width)
        slot = k % 2

        @pl.when(has_up)
        def _():
            down.wait_recv()
            acc_ref[slot, :, cols] += dot3(rbh_ref[k, 0:part_rows], rbl_ref[k, 0:part_rows], before[k, :, cols])

        @pl.when(has_dn)
        def _():
            up.wait_recv()
            acc_ref[slot, :, cols] += dot3(rbh_ref[k, 2 * part_rows:3 * part_rows], rbl_ref[k, 2 * part_rows:3 * part_rows], after[k, :, cols])

        return acc_ref[slot, :, cols]

    def emit(k, c, store, value):
        cols = pl.ds(c * width, width)
        store[:, cols] = value
        acc_ref[k % 2, :, cols] = dot3(rbh_ref[k, part_rows:2 * part_rows], rbl_ref[k, part_rows:2 * part_rows], store[:, cols])
        start(k, c, store)

    def write_blocks(c, x):
        high, low = split_bf16(x)
        for b in range(per_chunk):
            bmh_ref[c * per_chunk + b + 1] = high[:, b * LANE:(b + 1) * LANE]
            bml_ref[c * per_chunk + b + 1] = low[:, b * LANE:(b + 1) * LANE]

    def wave(k, store, store_next, finish_chunk, make_chunk):
        for c in range(CHUNKS):
            write_blocks(c, finish_chunk(c, halo(k, c, store)))
            if c >= 1:
                emit(k + 1, c - 1, store_next, make_chunk(c - 1))
        emit(k + 1, CHUNKS - 1, store_next, make_chunk(CHUNKS - 1))
        finish(k, store)

    def col_chunk(c, which):
        total = None
        f32 = jnp.float32
        first = c * per_chunk
        for t in range(3):
            xh = bmh_ref[first + t:first + t + per_chunk].reshape(per_chunk * 2 * height, LANE)
            xl = bml_ref[first + t:first + t + per_chunk].reshape(per_chunk * 2 * height, LANE)
            wh = chb_ref[which, t]
            wl = clb_ref[which, t]
            count = xh.shape[0]
            both = jnp.dot(jnp.concatenate([xh, xl], axis=0), wh, preferred_element_type=f32)
            part = both[:count] + both[count:] + jnp.dot(xh, wl, preferred_element_type=f32)
            total = part if total is None else total + part
        total = total.reshape(per_chunk, 2 * height, 2 * LANE)
        real_part = total[:, :height, :LANE] - total[:, height:, LANE:]
        imag_part = total[:, :height, LANE:] + total[:, height:, :LANE]
        out = jnp.concatenate([real_part, imag_part], axis=1)
        return jnp.concatenate([out[b] for b in range(per_chunk)], axis=1)

    def rotated(s, c, u):
        cols = pl.ds(c * width, width)
        cs = cos_ref[s, :, cols]
        sn = sin_ref[s, :, cols]
        ur = u[:height]
        ui = u[height:]
        return jnp.concatenate([cs * ur - sn * ui, cs * ui + sn * ur], axis=0)

    def adjoint_chunk(s, c, a):
        cols = pl.ds(c * width, width)
        ar = a[:height]
        ai = a[height:]
        y = y_store[s, :, cols]
        terms_ref[s, :, cols] = PHASE_SCALE * (y[:height] * ai - y[height:] * ar)
        cs = cos_ref[s, :, cols]
        sn = sin_ref[s, :, cols]
        return jnp.concatenate([cs * ar + sn * ai, cs * ai - sn * ar], axis=0)

    prepare(0)
    for c in range(CHUNKS):
        emit(0, c, y_store.at[0], rotated(0, c, field_ref[:, c * width:(c + 1) * width]))

    def forward(k, carry):
        prepare(k + 1)
        wave(k, y_store.at[k], y_store.at[k + 1], lambda c, a: a,
             lambda c: rotated(k + 1, c, col_chunk(c, 0)))
        return carry

    lax.fori_loop(0, layers - 1, forward, 0)
    for c in range(CHUNKS):
        write_blocks(c, halo(layers - 1, c, y_store.at[layers - 1]))
    finish(layers - 1, y_store.at[layers - 1])
    for c in range(CHUNKS):
        field_ref[:, c * width:(c + 1) * width] = col_chunk(c, 0)
    u = field_ref[...]
    ur = u[:height]
    ui = u[height:]
    errors = ur * ur + ui * ui - inten_ref[section % inten_ref.shape[0]].astype(jnp.float32)
    field_ref[...] = jnp.concatenate([2.0 * errors * ur, 2.0 * errors * ui], axis=0)
    for c in range(CHUNKS):
        write_blocks(c, field_ref[:, c * width:(c + 1) * width])
    for c in range(CHUNKS):
        emit(layers, c, b_store.at[0], col_chunk(c, 1))

    def backward(j, carry):
        s = layers - 1 - j
        wave(layers + j, b_store.at[j], b_store.at[j + 1], lambda c, a: adjoint_chunk(s, c, a),
             lambda c: col_chunk(c, 1))
        return carry

    lax.fori_loop(0, layers - 1, backward, 0)
    last = 2 * layers - 1
    for c in range(CHUNKS):
        adjoint_chunk(0, c, halo(last, c, b_store.at[layers - 1]))
    finish(last, b_store.at[layers - 1])
    own = terms_ref[section]
    exchange = pltpu.make_async_remote_copy(
        src_ref=terms_ref.at[partner], dst_ref=partner_ref, send_sem=send_pair, recv_sem=recv_pair,
        device_id={"depth": partner}, device_id_type=MESH)
    exchange.start()
    exchange.wait_send()
    exchange.wait_recv()
    out_ref[0] = own + partner_ref[...]
    for step in range(1, sections):
        for one in gathers(step, section):
            one.wait_send()


def run_chain(angles, index_volume, offsets, intensity, rows, sections):
    _, height, columns = index_volume.shape
    layers = sections
    blocks = columns // LANE
    field = (2 * height, columns)
    plane = (layers, height, columns)
    return pl.pallas_call(
        functools.partial(chain_kernel, rows, sections),
        out_shape=jax.ShapeDtypeStruct((1, height, columns), jnp.float32),
        in_specs=[pl.BlockSpec(memory_space=pltpu.SMEM), pl.BlockSpec(memory_space=pltpu.VMEM),
                  pl.BlockSpec(memory_space=pltpu.SMEM)] + [pl.BlockSpec(memory_space=pltpu.VMEM)] * 3,
        out_specs=pl.BlockSpec(memory_space=pltpu.VMEM),
        scratch_shapes=[
            pltpu.VMEM(plane, jnp.float32),
            pltpu.VMEM((height, columns), jnp.float32),
            pltpu.VMEM(field, jnp.float32),
            pltpu.VMEM((2,) + field, jnp.float32),
            pltpu.VMEM((layers,) + field, jnp.float32),
            pltpu.VMEM((layers,) + field, jnp.float32),
            pltpu.VMEM((2 * layers,) + field, jnp.float32),
            pltpu.VMEM((2 * layers,) + field, jnp.float32),
            pltpu.VMEM((blocks + 2, 2 * height, LANE), jnp.bfloat16),
            pltpu.VMEM((blocks + 2, 2 * height, LANE), jnp.bfloat16),
            pltpu.VMEM(plane, jnp.float32),
            pltpu.VMEM(plane, jnp.float32),
            pltpu.VMEM((2 * layers, 3 * 2 * height, 2 * height), jnp.float32),
            pltpu.VMEM(plane, index_volume.dtype),
            pltpu.VMEM((sections, 8, LANE), jnp.float32),
            pltpu.SemaphoreType.DMA((2 * layers * CHUNKS,)),
            pltpu.SemaphoreType.DMA((2 * layers * CHUNKS,)),
            pltpu.SemaphoreType.DMA((2 * layers * CHUNKS,)),
            pltpu.SemaphoreType.DMA((2 * layers * CHUNKS,)),
            pltpu.SemaphoreType.DMA,
            pltpu.SemaphoreType.DMA,
            pltpu.SemaphoreType.DMA((sections,)),
            pltpu.SemaphoreType.DMA((sections,)),
            pltpu.SemaphoreType.DMA((sections,)),
            pltpu.SemaphoreType.DMA((sections,)),
            pltpu.VMEM((2, 3, LANE, 2 * LANE), jnp.bfloat16),
            pltpu.VMEM((2, 3, LANE, 2 * LANE), jnp.bfloat16),
            pltpu.VMEM((2 * layers, 3 * 2 * height, 2 * height), jnp.bfloat16),
            pltpu.VMEM((2 * layers, 3 * 2 * height, 2 * height), jnp.bfloat16),
            pltpu.VMEM((8, LANE), jnp.float32),
        ],
        compiler_params=pltpu.CompilerParams(
            collective_id=0, has_side_effects=True, vmem_limit_bytes=56 * 1024 * 1024),
    )(angles, index_volume, offsets, intensity, band_table(height), column_bands())


def plane_wave(angle, row_start, height, columns, total_rows, total_cols):
    across = angle - TILTS // 2
    along = jnp.mod(3 * angle, TILTS) - TILTS // 2
    row_index = row_start + lax.broadcasted_iota(jnp.int32, (height, columns), 0)
    col_index = lax.broadcasted_iota(jnp.int32, (height, columns), 1)
    period = total_cols * total_rows
    cycles_int = jnp.mod(across * col_index * total_rows + along * row_index * total_cols, period)
    phase_arg = 2.0 * math.pi / period * cycles_int.astype(jnp.float32)
    return jnp.concatenate([jnp.cos(phase_arg), jnp.sin(phase_arg)], axis=0)


def body(index_volume, angles, offsets, measured):
    sections = lax.axis_size("depth")
    rows = lax.axis_size("row")
    section_no = lax.axis_index("depth")
    height = index_volume.shape[1]
    columns = index_volume.shape[2]
    row_start = lax.axis_index("row") * height
    total_rows = height * rows
    angle_count = angles.shape[0]
    angle_no = section_no % angle_count
    return run_chain(angles, index_volume, offsets, measured, rows, sections)


def solution(mesh):
    in_specs = (P("depth", "row", None), P(), P("depth"), P(None, "row", None))
    out_specs = P("depth", "row", None)
    return jax.shard_map(body, mesh=mesh, in_specs=in_specs, out_specs=out_specs, check_vma=False)
```
